32 devices in a mesh: seq: 16 (over z, y, x), mem: 2 (over core).
Axes of the slice: x: 2, y: 2, z: 4, core: 2. Of those that a mesh axis runs over, the one named last changes fastest.
Arguments:
- tokens: bfloat16 [16384, 768], P(('seq', 'mem')), may hold values from -6 to 6
- memory: bfloat16 [4096, 768], P(('seq', 'mem')), may hold values from -6 to 6
- lengths: int32 [16], P('seq'), may hold values from 256 to 1024, as said below
- tokens_cotangent: bfloat16 [16384, 768], P(('seq', 'mem')), may hold values from -6 to 6
- memory_cotangent: bfloat16 [4096, 768], P(('seq', 'mem')), may hold values from -6 to 6
- projections: float32 [6, 768, 768], P(None, ('seq', 'mem')), may hold values from -1 to 1
- output_maps: float32 [2, 768, 768], P(None, ('seq', 'mem')), may hold values from -1 to 1
- expand_weight: float32 [768, 3072], P(('seq', 'mem')), may hold values from -0.21875 to 0.21875
- shrink_weight: float32 [3072, 768], P(('seq', 'mem')), may hold values from -0.109375 to 0.109375
- projection_bias: float32 [6, 768], P(None, ('seq', 'mem')), may hold values from -2 to 2
- norm_gain: float32 [3, 768], P(None, ('seq', 'mem')), may hold values from 0.5 to 1.5
- norm_bias: float32 [3, 768], P(None, ('seq', 'mem')), may hold values from -2 to 2
- expand_bias: float32 [3072], P(('seq', 'mem')), may hold values from -2 to 2
- shrink_bias: float32 [768], P(('seq', 'mem')), may hold values from -2 to 2
Outputs:
- new_tokens: float32 [16384, 768], P(('seq', 'mem'))
- new_memory: float32 [4096, 768], P(('seq', 'mem'))
- tokens_grad: float32 [16384, 768], P(('seq', 'mem'))
- memory_grad: float32 [4096, 768], P(('seq', 'mem'))
- projections_grad: float32 [6, 768, 768], P(None, ('seq', 'mem'))
- output_maps_grad: float32 [2, 768, 768], P(None, ('seq', 'mem'))
- expand_weight_grad: float32 [768, 3072], P(('seq', 'mem'))
- shrink_weight_grad: float32 [3072, 768], P(('seq', 'mem'))
- projection_bias_grad: float32 [6, 768], P(None, ('seq', 'mem'))
- norm_gain_grad: float32 [3, 768], P(None, ('seq', 'mem'))
- norm_bias_grad: float32 [3, 768], P(None, ('seq', 'mem'))
- expand_bias_grad: float32 [3072], P(('seq', 'mem'))
- shrink_bias_grad: float32 [768], P(('seq', 'mem'))
The draws below stay inside these ranges and needn't reach their ends.
Inputs may be any that keep to these rules, and one draw needn't show every extreme that they name: `lengths`: every sequence has at least a quarter of its 1024 slots live; some sequence fills all 1024 in every draw; live tokens come first.
All inputs are finite; a program needn't handle non-finite values.
Results may differ from the reference program's by a relative error of at most 0.015.
Values may be sent and summed in bfloat16 or wider, within the bound.
A program may use at most 256 MiB of HBM per device.

```python
import jax
import jax.numpy as jnp
from jax import lax

D = 768
HEADS = 12
HEAD = 64
FF = 3072
MEM = 256
LEN = 1024
GROUPS = 16
TOKENS = 16384


def draw_lengths(key, part):
    first, second = jax.random.split(key)
    values = jax.random.randint(first, (GROUPS,), LEN // 4, LEN + 1)
    chosen = jax.random.randint(second, (), 0, GROUPS)
    return jnp.where(jnp.arange(GROUPS) == chosen, LEN, values).astype(jnp.int32)


def draw_tokens(key, part):
    sub = jax.random.fold_in(key, 11)
    return jax.random.truncated_normal(sub, -6.0, 6.0, (TOKENS, D), jnp.float32).astype(jnp.bfloat16)


def draw_memory(key, part):
    sub = jax.random.fold_in(key, 23)
    return jax.random.truncated_normal(sub, -6.0, 6.0, (GROUPS * MEM, D), jnp.float32).astype(jnp.bfloat16)


def draw_projections(key, part):
    sub = jax.random.fold_in(key, 37)
    values = jax.random.truncated_normal(sub, -6.0, 6.0, (6, D, D), jnp.float32)
    factors = jnp.array([1.6, 1.6, 1.0, 1.4, 1.4, 1.0], jnp.float32).reshape(6, 1, 1)
    return values * factors * float(D) ** (-0.5)


def draw_output_maps(key, part):
    sub = jax.random.fold_in(key, 41)
    values = jax.random.truncated_normal(sub, -3.0, 3.0, (2, D, D), jnp.float32)
    factors = jnp.array([1.6, 2.0], jnp.float32).reshape(2, 1, 1)
    return values * factors * float(D) ** (-0.5)


def levels(key, shape, cuts, smallest, largest):
    level, own = 1.0, jax.random.fold_in(key, 6)
    for position, shards_of in cuts:
        draws = jnp.exp(jax.random.uniform(jax.random.fold_in(own, position), (shards_of,), jnp.float32, smallest / len(cuts), largest / len(cuts)))
        level = level * jnp.repeat(draws, shape[position] // shards_of).reshape([-1 if axis == position else 1 for axis in range(len(shape))])
    return level


def scatter_about(rng, dims, width, limit, shards=(), kind=jnp.bfloat16):
    values = width * jax.random.normal(rng, dims, jnp.float32)
    if shards:
        values = values * levels(rng, dims, shards, -0.22, 0.18)
    return jnp.clip(values, -limit, limit).astype(kind)


def setup_inputs(seed: int = 0) -> dict:
    key_of = jax.random.split(jax.random.key(seed), 15)
    tokens = draw_tokens(jax.random.fold_in(key_of[14], 71), 0)
    memory = draw_memory(jax.random.fold_in(key_of[14], 71), 0)
    lengths = draw_lengths(jax.random.fold_in(key_of[14], 71), 0)
    tokens_cotangent = scatter_about(key_of[3], (TOKENS, D), 1.0, 6.0, ((0, 32),))
    memory_cotangent = scatter_about(key_of[4], (GROUPS * MEM, D), 1.0, 6.0, ((0, 32),))
    projections = draw_projections(jax.random.fold_in(key_of[14], 71), 0)
    output_maps = draw_output_maps(jax.random.fold_in(key_of[14], 71), 0)
    expand_weight = scatter_about(key_of[7], (D, FF), D ** -0.5, 0.21875, ((0, 32),), jnp.float32)
    shrink_weight = scatter_about(key_of[8], (FF, D), FF ** -0.5, 0.109375, ((0, 32),), jnp.float32)
    projection_bias = scatter_about(key_of[9], (6, D), 0.3, 2.0, ((1, 32),), jnp.float32)
    norm_gain = jnp.clip(1.0 + 0.1 * jax.random.normal(key_of[10], (3, D), jnp.float32), 0.5, 1.5)
    norm_bias = scatter_about(key_of[11], (3, D), 0.3, 2.0, ((1, 32),), jnp.float32)
    expand_bias = scatter_about(key_of[12], (FF,), 0.3, 2.0, ((0, 32),), jnp.float32)
    shrink_bias = scatter_about(key_of[13], (D,), 0.3, 2.0, ((0, 32),), jnp.float32)
    return {"tokens": tokens, "memory": memory, "lengths": lengths, "tokens_cotangent": tokens_cotangent, "memory_cotangent": memory_cotangent, "projections": projections, "output_maps": output_maps, "expand_weight": expand_weight, "shrink_weight": shrink_weight, "projection_bias": projection_bias, "norm_gain": norm_gain, "norm_bias": norm_bias, "expand_bias": expand_bias, "shrink_bias": shrink_bias}


@jax.custom_vjp
def low(v):
    return lax.optimization_barrier(v.astype(jnp.bfloat16)).astype(jnp.float32)

@jax.custom_vjp
def low_back(v):
    return v

def low_keep(v):
    return (low(v), None)

def low_pass(kept, grad):
    return (grad,)

def back_keep(v):
    return (v, None)

def back_low(kept, grad):
    return (low(grad),)
low.defvjp(low_keep, low_pass)
low_back.defvjp(back_keep, back_low)
highest = lax.Precision.HIGHEST
epsilon = 1e-05

def product(left, right):
    return jnp.dot(left, right, precision=highest)

def rounded(values):
    return low_back(low(values))

def layer_norm(values, gain, shift):
    centre = values - lax.optimization_barrier(jnp.mean(values, axis=-1, keepdims=True))
    spread = lax.optimization_barrier(jnp.mean(centre * centre, axis=-1, keepdims=True))
    return centre * lax.rsqrt(spread + epsilon) * gain + shift

def attend(queries, keys, values, valid):
    count_rows = queries.shape[0]
    count_cols = keys.shape[0]
    query_heads = queries.reshape(count_rows, HEADS, HEAD)
    key_heads = keys.reshape(count_cols, HEADS, HEAD)
    value_heads = values.reshape(count_cols, HEADS, HEAD)
    scores = low_back(jnp.einsum('rhd,chd->hrc', query_heads, key_heads, precision=highest) * HEAD ** (-0.5))
    if valid is not None:
        scores = jnp.where(valid[None, None, :], scores, -1e+30)
    probs = jax.nn.softmax(scores, axis=-1)
    mixed = jnp.einsum('hrc,chd->rhd', low(probs), value_heads, precision=highest)
    return rounded(mixed.reshape(count_rows, HEADS * HEAD))

def group_layer(inputs, memory_rows, length, weights):
    projections, output_maps, expand_weight, shrink_weight, projection_bias, norm_gain, norm_bias, expand_bias, shrink_bias = weights
    valid = jnp.arange(LEN) < length
    pack_query = rounded(product(memory_rows, projections[0]) + projection_bias[0])
    pack_keys = rounded(product(inputs, projections[1]))
    pack_values = rounded(product(inputs, projections[2]) + projection_bias[1])
    pack_mixed = attend(pack_query, pack_keys, pack_values, valid)
    packed = low_back(product(pack_mixed, output_maps[0]) + projection_bias[2])
    new_memory = layer_norm(memory_rows + packed, norm_gain[0], norm_bias[0])
    packed_low = low(packed)
    unpack_keys = rounded(product(packed_low, projections[4]))
    unpack_values = rounded(product(packed_low, projections[5]) + projection_bias[4])
    unpack_query = rounded(product(inputs, projections[3]) + projection_bias[3])
    unpack_mixed = attend(unpack_query, unpack_keys, unpack_values, None)
    unpacked = low_back(product(unpack_mixed, output_maps[1]) + projection_bias[5])
    middle = layer_norm(inputs + unpacked, norm_gain[1], norm_bias[1])
    hidden_in = low_back(product(low(middle), expand_weight) + expand_bias)
    hidden = low(jax.nn.gelu(hidden_in, approximate=False))
    branch = low_back(product(hidden, shrink_weight) + shrink_bias)
    result = layer_norm(middle + branch, norm_gain[2], norm_bias[2])
    return (jnp.where(valid[:, None], result, 0.0), new_memory)

def reference(tokens, memory, lengths, tokens_cotangent, memory_cotangent, projections, output_maps, expand_weight, shrink_weight, projection_bias, norm_gain, norm_bias, expand_bias, shrink_bias):
    masters = (projections, output_maps, expand_weight, shrink_weight, projection_bias, norm_gain, norm_bias, expand_bias, shrink_bias)
    layer = jax.checkpoint(group_layer)

    def forward(tokens_float, memory_float, weights):
        lowered = tuple((low(master) for master in weights))

        def per_group(pieces):
            return layer(pieces[0], pieces[1], pieces[2], lowered)
        results = lax.map(per_group, (tokens_float.reshape(GROUPS, LEN, D), memory_float.reshape(GROUPS, MEM, D), lengths))
        return (results[0].reshape(GROUPS * LEN, D), results[1].reshape(GROUPS * MEM, D))
    outputs, pullback = jax.vjp(forward, tokens.astype(jnp.float32), memory.astype(jnp.float32), masters)
    tokens_grad, memory_grad, weight_grads = pullback((tokens_cotangent.astype(jnp.float32), memory_cotangent.astype(jnp.float32)))
    return (outputs[0], outputs[1], tokens_grad, memory_grad, weight_grads[0], weight_grads[1], weight_grads[2], weight_grads[3], weight_grads[4], weight_grads[5], weight_grads[6], weight_grads[7], weight_grads[8])
```

```python
import functools

import jax
import jax.numpy as jnp
from jax import lax
from jax.experimental import pallas as pl
from jax.experimental.pallas import tpu as pltpu
from jax.sharding import PartitionSpec as P

HEAD = 64
epsilon = 1e-05
MESH = pl.DeviceIdType.MESH
LOW = jnp.bfloat16
F32 = jnp.float32
AXES = ("seq", "mem")


def matmul(left, right):
    return jnp.dot(left, right, preferred_element_type=F32)


def matmul_left(left, right):
    return lax.dot_general(left, right, (((0,), (0,)), ((), ())), preferred_element_type=F32)


def matmul_right(left, right):
    return lax.dot_general(left, right, (((1,), (1,)), ((), ())), preferred_element_type=F32)


def to_low(values):
    return values.astype(LOW)


def column_sum(values):
    return jnp.sum(values.astype(F32), axis=0)


def swap(values):
    return lax.ppermute(values, "mem", [(0, 1), (1, 0)])


def join(own, other, axis=0):
    first = lax.axis_index("mem") == 0
    return jnp.where(
        first, jnp.concatenate([own, other], axis), jnp.concatenate([other, own], axis)
    )


def both(values, axis=0):
    return join(values, swap(values), axis)


def half(values, index, axis):
    size = values.shape[axis] // 2
    return lax.dynamic_slice_in_dim(values, index * size, size, axis)


def place(seq):
    return lax.div(seq, 4), lax.rem(lax.div(seq, 2), 2), lax.rem(seq, 2)


def peers(seq, core, far_count):
    far, row, column = place(seq)
    flat = lambda f, r, c: f * 4 + r * 2 + c
    far_peers = [lax.rem(far + k, far_count) for k in range(1, far_count)]
    return {
        "far": [(flat(f, row, column), core) for f in far_peers],
        "far_index": far_peers,
        "column": (flat(far, row, 1 - column), core),
        "row": (flat(far, 1 - row, column), core),
        "core": (seq, 1 - core),
    }


def greet(targets):
    barrier = pltpu.get_barrier_semaphore()
    for target in targets:
        pl.semaphore_signal(barrier, inc=1, device_id=target, device_id_type=MESH)
    pl.semaphore_wait(barrier, len(targets))


class Gather:
    def __init__(self, where, to, first, own, at, shared, sems):
        self.where, self.to, self.own, self.at, self.shared = where, to, own, at, shared
        self.first, self.second = first, ("row" if first == "column" else "column")
        self.send, self.recv = sems
        self.started = []

    def _column(self, near):
        far, row, column = self.where
        row, column = (
            (1 - row if "row" in near else row),
            (1 - column if "column" in near else column),
        )
        return self.at(slice(None), row, column)

    def _copy(self, source, target, k, device):
        return pltpu.make_async_remote_copy(
            source, target, self.send.at[k], self.recv.at[k], device_id=device, device_id_type=MESH
        )

    def _go(self, *args):
        copy = self._copy(*args)
        copy.start()
        self.started.append(copy)

    def _arrived(self, ref, k):
        self._copy(ref, ref, k, self.to["core"]).wait_recv()

    def start(self):
        far, row, column = self.where
        mine = self.at(far, row, column)
        for k, device in enumerate(self.to["far"]):
            self._go(self.own, mine, k, device)

    def step(self, stage):
        far, row, column = self.where
        near = self._column(())
        if stage == 0:
            count = len(self.to["far"])
            for k in range(count):
                sender = self.to["far_index"][count - 1 - k]
                self._arrived(self.at(sender, row, column), k)
            self._go(near, near, 3, self.to[self.first])
            self._go(near, near, 4, self.to[self.second])
            if self.shared:
                self._go(near, near, 6, self.to["core"])
        if stage == 1:
            got = self._column((self.first,))
            self._arrived(got, 3)
            self._go(got, got, 5, self.to[self.second])
            if self.shared:
                self._go(got, got, 7, self.to["core"])
        if stage == 2:
            for k, names in ((4, (self.second,)), (5, (self.first, self.second))):
                got = self._column(names)
                self._arrived(got, k)
                if self.shared:
                    self._go(got, got, 4 + k, self.to["core"])
        if stage == 3 and self.shared:
            for k, names in enumerate(
                ((), (self.first,), (self.second,), (self.first, self.second))
            ):
                self._arrived(self._other(names), 6 + k)

    def _other(self, names):
        keep, self.at = self.at, self.shared
        ref = self._column(names)
        self.at = keep
        return ref

    def finish(self):
        for copy in self.started:
            copy.wait_send()


def gather_kernel(far_count, proj, maps, expand, shrink, vec,
                  proj_o, maps_o, expand_o, shrink_o, vec_o, send, recv, local):
    seq, core = lax.axis_index("seq"), lax.axis_index("mem")
    where = place(seq)
    far, row, column = where
    to = peers(seq, core, far_count)
    wide = maps.shape[-1]

    def cols(which, start=0):
        return pl.ds(pl.multiple_of(which * expand.shape[-1] + start, 128), wide)

    def span(which):
        return pl.ds(pl.multiple_of(which * wide, 128), wide)

    copies = []

    def keep(source, target):
        copy = pltpu.make_async_copy(source, target, local.at[len(copies)])
        copy.start()
        copies.append(copy)

    keep(proj, proj_o.at[:, far, row, column])
    keep(maps, maps_o.at[:, far, row, column, :, span(core)])
    keep(expand, expand_o.at[far, row, column, :, pl.ds(pl.multiple_of(core * expand.shape[-1], 128), expand.shape[-1])])
    keep(shrink, shrink_o.at[far, row, column, :, span(core)])
    keep(vec, vec_o.at[far, row, column])

    units = []

    def add(first, own, at, shared):
        k = len(units)
        units.append(Gather(where, to, first, own, at, shared, (send.at[k], recv.at[k])))

    def add_proj(first, p):
        add(first, proj.at[p], lambda f, r, c: proj_o.at[p, f, r, c], None)

    def add_map(first, p):
        add(first, maps.at[p], lambda f, r, c: maps_o.at[p, f, r, c, :, span(core)],
            lambda f, r, c: maps_o.at[p, f, r, c, :, span(1 - core)])

    def add_expand(first, k):
        add(first, expand.at[:, pl.ds(k * wide, wide)], lambda f, r, c: expand_o.at[f, r, c, :, cols(core, k * wide)],
            lambda f, r, c: expand_o.at[f, r, c, :, cols(1 - core, k * wide)])

    def add_shrink(first, k):
        rows = shrink.shape[0] // 4
        part = pl.ds(k * rows, rows)
        add(first, shrink.at[part], lambda f, r, c: shrink_o.at[f, r, c, part, span(core)],
            lambda f, r, c: shrink_o.at[f, r, c, part, span(1 - core)])

    add("column", vec, lambda f, r, c: vec_o.at[f, r, c], None)
    for first, second in (
        ((add_proj, 0), (add_proj, 1)), ((add_proj, 2), (add_map, 0)), ((add_proj, 4), (add_proj, 5)), ((add_proj, 3), (add_map, 1)),
        ((add_expand, 0), (add_expand, 1)), ((add_expand, 2), (add_expand, 3)), ((add_shrink, 0), (add_shrink, 1)), ((add_shrink, 2), (add_shrink, 3)),
    ):
        first[0]("column", first[1])
        second[0]("row", second[1])

    greet(to["far"] + [to["column"], to["row"], to["core"]])
    for unit in units:
        unit.start()
    for copy in copies:
        copy.wait()
    lanes = [units[:1]] + [units[k:k + 2] for k in range(1, len(units), 2)]
    for t in range(len(lanes) + 3):
        for stage in range(4):
            if 0 <= t - stage < len(lanes):
                for unit in lanes[t - stage]:
                    unit.step(stage)
    for unit in units:
        unit.finish()


def gather_chips(far_count, blocks):
    proj, maps, expand, shrink, vec = blocks
    grid = (far_count, 2, 2)
    rows = proj.shape[1]
    shapes = (
        (6,) + grid + proj.shape[1:],
        (2,) + grid + (rows, 2 * maps.shape[2]),
        grid + (rows, 2 * expand.shape[1]),
        grid + (shrink.shape[0], 2 * shrink.shape[1]),
        grid + vec.shape,
    )
    any_space = pl.BlockSpec(memory_space=pl.ANY)
    return pl.pallas_call(
        functools.partial(gather_kernel, far_count),
        out_shape=[jax.ShapeDtypeStruct(shape, LOW) for shape in shapes],
        in_specs=[any_space] * 5,
        out_specs=[any_space] * 5,
        scratch_shapes=[
            pltpu.SemaphoreType.DMA((17, 10)),
            pltpu.SemaphoreType.DMA((17, 10)),
            pltpu.SemaphoreType.DMA((5,)),
        ],
        compiler_params=pltpu.CompilerParams(collective_id=0, has_side_effects=True),
        name="gather_weights",
    )(*blocks)


class Reduce:
    def __init__(self, where, to, first, at, total, half_in, quarter_in, far_in, sems, kind):
        self.where, self.to, self.at, self.total = where, to, at, total
        self.half_in, self.quarter_in, self.far_in, self.kind = half_in, quarter_in, far_in, kind
        self.first, self.second = first, ("row" if first == "column" else "column")
        self.send, self.recv, self.load = sems
        self.started, self.loads = [], []

    def _copy(self, source, target, k, device):
        return pltpu.make_async_remote_copy(
            source, target, self.send.at[k], self.recv.at[k], device_id=device, device_id_type=MESH
        )

    def _go(self, *args):
        copy = self._copy(*args)
        copy.start()
        self.started.append(copy)

    def _arrived(self, ref, k):
        self._copy(ref, ref, k, self.to["core"]).wait_recv()

    def _column(self, near):
        far, row, column = self.where
        row, column = (
            (1 - row if "row" in near else row),
            (1 - column if "column" in near else column),
        )
        return self.at(slice(None), row, column)

    def start(self):
        for k, names in enumerate(((self.second,), (self.first, self.second))):
            self._go(self._column(names), self.half_in.at[k], k, self.to[self.second])
        for k, names in enumerate(((), (self.first,))):
            copy = pltpu.make_async_copy(self._column(names), self.total.at[k], self.load.at[k])
            copy.start()
            self.loads.append(copy)

    def _add(self, target, other):
        count = target.shape[0]
        for k in range(count):
            target[k] = (target[k].astype(F32) + other[k].astype(F32)).astype(self.kind)

    def step(self, stage):
        count = len(self.to["far"])
        if stage == 0:
            self.loads[1].wait()
            self._arrived(self.half_in.at[1], 1)
            self._add(self.total.at[1], self.half_in.at[1])
            self._go(self.total.at[1], self.quarter_in, 2, self.to[self.first])
            self.loads[0].wait()
            self._arrived(self.half_in.at[0], 0)
            self._add(self.total.at[0], self.half_in.at[0])
        if stage == 1:
            self._arrived(self.quarter_in, 2)
            self._add(self.total.at[0], self.quarter_in)
            for k, device in enumerate(self.to["far"]):
                self._go(self.total.at[0, self.to["far_index"][k]], self.far_in.at[k], 3 + k, device)
        if stage == 2:
            for k in range(count):
                self._arrived(self.far_in.at[k], 3 + k)

    def result(self):
        value = self.total[0, self.where[0]].astype(F32)
        for k in range(len(self.to["far"])):
            value = value + self.far_in[k].astype(F32)
        return value

    def finish(self):
        for copy in self.started:
            copy.wait_send()


def reduce_kernel(far_count, proj, maps, expand, shrink, vec,
                  proj_o, maps_o, expand_o, shrink_o, vec_o,
                  total, half_in, quarter_in, far_in, vtotal, vhalf, vquarter, vfar, sums, vsum, vother,
                  send, recv, load, last_send, last_recv, last_local):
    seq, core = lax.axis_index("seq"), lax.axis_index("mem")
    where = place(seq)
    to = peers(seq, core, far_count)
    wide = maps.shape[-1]
    rows = proj.shape[-2]
    part = rows // 2
    units, ends = [], []

    def span(which, start=0, whole=None):
        return pl.ds(pl.multiple_of(which * (whole or wide) + start, 128), wide)

    def add(at, end):
        k = len(units)
        first = "column" if k % 2 == 0 else "row"
        units.append(Reduce(where, to, first, at, total.at[k], half_in.at[k], quarter_in.at[k], far_in.at[k],
                            (send.at[k], recv.at[k], load.at[k]), LOW))
        ends.append(end)

    def add_expand(k):
        add(lambda f, r, c: expand.at[f, r, c, :, pl.ds(k * wide, wide)],
            lambda which: expand_o.at[:, span(which, k * wide, expand.shape[-1])])

    def add_shrink(k):
        add(lambda f, r, c: shrink.at[f, r, c, pl.ds(k * rows, rows)], None)

    def add_map(p):
        add(lambda f, r, c: maps.at[p, f, r, c], lambda which: maps_o.at[p, :, span(which)])

    def add_proj(p):
        add(lambda f, r, c: proj.at[p, f, r, c], lambda which: proj_o.at[p, :, span(which)])

    for k in range(4):
        add_shrink(k)
    for k in range(4):
        add_expand(k)
    for make, p in ((add_map, 1), (add_proj, 3), (add_proj, 4), (add_proj, 5), (add_map, 0), (add_proj, 0), (add_proj, 1), (add_proj, 2)):
        make(p)
    vectors = Reduce(where, to, "column", lambda f, r, c: vec.at[f, r, c], vtotal, vhalf, vquarter, vfar,
                     (send.at[16], recv.at[16], load.at[16]), F32)

    greet(to["far"] + [to["column"], to["row"], to["core"]])
    order = units + [vectors]
    for unit in order:
        unit.start()
    lanes = [units[k:k + 2] for k in range(0, 16, 2)]
    lanes[0] = [vectors] + lanes[0]
    final = []
    index = {id(unit): k for k, unit in enumerate(units)}

    def close(unit):
        if unit is vectors:
            vsum[...] = vectors.result()
            mine, other = pl.ds(pl.multiple_of(core * 8, 8), 8), pl.ds(pl.multiple_of((1 - core) * 8, 8), 8)
            copy = pltpu.make_async_remote_copy(vsum.at[other], vother, last_send.at[16], last_recv.at[16],
                                                device_id=to["core"], device_id_type=MESH)
            copy.start()
            final.append(copy)
            return
        k = index[id(unit)]
        sums[k] = unit.result()
        if ends[k] is None:
            low = part * 4
            owner = k // 2
            row = pl.ds((k % 2) * rows, rows)

            @pl.when(core == owner)
            def _():
                local = pltpu.make_async_copy(sums.at[k], shrink_o.at[row, span(core)], last_local.at[k])
                local.start()
                local.wait()
                pltpu.make_async_remote_copy(sums.at[k], shrink_o.at[row, span(1 - core)], last_send.at[k], last_recv.at[k],
                                             device_id=to["core"], device_id_type=MESH).wait_recv()

            @pl.when(core != owner)
            def _():
                copy = pltpu.make_async_remote_copy(sums.at[k], shrink_o.at[row, span(core)], last_send.at[k], last_recv.at[k],
                                                    device_id=to["core"], device_id_type=MESH)
                copy.start()
                copy.wait_send()
            return
        mine = sums.at[k, pl.ds(pl.multiple_of(core * part, 8), part)]
        other = sums.at[k, pl.ds(pl.multiple_of((1 - core) * part, 8), part)]
        local = pltpu.make_async_copy(mine, ends[k](core), last_local.at[k])
        local.start()
        copy = pltpu.make_async_remote_copy(other, ends[k](core), last_send.at[k], last_recv.at[k],
                                            device_id=to["core"], device_id_type=MESH)
        copy.start()
        final.append((local, copy, ends[k](1 - core), k))

    for t in range(len(lanes) + 2):
        for stage in range(3):
            if 0 <= t - stage < len(lanes):
                for unit in lanes[t - stage]:
                    unit.step(stage)
                    if stage == 2:
                        close(unit)
    for item in final:
        if not isinstance(item, tuple):
            item.wait()
            vec_o[...] = vsum[pl.ds(pl.multiple_of(core * 8, 8), 8)] + vother[...]
        else:
            local, copy, ref, k = item
            local.wait()
            copy.wait_send()
            pltpu.make_async_remote_copy(ref, ref, last_send.at[k], last_recv.at[k],
                                         device_id=to["core"], device_id_type=MESH).wait_recv()
    for unit in order:
        unit.finish()


def reduce_chips(far_count, grads):
    proj, maps, expand, shrink, vec = grads
    rows, wide = proj.shape[-2], proj.shape[-1]
    part = rows // 2
    any_space = pl.BlockSpec(memory_space=pl.ANY)
    vmem = pl.BlockSpec(memory_space=pltpu.VMEM)
    shapes = ((6, part, 2 * wide), (2, part, 2 * wide), (part, 8 * wide), (4 * part, 2 * wide), (8, 128))
    return pl.pallas_call(
        functools.partial(reduce_kernel, far_count),
        out_shape=[jax.ShapeDtypeStruct(shape, F32) for shape in shapes],
        in_specs=[any_space] * 5,
        out_specs=[vmem] * 5,
        scratch_shapes=[
            pltpu.VMEM((16, 2, far_count, rows, wide), LOW),
            pltpu.VMEM((16, 2, far_count, rows, wide), LOW),
            pltpu.VMEM((16, far_count, rows, wide), LOW),
            pltpu.VMEM((16, far_count - 1, rows, wide), LOW),
            pltpu.VMEM((2, far_count, 16, 128), F32),
            pltpu.VMEM((2, far_count, 16, 128), F32),
            pltpu.VMEM((far_count, 16, 128), F32),
            pltpu.VMEM((far_count - 1, 16, 128), F32),
            pltpu.VMEM((16, rows, wide), F32),
            pltpu.VMEM((16, 128), F32),
            pltpu.VMEM((8, 128), F32),
            pltpu.SemaphoreType.DMA((17, 6)),
            pltpu.SemaphoreType.DMA((17, 6)),
            pltpu.SemaphoreType.DMA((17, 2)),
            pltpu.SemaphoreType.DMA((17,)),
            pltpu.SemaphoreType.DMA((17,)),
            pltpu.SemaphoreType.DMA((17,)),
        ],
        compiler_params=pltpu.CompilerParams(
            collective_id=1, has_side_effects=True, vmem_limit_bytes=48 << 20
        ),
        name="sum_gradients",
    )(*grads)


def norm_apply(values, gain, shift):
    centre = values - jnp.mean(values, axis=-1, keepdims=True)
    spread = jnp.mean(centre * centre, axis=-1, keepdims=True)
    return centre * lax.rsqrt(spread + epsilon) * gain + shift


def gelu_exact(values):
    return jax.nn.gelu(values, approximate=False)


def heads_of(values):
    return values.reshape(values.shape[0], values.shape[1] // HEAD, HEAD)


def scores_of(queries, keys, valid):
    scores = jnp.einsum(
        "rhd,chd->hrc", heads_of(queries), heads_of(keys), preferred_element_type=F32
    ) * HEAD ** (-0.5)
    if valid is not None:
        scores = jnp.where(valid[None, None, :], scores, -1e30)
    return scores


def attend_forward(queries, keys, values, valid):
    scores = scores_of(queries, keys, valid)
    top = jnp.max(scores, axis=-1, keepdims=True)
    expon = jnp.exp(scores - top)
    total = jnp.sum(expon, axis=-1, keepdims=True)
    mixed = jnp.einsum(
        "hrc,chd->rhd", to_low(expon / total), heads_of(values), preferred_element_type=F32
    )
    return to_low(mixed.reshape(queries.shape)), top + jnp.log(total)


def attend_backward(queries, keys, values, valid, log_total, delta_mixed):
    probs = jnp.exp(scores_of(queries, keys, valid) - log_total)
    delta_heads = heads_of(delta_mixed)
    delta_values = jnp.einsum("hrc,rhd->chd", to_low(probs), delta_heads, preferred_element_type=F32)
    delta_probs = jnp.einsum("rhd,chd->hrc", delta_heads, heads_of(values), preferred_element_type=F32)
    row_delta = jnp.sum(delta_probs * probs, axis=-1, keepdims=True)
    score_low = to_low(probs * (delta_probs - row_delta))
    scale = HEAD ** (-0.5)
    delta_query = jnp.einsum("hrc,chd->rhd", score_low, heads_of(keys), preferred_element_type=F32) * scale
    delta_keys = jnp.einsum("hrc,rhd->chd", score_low, heads_of(queries), preferred_element_type=F32) * scale
    return (
        to_low(delta_query.reshape(queries.shape)),
        to_low(delta_keys.reshape(keys.shape)),
        to_low(delta_values.reshape(keys.shape)),
    )


def body(
    custom,
    tokens,
    memory,
    lengths,
    tokens_cotangent,
    memory_cotangent,
    projections,
    output_maps,
    expand_weight,
    shrink_weight,
    projection_bias,
    norm_gain,
    norm_bias,
    expand_bias,
    shrink_bias,
):
    share = lax.axis_index("mem")
    chips = lax.axis_size("seq")
    width = tokens.shape[1]
    hidden = expand_weight.shape[1]
    part = projections.shape[1]
    rows = 2 * part

    def block(values, axis):
        low = to_low(values)
        wide = axis + 1
        return join(half(low, share, wide), swap(half(low, 1 - share, wide)), axis)

    vectors = jnp.concatenate(
        [projection_bias, norm_gain, norm_bias, shrink_bias[None], expand_bias.reshape(-1, part)]
    )
    count = vectors.shape[0]
    vec = to_low(jnp.pad(vectors.reshape(-1), (0, 1024 - vectors.size)).reshape(8, 128))
    blocks = (
        block(projections, 1),
        block(output_maps, 1),
        block(expand_weight, 0),
        block(shrink_weight, 0),
        both(vec),
    )
    if custom:
        proj_all, maps_all, expand_mat, shrink_mat, vec_all = gather_chips(chips // 4, blocks)
        proj_all = proj_all.reshape(6, width, width // 2)
        maps_all = maps_all.reshape(2, width, width)
        expand_mat = expand_mat.reshape(width, hidden)
        shrink_mat = shrink_mat.reshape(hidden, width)
    else:
        gather = lambda values, axis: lax.all_gather(values, "seq", axis=axis, tiled=True)
        proj_all = gather(blocks[0], 1)
        maps_all = both(gather(blocks[1], 1), 2)
        expand_mat = both(gather(blocks[2], 0), 1)
        shrink_mat = both(gather(blocks[3], 0), 1)
        vec_all = gather(blocks[4], 0)
    vec_all = vec_all.reshape(2 * chips, 1024)[:, : vectors.size].astype(F32)
    vec_all = vec_all.reshape(2 * chips, count, part).transpose(1, 0, 2).reshape(count, width)
    biases, gains, shifts, shrink_shift = vec_all[0:6], vec_all[6:9], vec_all[9:12], vec_all[12]
    expand_shift = vec_all[13:].reshape(-1, 2 * chips, part).transpose(1, 0, 2).reshape(hidden)
    bias_half = half(biases, share, 1)

    own_count = tokens.shape[0]
    length = lengths[0]
    own_valid = share * own_count + jnp.arange(own_count) < length
    all_valid = jnp.arange(2 * own_count) < length
    inputs, rows_all, memory_cot = both(tokens), both(memory), both(memory_cotangent)

    pack_query = to_low(matmul(rows_all, proj_all[0]) + bias_half[0])
    pack_keys = to_low(matmul(inputs, proj_all[1]))
    pack_values = to_low(matmul(inputs, proj_all[2]) + bias_half[1])
    pack_own, pack_total = attend_forward(pack_query, pack_keys, pack_values, all_valid)
    pack_mixed = both(pack_own, 1)
    packed = matmul(pack_mixed, maps_all[0]) + biases[2]
    packed_low = to_low(packed)
    memory_sum = rows_all.astype(F32) + packed
    new_memory = norm_apply(half(memory_sum, share, 0), gains[0], shifts[0])
    unpack_keys = to_low(matmul(packed_low, proj_all[4]))
    unpack_values = to_low(matmul(packed_low, proj_all[5]) + bias_half[4])
    unpack_query = to_low(matmul(inputs, proj_all[3]) + bias_half[3])
    unpack_own, unpack_total = attend_forward(unpack_query, unpack_keys, unpack_values, None)
    unpack_mixed = both(unpack_own, 1)
    middle_sum = tokens.astype(F32) + matmul(half(unpack_mixed, share, 0), maps_all[1]) + biases[5]
    middle = norm_apply(middle_sum, gains[1], shifts[1])
    middle_low = to_low(middle)
    hidden_in = matmul(middle_low, expand_mat) + expand_shift
    hidden_low = to_low(gelu_exact(hidden_in))
    output_sum = middle + matmul(hidden_low, shrink_mat) + shrink_shift
    layer_out = norm_apply(output_sum, gains[2], shifts[2])
    new_tokens = jnp.where(own_valid[:, None], layer_out, 0.0)

    delta_out = jnp.where(own_valid[:, None], tokens_cotangent.astype(F32), 0.0)
    dropped, norm_back = jax.vjp(norm_apply, output_sum, gains[2], shifts[2])
    delta_sum2, delta_gain2, delta_shift2 = norm_back(delta_out)
    delta_branch = to_low(delta_sum2)
    delta_hidden = matmul_right(delta_branch, shrink_mat)
    dropped, gelu_back = jax.vjp(gelu_exact, hidden_in)
    delta_hidden_in = to_low(gelu_back(delta_hidden)[0])
    delta_shrink = matmul_left(
        both(hidden_low), join(half(delta_branch, share, 1), swap(half(delta_branch, 1 - share, 1)))
    )
    delta_expand = matmul_left(
        both(middle_low), join(half(delta_hidden_in, share, 1), swap(half(delta_hidden_in, 1 - share, 1)))
    )
    delta_middle = delta_sum2 + matmul_right(delta_hidden_in, expand_mat)
    dropped, norm_back = jax.vjp(norm_apply, middle_sum, gains[1], shifts[1])
    delta_sum1, delta_gain1, delta_shift1 = norm_back(delta_middle)
    delta_own = to_low(delta_sum1)
    delta_unpacked = both(delta_own)
    delta_map1 = matmul_left(unpack_mixed, half(delta_unpacked, share, 1))
    delta_mixed = to_low(matmul_right(delta_unpacked, half(maps_all[1], share, 0)))
    delta_uquery, delta_ukeys, delta_uvalues = attend_backward(
        unpack_query, unpack_keys, unpack_values, None, unpack_total, delta_mixed
    )
    delta_proj3 = matmul_left(inputs, delta_uquery)
    delta_proj4 = matmul_left(packed_low, delta_ukeys)
    delta_proj5 = matmul_left(packed_low, delta_uvalues)
    partial = matmul_right(delta_ukeys, proj_all[4]) + matmul_right(delta_uvalues, proj_all[5])
    dropped, norm_back = jax.vjp(norm_apply, memory_sum, gains[0], shifts[0])
    delta_sum0 = norm_back(memory_cot.astype(F32))[0]
    dropped, norm_back = jax.vjp(norm_apply, half(memory_sum, share, 0), gains[0], shifts[0])
    dropped, delta_gain0, delta_shift0 = norm_back(memory_cotangent.astype(F32))
    delta_packed = to_low(delta_sum0 + (partial + swap(partial)))
    delta_map0 = matmul_left(pack_mixed, half(delta_packed, share, 1))
    delta_mixed = to_low(matmul_right(delta_packed, half(maps_all[0], share, 0)))
    delta_pquery, delta_pkeys, delta_pvalues = attend_backward(
        pack_query, pack_keys, pack_values, all_valid, pack_total, delta_mixed
    )
    delta_proj0 = matmul_left(rows_all, delta_pquery)
    delta_proj1 = matmul_left(inputs, delta_pkeys)
    delta_proj2 = matmul_left(inputs, delta_pvalues)
    partial = matmul_right(delta_pquery, proj_all[0])
    memory_grad = half(delta_sum0, share, 0) + half(partial, share, 0) + swap(half(partial, 1 - share, 0))
    partial = (
        matmul_right(delta_uquery, proj_all[3])
        + matmul_right(delta_pkeys, proj_all[1])
        + matmul_right(delta_pvalues, proj_all[2])
    )
    tokens_grad = delta_sum1 + half(partial, share, 0) + swap(half(partial, 1 - share, 0))

    zero = jnp.zeros((1, width // 2), F32)

    def spread(values):
        return join(values, zero[0])

    bias_grads = [
        spread(column_sum(delta_pquery)),
        spread(column_sum(delta_pvalues)),
        column_sum(half(delta_packed, share, 0)),
        spread(column_sum(delta_uquery)),
        spread(column_sum(delta_uvalues)),
        column_sum(delta_own),
    ]
    vec_grads = jnp.stack(
        bias_grads
        + [delta_gain0, delta_gain1, delta_gain2, delta_shift0, delta_shift1, delta_shift2, column_sum(delta_branch)]
    )
    vec_grads = vec_grads.reshape(13, 2 * chips, part).transpose(1, 0, 2).reshape(2 * chips, 13 * part)
    vec_grads = jnp.concatenate([vec_grads, column_sum(delta_hidden_in).reshape(2 * chips, -1)], axis=1)
    vec_grads = jnp.pad(vec_grads, ((0, 0), (0, 1024 - vec_grads.shape[1])))
    grads = (
        [delta_proj0, delta_proj1, delta_proj2, delta_proj3, delta_proj4, delta_proj5],
        [delta_map0, delta_map1],
    )
    if custom:
        grid = (chips // 4, 2, 2)
        proj_o, maps_o, expand_o, shrink_o, vec_o = reduce_chips(
            chips // 4,
            (
                jnp.stack([to_low(g) for g in grads[0]]).reshape((6,) + grid + (rows, width // 2)),
                jnp.stack([to_low(g) for g in grads[1]]).reshape((2,) + grid + (rows, width // 2)),
                to_low(delta_expand).reshape(grid + (rows, hidden // 2)),
                to_low(delta_shrink).reshape(grid + (hidden // chips, width // 2)),
                vec_grads.reshape(grid + (16, 128)),
            ),
        )
    else:
        reduce = lambda values, axis: lax.psum_scatter(values, "seq", scatter_dimension=axis, tiled=True)

        def finish(values, axis):
            return join(half(values, share, axis), swap(half(values, 1 - share, axis)), axis + 1)

        proj_o = finish(reduce(jnp.stack(grads[0]), 1), 1)
        maps_o = finish(reduce(jnp.stack(grads[1]), 1), 1)
        expand_o = finish(reduce(delta_expand, 0), 0)
        shrink_o = finish(reduce(delta_shrink, 0), 0)
        vec_o = lax.psum_scatter(vec_grads, AXES, scatter_dimension=0, tiled=True)
    vec_o = vec_o.reshape(-1)
    small = vec_o[: 13 * part].reshape(13, part)
    return (
        new_tokens,
        new_memory,
        tokens_grad,
        memory_grad,
        proj_o,
        maps_o,
        expand_o,
        shrink_o,
        small[0:6],
        small[6:9],
        small[9:12],
        vec_o[13 * part : 13 * part + hidden // (2 * chips)],
        small[12],
    )


def solution(mesh):
    rows, stacked = P(AXES, None), P(None, AXES, None)
    table, line = P(None, AXES), P(AXES)
    custom = mesh.shape["seq"] == 16 and mesh.shape["mem"] == 2
    return jax.shard_map(
        functools.partial(body, custom),
        mesh=mesh,
        in_specs=(rows, rows, P("seq"), rows, rows, stacked, stacked, rows, rows, table, table, table, line, line),
        out_specs=(rows, rows, rows, rows, stacked, stacked, rows, rows, table, table, table, line, line),
        check_vma=False,
    )
```

```python
import functools

import jax
import jax.numpy as jnp
from jax import lax
from jax.experimental import pallas as pl
from jax.experimental.pallas import tpu as pltpu
from jax.sharding import PartitionSpec as P

HEAD = 64
epsilon = 1e-05
MESH = pl.DeviceIdType.MESH
LOW = jnp.bfloat16
F32 = jnp.float32
AXES = ("seq", "mem")


def matmul(left, right):
    return jnp.dot(left, right, preferred_element_type=F32)


def matmul_left(left, right):
    return lax.dot_general(left, right, (((0,), (0,)), ((), ())), preferred_element_type=F32)


def matmul_right(left, right):
    return lax.dot_general(left, right, (((1,), (1,)), ((), ())), preferred_element_type=F32)


def to_low(values):
    return values.astype(LOW)


def column_sum(values):
    return jnp.sum(values.astype(F32), axis=0)


def swap(values):
    return lax.ppermute(values, "mem", [(0, 1), (1, 0)])


def join(own, other, axis=0):
    first = lax.axis_index("mem") == 0
    return jnp.where(
        first, jnp.concatenate([own, other], axis), jnp.concatenate([other, own], axis)
    )


def both(values, axis=0):
    return join(values, swap(values), axis)


def half(values, index, axis):
    size = values.shape[axis] // 2
    return lax.dynamic_slice_in_dim(values, index * size, size, axis)


def place(seq):
    return lax.div(seq, 4), lax.rem(lax.div(seq, 2), 2), lax.rem(seq, 2)


def peers(seq, core, far_count):
    far, row, column = place(seq)
    flat = lambda f, r, c: f * 4 + r * 2 + c
    far_peers = [lax.rem(far + k, far_count) for k in range(1, far_count)]
    return {
        "far": [(flat(f, row, column), core) for f in far_peers],
        "far_index": far_peers,
        "column": (flat(far, row, 1 - column), core),
        "row": (flat(far, 1 - row, column), core),
        "core": (seq, 1 - core),
    }


def greet(targets):
    barrier = pltpu.get_barrier_semaphore()
    for target in targets:
        pl.semaphore_signal(barrier, inc=1, device_id=target, device_id_type=MESH)
    pl.semaphore_wait(barrier, len(targets))


class Gather:
    def __init__(self, where, to, first, own, at, shared, sems):
        self.where, self.to, self.own, self.at, self.shared = where, to, own, at, shared
        self.first, self.second = first, ("row" if first == "column" else "column")
        self.send, self.recv = sems
        self.started = []

    def _column(self, near):
        far, row, column = self.where
        row, column = (
            (1 - row if "row" in near else row),
            (1 - column if "column" in near else column),
        )
        return self.at(slice(None), row, column)

    def _copy(self, source, target, k, device):
        return pltpu.make_async_remote_copy(
            source, target, self.send.at[k], self.recv.at[k], device_id=device, device_id_type=MESH
        )

    def _go(self, *args):
        copy = self._copy(*args)
        copy.start()
        self.started.append(copy)

    def _arrived(self, ref, k):
        self._copy(ref, ref, k, self.to["core"]).wait_recv()

    def start(self):
        far, row, column = self.where
        mine = self.at(far, row, column)
        for k, device in enumerate(self.to["far"]):
            self._go(self.own, mine, k, device)

    def step(self, stage):
        far, row, column = self.where
        near = self._column(())
        if stage == 0:
            count = len(self.to["far"])
            for k in range(count):
                sender = self.to["far_index"][count - 1 - k]
                self._arrived(self.at(sender, row, column), k)
            self._go(near, near, 3, self.to[self.first])
            self._go(near, near, 4, self.to[self.second])
            if self.shared:
                self._go(near, near, 6, self.to["core"])
        if stage == 1:
            got = self._column((self.first,))
            self._arrived(got, 3)
            self._go(got, got, 5, self.to[self.second])
            if self.shared:
                self._go(got, got, 7, self.to["core"])
        if stage == 2:
            for k, names in ((4, (self.second,)), (5, (self.first, self.second))):
                got = self._column(names)
                self._arrived(got, k)
                if self.shared:
                    self._go(got, got, 4 + k, self.to["core"])
        if stage == 3 and self.shared:
            for k, names in enumerate(
                ((), (self.first,), (self.second,), (self.first, self.second))
            ):
                self._arrived(self._other(names), 6 + k)

    def _other(self, names):
        keep, self.at = self.at, self.shared
        ref = self._column(names)
        self.at = keep
        return ref

    def finish(self):
        for copy in self.started:
            copy.wait_send()


class GatherNear(Gather):
    def start(self):
        far, row, column = self.where
        mine = self.at(far, row, column)
        self._go(self.own, mine, 0, self.to[self.first])
        self._go(self.own, mine, 1, self.to[self.second])

    def _near(self, names):
        far, row, column = self.where
        return self.at(
            far, 1 - row if "row" in names else row, 1 - column if "column" in names else column
        )

    def step(self, stage):
        far = self.where[0]
        all_of = slice(None)
        count = len(self.to["far"])
        if stage == 0:
            got = self._near((self.first,))
            self._arrived(got, 0)
            self._go(got, got, 2, self.to[self.second])
        if stage == 1:
            self._arrived(self._near((self.second,)), 1)
            self._arrived(self._near((self.first, self.second)), 2)
            plane = self.at(far, all_of, all_of)
            for k, device in enumerate(self.to["far"]):
                self._go(plane, plane, 3 + k, device)
            if self.shared:
                self._go(plane, plane, 3 + count, self.to["core"])
        if stage == 2:
            for k in range(count):
                plane = self.at(self.to["far_index"][count - 1 - k], all_of, all_of)
                self._arrived(plane, 3 + k)
                if self.shared:
                    self._go(plane, plane, 4 + count + k, self.to["core"])
        if stage == 3 and self.shared:
            self._arrived(self.shared(far, all_of, all_of), 3 + count)
            for k in range(count):
                plane = self.shared(self.to["far_index"][count - 1 - k], all_of, all_of)
                self._arrived(plane, 4 + count + k)


def transposed(left, right):
    return lax.dot_general(left, right, (((0,), (0,)), ((), ())), preferred_element_type=F32)


def against(left, right):
    return lax.dot_general(left, right, (((1,), (1,)), ((), ())), preferred_element_type=F32)


def plain(left, right):
    return lax.dot_general(left, right, (((1,), (0,)), ((), ())), preferred_element_type=F32)


def over_rows(count, tile, work):
    def one(t, carry):
        work(pl.ds(pl.multiple_of(t * tile, tile), tile))
        return carry

    lax.fori_loop(0, count // tile, one, 0)


class Vectors:
    def __init__(self, to, held, arrived, send, recv):
        self.to, self.held, self.arrived, self.sems = to, held, arrived, (send, recv)
        self.flying = []

    def _go(self, k, device, slot):
        copy = pltpu.make_async_remote_copy(
            self.held.at[k], self.arrived.at[slot], self.sems[0].at[slot], self.sems[1].at[slot],
            device_id=device, device_id_type=MESH,
        )
        copy.start()
        self.flying.append((slot, copy))

    def start(self):
        self._go(0, self.to["core"], 0)

    def step(self, k):
        (slot, copy), = self.flying
        copy.wait()
        self.flying = []
        self.held[k] = self.held[k - 1] + self.arrived[slot]
        if k < 3:
            self._go(k, self.to[("core", "column", "row")[k]], k)
        else:
            for j, device in enumerate(self.to["far"]):
                self._go(3, device, 3 + j)

    def result(self):
        for slot, copy in self.flying:
            copy.wait()
        value = self.held[3]
        for slot, copy in self.flying:
            value = value + self.arrived[slot]
        return value


def attention_forward(pairs, queries, keys, values, valid, probs, mixed, first_lane, turned):
    for pair in range(*pairs):
        lanes = slice(pair * 128, pair * 128 + 128)
        query, key, value = queries[:, lanes] * LOW(HEAD ** (-0.5)), keys[:, lanes], values[:, lanes]
        outs = []
        for j in range(2):
            part = slice(j * HEAD, (j + 1) * HEAD)
            scores = against(key[:, part], query[:, part]) if turned else against(query[:, part], key[:, part])
            if valid is not None:
                scores = jnp.where(valid[...] > 0.5, scores, -1e30)
            axis = 0 if turned else 1
            expon = jnp.exp(scores - jnp.max(scores, axis=axis, keepdims=True))
            prob = (expon * (1.0 / jnp.sum(expon, axis=axis, keepdims=True))).astype(LOW)
            probs[pair * 2 + j] = prob
            outs.append((transposed if turned else plain)(prob, value[:, part]))
        mixed[:, pl.ds(pl.multiple_of(first_lane + pair * 128, 128), 128)] = jnp.concatenate(outs, axis=1).astype(LOW)


def norm_parts(values):
    centre = values - jnp.mean(values, axis=-1, keepdims=True)
    factor = lax.rsqrt(jnp.mean(centre * centre, axis=-1, keepdims=True) + epsilon)
    return centre * factor, factor


def norm_backward(unit, factor, gain, delta):
    scaled = delta * gain
    return factor * (scaled - jnp.mean(scaled, axis=-1, keepdims=True) - unit * jnp.mean(scaled * unit, axis=-1, keepdims=True))


def total_rows(values):
    return jnp.sum(values, axis=0, keepdims=True)


def gather_kernel(far_count, proj, maps, expand, shrink, vec, tokens, rows_in, valid, own_valid, token_cot, memory_cot,
                  proj_o, maps_o, expand_o, shrink_o, vec_o, hidden_o, middle_full_o, d_branch_x_o,
                  inputs_o, memory_o, qp_o, kp_o, vp_o, qu_o, ku_o, vu_o,
                  probs_p_o, probs_u_o, mixed_p_o, mixed_u_o, packed_o, new_memory_o, middle_sum_o,
                  slope_o, d_sum2_o, d_branch_o, new_tokens_o, d_sum0_o, grad_table_o,
                  inputs, memory, qp, kp, vp, qu, ku, vu, probs_p, probs_u, mixed_p, mixed_u, packed, new_memory, middle_sum,
                  slope, d_sum2, d_branch, new_tokens, d_sum0, grad_table,
                  memory_sum, middle, middle_low, hidden, cot, expand_w, shrink_w,
                  weights, map_p, map_u, held, arrived, table,
                  send, recv, local, out_sems, cross_send, cross_recv, vec_send, vec_recv):
    seq, core = lax.axis_index("seq"), lax.axis_index("mem")
    where = place(seq)
    far, row, column = where
    to = peers(seq, core, far_count)
    wide = maps.shape[-1]
    own_tokens, own_rows = tokens.shape[0], rows_in.shape[0]

    def cols(which, start=0):
        return pl.ds(pl.multiple_of(which * expand.shape[-1] + start, 128), wide)

    def span(which):
        return pl.ds(pl.multiple_of(which * wide, 128), wide)

    copies, stores = [], []

    def keep(source, target):
        copy = pltpu.make_async_copy(source, target, local.at[len(copies)])
        copy.start()
        copies.append(copy)
        return copy

    def store(source, target):
        copy = pltpu.make_async_copy(source, target, out_sems.at[len(stores)])
        copy.start()
        stores.append(copy)

    keep(proj, proj_o.at[:, far, row, column])
    keep(maps, maps_o.at[:, far, row, column, :, span(core)])
    keep(expand, expand_o.at[far, row, column, :, pl.ds(pl.multiple_of(core * expand.shape[-1], 128), expand.shape[-1])])
    keep(shrink, shrink_o.at[far, row, column, :, span(core)])
    own_t = pl.ds(pl.multiple_of(core * own_tokens, 128), own_tokens)
    own_m = pl.ds(pl.multiple_of(core * own_rows, 128), own_rows)
    keep(tokens, inputs.at[own_t])
    keep(rows_in, memory.at[own_m])
    keep(memory_cot, cot.at[own_m])

    units = []

    def add(first, own, at, shared, kind=Gather):
        k = len(units)
        units.append(kind(where, to, first, own, at, shared, (send.at[k], recv.at[k])))

    def add_proj(first, p):
        add(first, proj.at[p], lambda f, r, c: proj_o.at[p, f, r, c], None)

    def add_map(first, p):
        add(first, maps.at[p], lambda f, r, c: maps_o.at[p, f, r, c, :, span(core)],
            lambda f, r, c: maps_o.at[p, f, r, c, :, span(1 - core)])

    def add_expand(first, k):
        add(first, expand.at[:, pl.ds(k * wide, wide)], lambda f, r, c: expand_o.at[f, r, c, :, cols(core, k * wide)],
            lambda f, r, c: expand_o.at[f, r, c, :, cols(1 - core, k * wide)])

    def add_shrink(first, k):
        rows = shrink.shape[0] // 4
        part = pl.ds(k * rows, rows)
        add(first, shrink.at[part], lambda f, r, c: shrink_o.at[f, r, c, part, span(core)],
            lambda f, r, c: shrink_o.at[f, r, c, part, span(1 - core)], GatherNear if k >= 2 else Gather)

    for first, second in (
        ((add_proj, 0), (add_proj, 1)), ((add_proj, 2), (add_map, 0)), ((add_proj, 4), (add_proj, 5)), ((add_proj, 3), (add_map, 1)),
        ((add_expand, 0), (add_expand, 1)), ((add_expand, 2), (add_expand, 3)), ((add_shrink, 0), (add_shrink, 1)), ((add_shrink, 2), (add_shrink, 3)),
    ):
        first[0]("column", first[1])
        second[0]("row", second[1])

    held[0] = vec[...]
    vectors = Vectors(to, held, arrived, vec_send, vec_recv)

    def cross(k, source, target):
        copy = pltpu.make_async_remote_copy(source, target, cross_send.at[k], cross_recv.at[k], device_id=to["core"], device_id_type=MESH)
        copy.start()
        return copy

    greet(to["far"] + [to["column"], to["row"], to["core"]])
    vectors.start()
    crossed = [cross(0, tokens, inputs.at[own_t]), cross(1, rows_in, memory.at[own_m]), cross(4, memory_cot, cot.at[own_m])]
    for unit in units:
        unit.start()
    vectors.step(1)
    for copy in copies:
        copy.wait()
    lanes = [units[k:k + 2] for k in range(0, len(units), 2)]
    late = lanes.pop()
    plan = [(t + stage, -stage, lane, stage) for t, lane in enumerate(lanes) for stage in range(4)]
    plan += [(time, -9, late, stage) for stage, time in enumerate((0.5, 2.5, len(lanes) + 0.5, len(lanes) + 2.5))]
    plan = sorted(plan, key=lambda step: step[:2])
    taken = [0]

    def advance(until):
        while taken[0] < len(plan) and plan[taken[0]][0] <= until:
            time, rank, lane, stage = plan[taken[0]]
            taken[0] += 1
            for unit in lane:
                unit.step(stage)

    fetched = {}

    def fetch_proj(p):
        size = proj_o.shape[-2]
        copy = pltpu.make_async_copy(proj_o.at[p], weights.at[p], local.at[7 + p])
        copy.start()
        fetched[p] = copy

    def fetch_map(p, target):
        copy = pltpu.make_async_copy(maps_o.at[p], target, local.at[13 + p])
        copy.start()
        fetched[6 + p] = copy

    def weight(p):
        return weights[p].reshape(-1, wide)

    def project(p, source, target, bias):
        fetched[p].wait()

        def one(piece):
            value = plain(source[piece], weight(p))
            if bias is not None:
                value = value + table[bias : bias + 1, span(core)]
            target[piece] = value.astype(LOW)

        over_rows(source.shape[0], 256, one)

    def gain(k):
        return table[6 + k : 7 + k]

    def shift(k):
        return table[9 + k : 10 + k]

    advance(0)
    vectors.step(2)
    advance(0.5)
    vectors.step(3)
    advance(1)
    table[...] = vectors.result()
    store(table, vec_o)
    for copy in crossed:
        copy.wait()
    store(inputs, inputs_o)
    store(memory, memory_o)
    advance(2)
    fetch_proj(0)
    fetch_proj(1)
    project(0, memory, qp, 0)
    project(1, inputs, kp, None)
    advance(3)
    fetch_proj(2)
    project(2, inputs, vp, 1)
    attention_forward((0, 1), qp, kp, vp, valid, probs_p, mixed_p, core * wide, False)
    advance(3.5)
    attention_forward((1, 3), qp, kp, vp, valid, probs_p, mixed_p, core * wide, False)
    packing = cross(2, mixed_p.at[:, span(core)], mixed_p.at[:, span(core)])
    advance(4)
    fetch_map(0, map_p)
    fetch_proj(4)
    fetch_proj(5)
    packing.wait_send()
    pltpu.make_async_remote_copy(mixed_p.at[:, span(1 - core)], mixed_p.at[:, span(1 - core)], cross_send.at[2], cross_recv.at[2],
                                 device_id=to["core"], device_id_type=MESH).wait_recv()
    fetched[6].wait()
    for source, target in ((qp, qp_o), (kp, kp_o), (vp, vp_o), (probs_p, probs_p_o), (mixed_p, mixed_p_o)):
        store(source, target)
    value = plain(mixed_p[...], map_p[...].reshape(-1, 2 * wide)) + table[2:3]
    packed[...] = value.astype(LOW)
    memory_sum[...] = memory[...].astype(F32) + value
    project(4, packed, ku, None)
    project(5, packed, vu, 4)
    unit, factor = norm_parts(memory_sum[...])
    memory_sum[...] = unit
    d_sum0[...] = norm_backward(unit, factor, gain(0), cot[...].astype(F32))
    unit, delta = memory_sum[own_m], memory_cot[...].astype(F32)
    new_memory[...] = unit * gain(0) + shift(0)
    grad_table[...] = jnp.zeros_like(grad_table)
    grad_table[6:7] = total_rows(delta * unit)
    grad_table[9:10] = total_rows(delta)
    advance(5)
    fetch_proj(3)
    for source, target in ((packed, packed_o), (d_sum0, d_sum0_o), (new_memory, new_memory_o), (ku, ku_o), (vu, vu_o)):
        store(source, target)
    project(3, inputs, qu, 3)
    attention_forward((0, 1), qu, ku, vu, None, probs_u, mixed_u, core * wide, True)
    advance(6)
    fetch_map(1, map_u)
    attention_forward((1, 3), qu, ku, vu, None, probs_u, mixed_u, core * wide, True)
    unpacking = cross(3, mixed_u.at[:, span(core)], mixed_u.at[:, span(core)])
    advance(7)
    unpacking.wait_send()
    pltpu.make_async_remote_copy(mixed_u.at[:, span(1 - core)], mixed_u.at[:, span(1 - core)], cross_send.at[3], cross_recv.at[3],
                                 device_id=to["core"], device_id_type=MESH).wait_recv()
    for source, target in ((qu, qu_o), (probs_u, probs_u_o), (mixed_u, mixed_u_o)):
        store(source, target)
    fetched[7].wait()

    def attended(t, carry):
        here = pl.ds(pl.multiple_of(t * 256, 256), 256)
        there = pl.ds(pl.multiple_of(core * own_tokens + t * 256, 256), 256)
        value = plain(mixed_u[there], map_u[...].reshape(-1, 2 * wide)) + table[5:6]
        value = tokens[here].astype(F32) + value
        middle_sum[here] = value
        value = norm_parts(value)[0] * gain(1) + shift(1)
        middle[here] = value
        middle_low[here] = value.astype(LOW)
        return carry

    lax.fori_loop(0, own_tokens // 256, attended, 0)
    store(middle_sum, middle_sum_o)
    store(middle_low, middle_full_o.at[own_t])
    sent = [cross(5, middle_low, middle_full_o.at[own_t])]
    tall = 2 * wide
    first_bias = 13

    def widen(n):
        columns = pl.ds(n * tall, tall)
        fetched[8 + n].wait()
        value = plain(middle_low[...], expand_w[:, :, :, :, columns].reshape(-1, tall)) + table[first_bias + n : first_bias + n + 1]
        share = 0.5 + 0.5 * lax.erf(value * 0.5**0.5)
        hidden[:, columns] = (value * share).astype(LOW)
        slope[:, columns] = (share + value * (0.3989422804014327 * jnp.exp(-0.5 * value * value))).astype(LOW)
        store(hidden.at[:, columns], hidden_o.at[own_t, columns])
        sent.append(cross(6 + n, hidden.at[:, columns], hidden_o.at[own_t, columns]))

    def fetch_expand(n):
        columns = pl.ds(n * tall, tall)
        copy = pltpu.make_async_copy(expand_o.at[:, :, :, :, columns], expand_w.at[:, :, :, :, columns], local.at[15 + n])
        copy.start()
        fetched[8 + n] = copy

    fetch_expand(0)
    fetch_expand(2)
    widen(0)
    advance(7.5)
    widen(2)
    advance(8)
    fetch_expand(1)
    fetch_expand(3)
    widen(1)
    advance(8.5)
    widen(3)
    store(slope, slope_o)
    advance(99)
    last = pltpu.make_async_copy(shrink_o, shrink_w, local.at[19])
    last.start()
    last.wait()

    def narrow(t, carry):
        here = pl.ds(pl.multiple_of(t * 256, 256), 256)
        value = middle[here] + (plain(hidden[here], shrink_w[...].reshape(-1, 2 * wide)) + table[12:13])
        unit, factor = norm_parts(value)
        live = own_valid[here] > 0.5
        new_tokens[here] = jnp.where(live, unit * gain(2) + shift(2), 0.0)
        delta = jnp.where(live, token_cot[here].astype(F32), 0.0)
        grad_table[8:9] += total_rows(delta * unit)
        grad_table[11:12] += total_rows(delta)
        value = norm_backward(unit, factor, gain(2), delta)
        d_sum2[here] = value
        value = value.astype(LOW)
        d_branch[here] = value
        grad_table[12:13] += total_rows(value.astype(F32))
        return carry

    lax.fori_loop(0, own_tokens // 256, narrow, 0)
    sent.append(cross(10, d_branch.at[:, span(1 - core)], d_branch_x_o.at[own_t]))
    store(d_branch.at[:, span(core)], d_branch_x_o.at[own_t])
    for source, target in ((d_sum2, d_sum2_o), (d_branch, d_branch_o), (new_tokens, new_tokens_o), (grad_table, grad_table_o)):
        store(source, target)
    for copy in sent:
        copy.wait()
    for copy in stores:
        copy.wait()
    for unit in units:
        unit.finish()


def gather_chips(far_count, blocks, vec, tokens, memory, valid, own_valid, token_cot, memory_cot):
    proj, maps, expand, shrink = blocks
    grid = (far_count, 2, 2)
    rows, wide = proj.shape[1:]
    width, hidden = 2 * wide, 2 * expand.shape[1]
    own_tokens, own_rows = tokens.shape[0], memory.shape[0]
    all_tokens, all_rows = 2 * own_tokens, 2 * own_rows
    count = wide // HEAD
    passed = (
        ((6,) + grid + proj.shape[1:], LOW),
        ((2,) + grid + (rows, width), LOW),
        (grid + (rows, hidden), LOW),
        (grid + (shrink.shape[0], width), LOW),
        (vec.shape, F32),
        ((all_tokens, hidden), LOW),
        ((all_tokens, width), LOW),
        ((all_tokens, wide), LOW),
    )
    kept = (
        ((all_tokens, width), LOW),
        ((all_rows, width), LOW),
        ((all_rows, wide), LOW),
        ((all_tokens, wide), LOW),
        ((all_tokens, wide), LOW),
        ((all_tokens, wide), LOW),
        ((all_rows, wide), LOW),
        ((all_rows, wide), LOW),
        ((count, all_rows, all_tokens), LOW),
        ((count, all_rows, all_tokens), LOW),
        ((all_rows, width), LOW),
        ((all_tokens, width), LOW),
        ((all_rows, width), LOW),
        ((own_rows, width), F32),
        ((own_tokens, width), F32),
        ((own_tokens, hidden), LOW),
        ((own_tokens, width), F32),
        ((own_tokens, width), LOW),
        ((own_tokens, width), F32),
        ((all_rows, width), F32),
        (vec.shape, F32),
    )
    inner = (
        ((all_rows, width), F32),
        ((own_tokens, width), F32),
        ((own_tokens, width), LOW),
        ((own_tokens, hidden), LOW),
        ((all_rows, width), LOW),
        passed[2],
        passed[3],
        passed[0],
        (passed[1][0][1:], LOW),
        (passed[1][0][1:], LOW),
        ((4,) + vec.shape, F32),
        ((2 + far_count,) + vec.shape, F32),
        (vec.shape, F32),
    )
    any_space = pl.BlockSpec(memory_space=pl.ANY)
    return pl.pallas_call(
        functools.partial(gather_kernel, far_count),
        out_shape=[jax.ShapeDtypeStruct(*entry) for entry in passed + kept],
        in_specs=[pl.BlockSpec(memory_space=pltpu.VMEM)] * 11,
        out_specs=[any_space] * (len(passed) + len(kept)),
        scratch_shapes=[pltpu.VMEM(*entry) for entry in kept + inner]
        + [
            pltpu.SemaphoreType.DMA((16, 10)),
            pltpu.SemaphoreType.DMA((16, 10)),
            pltpu.SemaphoreType.DMA((20,)),
            pltpu.SemaphoreType.DMA((32,)),
            pltpu.SemaphoreType.DMA((11,)),
            pltpu.SemaphoreType.DMA((11,)),
            pltpu.SemaphoreType.DMA((2 + far_count,)),
            pltpu.SemaphoreType.DMA((2 + far_count,)),
        ],
        compiler_params=pltpu.CompilerParams(
            collective_id=0, has_side_effects=True, vmem_limit_bytes=62 << 20
        ),
        name="gather_and_forward",
    )(*blocks, vec, tokens, memory, valid, own_valid, token_cot, memory_cot)


class Reduce:
    def __init__(self, where, to, first, at, total, half_in, quarter_in, far_in, sems, kind):
        self.where, self.to, self.at, self.total = where, to, at, total
        self.half_in, self.quarter_in, self.far_in, self.kind = half_in, quarter_in, far_in, kind
        self.first, self.second = first, ("row" if first == "column" else "column")
        self.send, self.recv, self.load = sems
        self.started, self.loads = [], []

    def _copy(self, source, target, k, device):
        return pltpu.make_async_remote_copy(
            source, target, self.send.at[k], self.recv.at[k], device_id=device, device_id_type=MESH
        )

    def _go(self, *args):
        copy = self._copy(*args)
        copy.start()
        self.started.append(copy)

    def _arrived(self, ref, k):
        self._copy(ref, ref, k, self.to["core"]).wait_recv()

    def _column(self, near):
        far, row, column = self.where
        row, column = (
            (1 - row if "row" in near else row),
            (1 - column if "column" in near else column),
        )
        return self.at(slice(None), row, column)

    def start(self):
        for k, names in enumerate(((self.second,), (self.first, self.second))):
            self._go(self._column(names), self.half_in.at[k], k, self.to[self.second])
        for k, names in enumerate(((), (self.first,))):
            copy = pltpu.make_async_copy(self._column(names), self.total.at[k], self.load.at[k])
            copy.start()
            self.loads.append(copy)

    def _add(self, target, other):
        count = target.shape[0]
        for k in range(count):
            target[k] = (target[k].astype(F32) + other[k].astype(F32)).astype(self.kind)

    def step(self, stage):
        count = len(self.to["far"])
        if stage == 0:
            self.loads[1].wait()
            self._arrived(self.half_in.at[1], 1)
            self._add(self.total.at[1], self.half_in.at[1])
            self._go(self.total.at[1], self.quarter_in, 2, self.to[self.first])
            self.loads[0].wait()
            self._arrived(self.half_in.at[0], 0)
            self._add(self.total.at[0], self.half_in.at[0])
        if stage == 1:
            self._arrived(self.quarter_in, 2)
            self._add(self.total.at[0], self.quarter_in)
            for k, device in enumerate(self.to["far"]):
                self._go(self.total.at[0, self.to["far_index"][k]], self.far_in.at[k], 3 + k, device)
        if stage == 2:
            for k in range(count):
                self._arrived(self.far_in.at[k], 3 + k)

    def result(self):
        value = self.total[0, self.where[0]].astype(F32)
        for k in range(len(self.to["far"])):
            value = value + self.far_in[k].astype(F32)
        return value

    def finish(self):
        for copy in self.started:
            copy.wait_send()


def attention_backward(pairs, queries, keys, values, probs, mixed, d_query, d_key, d_value, turned):
    scale = HEAD ** (-0.5)
    for pair in range(*pairs):
        lanes = slice(pair * 128, pair * 128 + 128)
        query, delta = queries[:, lanes], mixed[:, lanes]
        key, value = keys[:, lanes], values[:, lanes]
        by_query, by_key = (transposed, plain) if turned else (plain, transposed)
        parts = ([], [], [])
        for j in range(2):
            part = slice(j * HEAD, (j + 1) * HEAD)
            prob_low = probs[pair * 2 + j]
            prob = prob_low.astype(F32)
            d_prob = against(value[:, part], delta[:, part]) if turned else against(delta[:, part], value[:, part])
            row_delta = jnp.sum(d_prob * prob, axis=0 if turned else 1, keepdims=True)
            d_score = (prob * (d_prob - row_delta)).astype(LOW)
            parts[0].append(by_query(d_score, key[:, part]))
            parts[1].append(by_key(d_score, query[:, part]))
            parts[2].append(by_key(prob_low, delta[:, part]))
        d_query[:, lanes] = (jnp.concatenate(parts[0], axis=1) * scale).astype(LOW)
        d_key[:, lanes] = (jnp.concatenate(parts[1], axis=1) * scale).astype(LOW)
        d_value[:, lanes] = jnp.concatenate(parts[2], axis=1).astype(LOW)


def reduce_kernel(far_count, expand, shrink, vectors_in, d_unpacked_h, mixed_u_h, mixed_p_h, inputs_h, memory_h,
                  qu_h, ku_h, vu_h, qp_h, kp_h, vp_h, probs_u_h, probs_p_h, packed_h, d_sum0_h, d_sum1_h, proj_h, maps_h,
                  proj_o, maps_o, expand_o, shrink_o, vec_o, tokens_o, memory_o,
                  total, half_in, quarter_in, far_in, vec_sum, vec_in, sums,
                  d_unpacked, mixed_u, mixed_p, inputs, memory, qu, ku, vu, qp, kp, vp, probs_u, probs_p, packed, d_sum0, d_sum1,
                  weights, map_u, map_p, grads, d_mixed, d_query, d_key, d_value, d_token_key, d_token_value, d_packed,
                  partial, partial_in, wide_out, wide_in, rows_out, rows_in,
                  send, recv, load, last_send, last_recv, last_local, in_sems, cross_send, cross_recv, vec_send, vec_recv):
    seq, core = lax.axis_index("seq"), lax.axis_index("mem")
    where = place(seq)
    to = peers(seq, core, far_count)
    wide = proj_h.shape[-1]
    rows = proj_o.shape[-2] * 2
    part = rows // 2
    own_rows = d_sum1.shape[0]
    mem_rows = packed.shape[0] // 2
    units, ends = [], []

    def span(which, start=0, whole=None):
        return pl.ds(pl.multiple_of(which * (whole or wide) + start, 128), wide)

    loads = {}

    def fetch(name, source, target):
        copy = pltpu.make_async_copy(source, target, in_sems.at[len(loads)])
        copy.start()
        loads[name] = copy

    def need(*names):
        for name in names:
            loads[name].wait()

    fetch("d_unpacked", d_unpacked_h, d_unpacked)
    mine = pl.ds(pl.multiple_of(core * wide, 128), wide)
    fetch("map_u", maps_h.at[1, mine], map_u)
    for name, source, target in (
        ("mixed_u", mixed_u_h, mixed_u), ("qu", qu_h, qu), ("ku", ku_h, ku), ("vu", vu_h, vu), ("probs_u", probs_u_h, probs_u),
        ("inputs", inputs_h, inputs), ("packed", packed_h, packed), ("weights", proj_h, weights), ("d_sum0", d_sum0_h, d_sum0),
        ("vectors", vectors_in, vec_sum.at[0]), ("map_p", maps_h.at[0, mine], map_p), ("mixed_p", mixed_p_h, mixed_p), ("qp", qp_h, qp), ("kp", kp_h, kp),
        ("vp", vp_h, vp), ("probs_p", probs_p_h, probs_p), ("memory", memory_h, memory), ("d_sum1", d_sum1_h, d_sum1),
    ):
        fetch(name, source, target)

    def add(at, end):
        k = len(units)
        first = "column" if k % 2 == 0 else "row"
        units.append(Reduce(where, to, first, at, total.at[k], half_in.at[k], quarter_in.at[k], far_in.at[k],
                            (send.at[k], recv.at[k], load.at[k]), LOW))
        ends.append(end)

    def add_expand(k):
        add(lambda f, r, c: expand.at[f, r, c, :, pl.ds(k * wide, wide)],
            lambda which: expand_o.at[:, span(which, k * wide, expand.shape[-1])])

    def add_shrink(k):
        add(lambda f, r, c: shrink.at[f, r, c, pl.ds(k * rows, rows)], None)

    def add_map(p):
        add(lambda f, r, c: grads.at[6 + p, f, r, c], lambda which: maps_o.at[p, :, span(which)])

    def add_proj(p):
        add(lambda f, r, c: grads.at[p, f, r, c], lambda which: proj_o.at[p, :, span(which)])

    for k in range(4):
        add_shrink(k)
    for k in range(4):
        add_expand(k)
    for make, p in ((add_map, 1), (add_proj, 3), (add_proj, 4), (add_proj, 5), (add_map, 0), (add_proj, 0), (add_proj, 1), (add_proj, 2)):
        make(p)

    greet(to["far"] + [to["column"], to["row"], to["core"]])
    bias_sums = Vectors(to, vec_sum, vec_in, vec_send, vec_recv)
    lanes = [units[k:k + 2] for k in range(0, 16, 2)]
    final = []
    index = {id(unit): k for k, unit in enumerate(units)}

    def close(unit):
        k = index[id(unit)]
        sums[k] = unit.result()
        if ends[k] is None:
            owner = k // 2
            row = pl.ds((k % 2) * rows, rows)

            @pl.when(core == owner)
            def _():
                local = pltpu.make_async_copy(sums.at[k], shrink_o.at[row, span(core)], last_local.at[k])
                local.start()
                local.wait()
                pltpu.make_async_remote_copy(sums.at[k], shrink_o.at[row, span(1 - core)], last_send.at[k], last_recv.at[k],
                                             device_id=to["core"], device_id_type=MESH).wait_recv()

            @pl.when(core != owner)
            def _():
                copy = pltpu.make_async_remote_copy(sums.at[k], shrink_o.at[row, span(core)], last_send.at[k], last_recv.at[k],
                                                    device_id=to["core"], device_id_type=MESH)
                copy.start()
                copy.wait_send()
            return
        own = sums.at[k, pl.ds(pl.multiple_of(core * part, 8), part)]
        other = sums.at[k, pl.ds(pl.multiple_of((1 - core) * part, 8), part)]
        local = pltpu.make_async_copy(own, ends[k](core), last_local.at[k])
        local.start()
        copy = pltpu.make_async_remote_copy(other, ends[k](core), last_send.at[k], last_recv.at[k],
                                            device_id=to["core"], device_id_type=MESH)
        copy.start()
        final.append((local, copy, ends[k](1 - core), k))

    def advance(t):
        if 2 <= t + 1 < len(lanes):
            for unit in lanes[t + 1]:
                unit.start()
        for stage in range(3):
            if 0 <= t - stage < len(lanes):
                for unit in lanes[t - stage]:
                    unit.step(stage)
                    if stage == 2:
                        close(unit)

    def weight_grad(slot, left, right):
        def one(piece, carry):
            value = transposed(left[:, pl.ds(pl.multiple_of(piece * wide, 128), wide)], right).astype(LOW)
            count = wide // rows
            for b in range(count):
                grads[slot, piece * (count // 4) + b // 4, (b // 2) % 2, b % 2] = value[b * rows : (b + 1) * rows]
            return carry

        lax.fori_loop(0, left.shape[1] // wide, one, 0)

    def put_bias(row, values):
        vec_sum[0, row : row + 1, span(core)] = jnp.sum(values.astype(F32), axis=0, keepdims=True)

    def cross(k, source, target):
        copy = pltpu.make_async_remote_copy(source, target, cross_send.at[k], cross_recv.at[k], device_id=to["core"], device_id_type=MESH)
        copy.start()
        return copy

    for lane in lanes[:2]:
        for unit in lane:
            unit.start()

    need("d_unpacked", "map_u")

    def from_map_u(piece):
        d_mixed[piece] = against(d_unpacked[piece], map_u[...]).astype(LOW)

    over_rows(d_unpacked.shape[0], 256, from_map_u)
    need("mixed_u")
    weight_grad(7, mixed_u, d_unpacked[:, span(core)])
    advance(0)
    need("qu", "ku", "vu", "probs_u")
    unpack = (qu, ku, vu, probs_u, d_mixed, d_query, d_key, d_value, True)
    attention_backward((0, 2), *unpack)
    advance(1)
    attention_backward((2, 3), *unpack)
    need("inputs", "packed", "weights", "d_sum0", "vectors")

    def from_query(piece):
        wide_out[piece] = against(d_query[piece], weights[3])

    partial[...] = against(d_key[...], weights[4]) + against(d_value[...], weights[5])
    packing = cross(0, partial, partial_in)
    weight_grad(3, inputs, d_query[...])
    weight_grad(4, packed, d_key[...])
    weight_grad(5, packed, d_value[...])
    put_bias(3, d_query[...])
    put_bias(4, d_value[...])
    over_rows(d_query.shape[0], 256, from_query)
    advance(2)

    packing.wait()
    d_packed[...] = (d_sum0[...] + (partial[...] + partial_in[...])).astype(LOW)
    need("map_p", "mixed_p")
    d_mixed_p = d_mixed.at[pl.ds(0, 2 * mem_rows)]
    d_mixed_p[...] = against(d_packed[...], map_p[...]).astype(LOW)
    weight_grad(6, mixed_p, d_packed[:, span(core)])
    vec_sum[0, 2:3, :] = jnp.sum(d_packed[pl.ds(pl.multiple_of(core * mem_rows, 128), mem_rows)].astype(F32), axis=0, keepdims=True)
    need("qp", "kp", "vp", "probs_p")
    pack = (qp, kp, vp, probs_p, d_mixed_p, d_key, d_token_key, d_token_value, False)
    attention_backward((0, 1), *pack)
    advance(3)
    attention_backward((1, 3), *pack)
    need("memory")
    weight_grad(0, memory, d_key[...])
    weight_grad(1, inputs, d_token_key[...])
    advance(4)
    weight_grad(2, inputs, d_token_value[...])
    put_bias(0, d_key[...])
    put_bias(1, d_token_value[...])

    bias_sums.start()
    rows_out[...] = against(d_key[...], weights[0])

    def from_token_keys(piece):
        wide_out[piece] = wide_out[piece] + against(d_token_key[piece], weights[1]) + against(d_token_value[piece], weights[2])

    over_rows(d_query.shape[0], 256, from_token_keys)
    own = pl.ds(pl.multiple_of(core * own_rows, 128), own_rows)
    other = pl.ds(pl.multiple_of((1 - core) * own_rows, 128), own_rows)
    own_mem = pl.ds(pl.multiple_of(core * mem_rows, 128), mem_rows)
    other_mem = pl.ds(pl.multiple_of((1 - core) * mem_rows, 128), mem_rows)
    token_terms = cross(1, wide_out.at[other], wide_in)
    memory_terms = cross(2, rows_out.at[other_mem], rows_in)
    advance(5)
    bias_sums.step(1)
    token_terms.wait()
    need("d_sum1")

    def close_tokens(piece):
        tokens_o[piece] = d_sum1[piece] + wide_in[piece]

    over_rows(own_rows, 128, close_tokens)
    tokens_o[...] = tokens_o[...] + wide_out[own]
    memory_terms.wait()
    memory_o[...] = d_sum0[own_mem] + rows_out[own_mem] + rows_in[...]
    advance(6)
    bias_sums.step(2)
    advance(7)
    bias_sums.step(3)
    advance(8)
    advance(9)
    vec_o[...] = bias_sums.result()
    for local, copy, ref, k in final:
        local.wait()
        copy.wait_send()
        pltpu.make_async_remote_copy(ref, ref, last_send.at[k], last_recv.at[k],
                                     device_id=to["core"], device_id_type=MESH).wait_recv()
    for unit in units:
        unit.finish()


def reduce_chips(far_count, expand, shrink, vectors, arrays):
    (d_unpacked, mixed_u, mixed_p, inputs, memory, qu, ku, vu, qp, kp, vp, probs_u, probs_p, packed, d_sum0, d_sum1, proj, maps) = arrays
    rows, wide = expand.shape[-2], proj.shape[-1]
    part = rows // 2
    width = inputs.shape[1]
    any_space = pl.BlockSpec(memory_space=pl.ANY)
    vmem = pl.BlockSpec(memory_space=pltpu.VMEM)
    shapes = ((6, part, 2 * wide), (2, part, 2 * wide), (part, 8 * wide), (4 * part, 2 * wide), vectors.shape, d_sum1.shape, (memory.shape[0] // 2, width))
    tokens = inputs.shape[0]
    like = lambda array: pltpu.VMEM(array.shape, array.dtype)
    return pl.pallas_call(
        functools.partial(reduce_kernel, far_count),
        out_shape=[jax.ShapeDtypeStruct(shape, F32) for shape in shapes],
        in_specs=[any_space] * 21,
        out_specs=[vmem] * 7,
        scratch_shapes=[
            pltpu.VMEM((16, 2, far_count, rows, wide), LOW),
            pltpu.VMEM((16, 2, far_count, rows, wide), LOW),
            pltpu.VMEM((16, far_count, rows, wide), LOW),
            pltpu.VMEM((16, far_count - 1, rows, wide), LOW),
            pltpu.VMEM((4,) + vectors.shape, F32),
            pltpu.VMEM((2 + far_count,) + vectors.shape, F32),
            pltpu.VMEM((16, rows, wide), F32),
        ]
        + [like(array) for array in arrays[:16]]
        + [
            like(proj),
            pltpu.VMEM((wide, width), LOW),
            pltpu.VMEM((wide, width), LOW),
            pltpu.VMEM((8, far_count, 2, 2, rows, wide), LOW),
            like(qu),
            like(qu),
            like(ku),
            like(ku),
            like(kp),
            like(kp),
            pltpu.VMEM(packed.shape, LOW),
            pltpu.VMEM(packed.shape, F32),
            pltpu.VMEM(packed.shape, F32),
            pltpu.VMEM((tokens, width), F32),
            pltpu.VMEM((tokens // 2, width), F32),
            pltpu.VMEM(packed.shape, F32),
            pltpu.VMEM((packed.shape[0] // 2, width), F32),
            pltpu.SemaphoreType.DMA((16, 6)),
            pltpu.SemaphoreType.DMA((16, 6)),
            pltpu.SemaphoreType.DMA((16, 2)),
            pltpu.SemaphoreType.DMA((16,)),
            pltpu.SemaphoreType.DMA((16,)),
            pltpu.SemaphoreType.DMA((16,)),
            pltpu.SemaphoreType.DMA((20,)),
            pltpu.SemaphoreType.DMA((3,)),
            pltpu.SemaphoreType.DMA((3,)),
            pltpu.SemaphoreType.DMA((2 + far_count,)),
            pltpu.SemaphoreType.DMA((2 + far_count,)),
        ],
        compiler_params=pltpu.CompilerParams(
            collective_id=1, has_side_effects=True, vmem_limit_bytes=60 << 20
        ),
        name="backward_and_sums",
    )(expand, shrink, vectors, *arrays)


def norm_apply(values, gain, shift):
    centre = values - jnp.mean(values, axis=-1, keepdims=True)
    spread = jnp.mean(centre * centre, axis=-1, keepdims=True)
    return centre * lax.rsqrt(spread + epsilon) * gain + shift


def gelu_exact(values):
    return jax.nn.gelu(values, approximate=False)


def heads_of(values):
    return values.reshape(values.shape[0], values.shape[1] // HEAD, HEAD)


def scores_of(queries, keys, valid):
    scores = jnp.einsum(
        "rhd,chd->hrc", heads_of(queries), heads_of(keys), preferred_element_type=F32
    ) * HEAD ** (-0.5)
    if valid is not None:
        scores = jnp.where(valid[None, None, :], scores, -1e30)
    return scores


def attend_forward(queries, keys, values, valid):
    scores = scores_of(queries, keys, valid)
    top = jnp.max(scores, axis=-1, keepdims=True)
    expon = jnp.exp(scores - top)
    total = jnp.sum(expon, axis=-1, keepdims=True)
    probs = to_low(expon / total)
    mixed = jnp.einsum("hrc,chd->rhd", probs, heads_of(values), preferred_element_type=F32)
    return to_low(mixed.reshape(queries.shape)), top + jnp.log(total), probs


def attend_backward(queries, keys, values, valid, log_total, delta_mixed):
    probs = jnp.exp(scores_of(queries, keys, valid) - log_total)
    delta_heads = heads_of(delta_mixed)
    delta_values = jnp.einsum("hrc,rhd->chd", to_low(probs), delta_heads, preferred_element_type=F32)
    delta_probs = jnp.einsum("rhd,chd->hrc", delta_heads, heads_of(values), preferred_element_type=F32)
    row_delta = jnp.sum(delta_probs * probs, axis=-1, keepdims=True)
    score_low = to_low(probs * (delta_probs - row_delta))
    scale = HEAD ** (-0.5)
    delta_query = jnp.einsum("hrc,chd->rhd", score_low, heads_of(keys), preferred_element_type=F32) * scale
    delta_keys = jnp.einsum("hrc,rhd->chd", score_low, heads_of(queries), preferred_element_type=F32) * scale
    return (
        to_low(delta_query.reshape(queries.shape)),
        to_low(delta_keys.reshape(keys.shape)),
        to_low(delta_values.reshape(keys.shape)),
    )


def body(
    custom,
    tokens,
    memory,
    lengths,
    tokens_cotangent,
    memory_cotangent,
    projections,
    output_maps,
    expand_weight,
    shrink_weight,
    projection_bias,
    norm_gain,
    norm_bias,
    expand_bias,
    shrink_bias,
):
    share = lax.axis_index("mem")
    chips = lax.axis_size("seq")
    width = tokens.shape[1]
    hidden = expand_weight.shape[1]
    part = projections.shape[1]
    rows = 2 * part

    def block(values, axis):
        low = to_low(values)
        wide = axis + 1
        return join(half(low, share, wide), swap(half(low, 1 - share, wide)), axis)

    vectors = [to_low(v).astype(F32) for v in (projection_bias, norm_gain, norm_bias, shrink_bias[None], expand_bias)]
    blocks = (
        block(projections, 1),
        block(output_maps, 1),
        block(expand_weight, 0),
        block(shrink_weight, 0),
    )
    own_count = tokens.shape[0]
    length = lengths[0]
    own_valid = share * own_count + jnp.arange(own_count) < length
    all_valid = jnp.arange(2 * own_count) < length
    device = 2 * lax.axis_index("seq") + share
    if custom:
        table = lax.dynamic_update_slice(jnp.zeros((13, width), F32), jnp.concatenate(vectors[:4]), (0, device * part))
        line = lax.dynamic_update_slice(jnp.zeros((hidden,), F32), vectors[4], (device * vectors[4].shape[0],))
        table = jnp.concatenate([table, line.reshape(-1, width)])
        table = jnp.pad(table, ((0, -table.shape[0] % 8), (0, 0)))
        (
            proj_all, maps_all, expand_mat, shrink_mat, table, hidden_full, middle_full, d_branch_x, inputs, rows_all, pack_query, pack_keys,
            pack_values, unpack_query, unpack_keys, unpack_values, pack_probs, unpack_probs, pack_mixed, unpack_mixed, packed_low, new_memory,
            middle_sum, slope, delta_sum2, delta_branch, new_tokens, delta_sum0, vectors,
        ) = gather_chips(
            chips // 4, blocks, table, tokens, memory, all_valid.astype(F32)[None], own_valid.astype(F32)[:, None], tokens_cotangent, memory_cotangent
        )
        proj_all = proj_all.reshape(6, width, width // 2)
        maps_all = maps_all.reshape(2, width, width)
        expand_mat = expand_mat.reshape(width, hidden)
        shrink_mat = shrink_mat.reshape(hidden, width)
        gains, shifts = table[6:9], table[9:12]
        delta_hidden_in = to_low(matmul_right(delta_branch, shrink_mat) * slope.astype(F32))
        delta_shrink = matmul_left(hidden_full, d_branch_x)
        delta_expand = matmul_left(
            middle_full, join(half(delta_hidden_in, share, 1), swap(half(delta_hidden_in, 1 - share, 1)))
        )
        delta_middle = delta_sum2 + matmul_right(delta_hidden_in, expand_mat)
        dropped, norm_back = jax.vjp(norm_apply, middle_sum, gains[1], shifts[1])
        delta_sum1, delta_gain1, delta_shift1 = norm_back(delta_middle)
        delta_own = to_low(delta_sum1)
        delta_unpacked = both(delta_own)
        grid = (chips // 4, 2, 2)
        zero = jnp.zeros((width,), F32)
        more = jnp.stack([zero] * 5 + [column_sum(delta_own), zero, delta_gain1, zero, zero, delta_shift1, zero, zero])
        more = jnp.concatenate([more, column_sum(delta_hidden_in).reshape(-1, width)])
        vectors = vectors + jnp.pad(more, ((0, -more.shape[0] % 8), (0, 0)))
        proj_o, maps_o, expand_o, shrink_o, vec_o, tokens_grad, memory_grad = reduce_chips(
            chips // 4,
            to_low(delta_expand).reshape(grid + (rows, hidden // 2)),
            to_low(delta_shrink).reshape(grid + (hidden // chips, width // 2)),
            vectors,
            (
                delta_unpacked, unpack_mixed, pack_mixed, inputs, rows_all, unpack_query, unpack_keys, unpack_values,
                pack_query, pack_keys, pack_values, unpack_probs, pack_probs, packed_low, delta_sum0, delta_sum1, proj_all, maps_all,
            ),
        )
        small = lax.dynamic_slice(vec_o, (0, device * part), (13, part))
        count = hidden // (2 * chips)
        expand_small = lax.dynamic_slice(vec_o[13 : 13 + hidden // width].reshape(-1), (device * count,), (count,))
    else:
        gather = lambda values, axis: lax.all_gather(values, "seq", axis=axis, tiled=True)
        proj_all = gather(blocks[0], 1)
        maps_all = both(gather(blocks[1], 1), 2)
        expand_mat = both(gather(blocks[2], 0), 1)
        shrink_mat = both(gather(blocks[3], 0), 1)
        table = lax.all_gather(jnp.concatenate(vectors[:4]), AXES, axis=1, tiled=True)
        line = lax.all_gather(vectors[4], AXES, axis=0, tiled=True)
        table = jnp.concatenate([table, line.reshape(-1, width)])
        biases, gains, shifts, shrink_shift = table[0:6], table[6:9], table[9:12], table[12]
        expand_shift = table[13 : 13 + hidden // width].reshape(hidden)
        bias_half = half(biases, share, 1)
        inputs, rows_all, memory_cot = both(tokens), both(memory), both(memory_cotangent)
        pack_query = to_low(matmul(rows_all, proj_all[0]) + bias_half[0])
        pack_keys = to_low(matmul(inputs, proj_all[1]))
        pack_values = to_low(matmul(inputs, proj_all[2]) + bias_half[1])
        pack_own, pack_total, pack_probs = attend_forward(pack_query, pack_keys, pack_values, all_valid)
        pack_mixed = both(pack_own, 1)
        packed = matmul(pack_mixed, maps_all[0]) + biases[2]
        packed_low = to_low(packed)
        memory_sum = rows_all.astype(F32) + packed
        new_memory = norm_apply(half(memory_sum, share, 0), gains[0], shifts[0])
        unpack_keys = to_low(matmul(packed_low, proj_all[4]))
        unpack_values = to_low(matmul(packed_low, proj_all[5]) + bias_half[4])
        unpack_query = to_low(matmul(inputs, proj_all[3]) + bias_half[3])
        unpack_own, unpack_total, unpack_probs = attend_forward(unpack_query, unpack_keys, unpack_values, None)
        unpack_mixed = both(unpack_own, 1)
        middle_sum = tokens.astype(F32) + matmul(half(unpack_mixed, share, 0), maps_all[1]) + biases[5]
        middle = norm_apply(middle_sum, gains[1], shifts[1])
        middle_low = to_low(middle)
        hidden_in = matmul(middle_low, expand_mat) + expand_shift
        hidden_low = to_low(gelu_exact(hidden_in))
        output_sum = middle + matmul(hidden_low, shrink_mat) + shrink_shift
        layer_out = norm_apply(output_sum, gains[2], shifts[2])
        new_tokens = jnp.where(own_valid[:, None], layer_out, 0.0)

        delta_out = jnp.where(own_valid[:, None], tokens_cotangent.astype(F32), 0.0)
        dropped, norm_back = jax.vjp(norm_apply, output_sum, gains[2], shifts[2])
        delta_sum2, delta_gain2, delta_shift2 = norm_back(delta_out)
        delta_branch = to_low(delta_sum2)
        delta_hidden = matmul_right(delta_branch, shrink_mat)
        dropped, gelu_back = jax.vjp(gelu_exact, hidden_in)
        delta_hidden_in = to_low(gelu_back(delta_hidden)[0])
        delta_shrink = matmul_left(
            both(hidden_low), join(half(delta_branch, share, 1), swap(half(delta_branch, 1 - share, 1)))
        )
        delta_expand = matmul_left(
            both(middle_low), join(half(delta_hidden_in, share, 1), swap(half(delta_hidden_in, 1 - share, 1)))
        )
        delta_middle = delta_sum2 + matmul_right(delta_hidden_in, expand_mat)
        dropped, norm_back = jax.vjp(norm_apply, middle_sum, gains[1], shifts[1])
        delta_sum1, delta_gain1, delta_shift1 = norm_back(delta_middle)
        delta_own = to_low(delta_sum1)
        delta_unpacked = both(delta_own)
        dropped, norm_back = jax.vjp(norm_apply, memory_sum, gains[0], shifts[0])
        delta_sum0 = norm_back(memory_cot.astype(F32))[0]
        dropped, norm_back = jax.vjp(norm_apply, half(memory_sum, share, 0), gains[0], shifts[0])
        dropped, delta_gain0, delta_shift0 = norm_back(memory_cotangent.astype(F32))
        known = [delta_gain0, delta_gain1, delta_gain2, delta_shift0, delta_shift1, delta_shift2, column_sum(delta_branch)]
        delta_map1 = matmul_left(unpack_mixed, half(delta_unpacked, share, 1))
        delta_mixed = to_low(matmul_right(delta_unpacked, half(maps_all[1], share, 0)))
        delta_uquery, delta_ukeys, delta_uvalues = attend_backward(
            unpack_query, unpack_keys, unpack_values, None, unpack_total, delta_mixed
        )
        delta_proj3 = matmul_left(inputs, delta_uquery)
        delta_proj4 = matmul_left(packed_low, delta_ukeys)
        delta_proj5 = matmul_left(packed_low, delta_uvalues)
        partial = matmul_right(delta_ukeys, proj_all[4]) + matmul_right(delta_uvalues, proj_all[5])
        delta_packed = to_low(delta_sum0 + (partial + swap(partial)))
        delta_map0 = matmul_left(pack_mixed, half(delta_packed, share, 1))
        delta_mixed = to_low(matmul_right(delta_packed, half(maps_all[0], share, 0)))
        delta_pquery, delta_pkeys, delta_pvalues = attend_backward(
            pack_query, pack_keys, pack_values, all_valid, pack_total, delta_mixed
        )
        delta_proj0 = matmul_left(rows_all, delta_pquery)
        delta_proj1 = matmul_left(inputs, delta_pkeys)
        delta_proj2 = matmul_left(inputs, delta_pvalues)
        partial = matmul_right(delta_pquery, proj_all[0])
        memory_grad = half(delta_sum0, share, 0) + half(partial, share, 0) + swap(half(partial, 1 - share, 0))
        partial = (
            matmul_right(delta_uquery, proj_all[3])
            + matmul_right(delta_pkeys, proj_all[1])
            + matmul_right(delta_pvalues, proj_all[2])
        )
        tokens_grad = delta_sum1 + half(partial, share, 0) + swap(half(partial, 1 - share, 0))

        zero = jnp.zeros((1, width // 2), F32)

        def spread(values):
            return join(values, zero[0])

        bias_grads = [
            spread(column_sum(delta_pquery)),
            spread(column_sum(delta_pvalues)),
            column_sum(half(delta_packed, share, 0)),
            spread(column_sum(delta_uquery)),
            spread(column_sum(delta_uvalues)),
            column_sum(delta_own),
        ]
        vec_grads = jnp.stack(
            bias_grads + known
        )
        vec_grads = vec_grads.reshape(13, 2 * chips, part).transpose(1, 0, 2).reshape(2 * chips, 13 * part)
        vec_grads = jnp.concatenate([vec_grads, column_sum(delta_hidden_in).reshape(2 * chips, -1)], axis=1)
        vec_grads = jnp.pad(vec_grads, ((0, 0), (0, 1024 - vec_grads.shape[1])))
        reduce = lambda values, axis: lax.psum_scatter(values, "seq", scatter_dimension=axis, tiled=True)

        def finish(values, axis):
            return join(half(values, share, axis), swap(half(values, 1 - share, axis)), axis + 1)

        proj_o = finish(reduce(jnp.stack([delta_proj0, delta_proj1, delta_proj2, delta_proj3, delta_proj4, delta_proj5]), 1), 1)
        maps_o = finish(reduce(jnp.stack([delta_map0, delta_map1]), 1), 1)
        expand_o = finish(reduce(delta_expand, 0), 0)
        shrink_o = finish(reduce(delta_shrink, 0), 0)
        vec_o = lax.psum_scatter(vec_grads, AXES, scatter_dimension=0, tiled=True).reshape(-1)
        small = vec_o[: 13 * part].reshape(13, part)
        expand_small = vec_o[13 * part : 13 * part + hidden // (2 * chips)]
    return (
        new_tokens,
        new_memory,
        tokens_grad,
        memory_grad,
        proj_o,
        maps_o,
        expand_o,
        shrink_o,
        small[0:6],
        small[6:9],
        small[9:12],
        expand_small,
        small[12],
    )


def solution(mesh):
    rows, stacked = P(AXES, None), P(None, AXES, None)
    table, line = P(None, AXES), P(AXES)
    custom = mesh.shape["seq"] == 16 and mesh.shape["mem"] == 2
    return jax.shard_map(
        functools.partial(body, custom),
        mesh=mesh,
        in_specs=(rows, rows, P("seq"), rows, rows, stacked, stacked, rows, rows, table, table, table, line, line),
        out_specs=(rows, rows, rows, rows, stacked, stacked, rows, rows, table, table, table, line, line),
        check_vma=False,
    )
```

```python
import functools

import jax
import jax.numpy as jnp
from jax import lax
from jax.experimental import pallas as pl
from jax.experimental.pallas import tpu as pltpu
from jax.sharding import PartitionSpec as P

HEAD = 64
epsilon = 1e-05
MESH = pl.DeviceIdType.MESH
LOW = jnp.bfloat16
F32 = jnp.float32
AXES = ("seq", "mem")


def matmul(left, right):
    return jnp.dot(left, right, preferred_element_type=F32)


def matmul_left(left, right):
    return lax.dot_general(left, right, (((0,), (0,)), ((), ())), preferred_element_type=F32)


def matmul_right(left, right):
    return lax.dot_general(left, right, (((1,), (1,)), ((), ())), preferred_element_type=F32)


def to_low(values):
    return values.astype(LOW)


def column_sum(values):
    return jnp.sum(values.astype(F32), axis=0)


def swap(values):
    return lax.ppermute(values, "mem", [(0, 1), (1, 0)])


def join(own, other, axis=0):
    first = lax.axis_index("mem") == 0
    return jnp.where(
        first, jnp.concatenate([own, other], axis), jnp.concatenate([other, own], axis)
    )


def both(values, axis=0):
    return join(values, swap(values), axis)


def half(values, index, axis):
    size = values.shape[axis] // 2
    return lax.dynamic_slice_in_dim(values, index * size, size, axis)


def place(seq):
    return lax.div(seq, 4), lax.rem(lax.div(seq, 2), 2), lax.rem(seq, 2)


def peers(seq, core, far_count):
    far, row, column = place(seq)
    flat = lambda f, r, c: f * 4 + r * 2 + c
    far_peers = [lax.rem(far + k, far_count) for k in range(1, far_count)]
    return {
        "far": [(flat(f, row, column), core) for f in far_peers],
        "far_index": far_peers,
        "column": (flat(far, row, 1 - column), core),
        "row": (flat(far, 1 - row, column), core),
        "core": (seq, 1 - core),
    }


def greet(targets):
    barrier = pltpu.get_barrier_semaphore()
    for target in targets:
        pl.semaphore_signal(barrier, inc=1, device_id=target, device_id_type=MESH)
    pl.semaphore_wait(barrier, len(targets))


class Gather:
    def __init__(self, where, to, first, own, at, shared, sems):
        self.where, self.to, self.own, self.at, self.shared = where, to, own, at, shared
        self.first, self.second = first, ("row" if first == "column" else "column")
        self.send, self.recv = sems
        self.started = []

    def _column(self, near):
        far, row, column = self.where
        row, column = (
            (1 - row if "row" in near else row),
            (1 - column if "column" in near else column),
        )
        return self.at(slice(None), row, column)

    def _copy(self, source, target, k, device):
        return pltpu.make_async_remote_copy(
            source, target, self.send.at[k], self.recv.at[k], device_id=device, device_id_type=MESH
        )

    def _go(self, *args):
        copy = self._copy(*args)
        copy.start()
        self.started.append(copy)

    def _arrived(self, ref, k):
        self._copy(ref, ref, k, self.to["core"]).wait_recv()

    def start(self):
        far, row, column = self.where
        mine = self.at(far, row, column)
        for k, device in enumerate(self.to["far"]):
            self._go(self.own, mine, k, device)

    def step(self, stage):
        far, row, column = self.where
        near = self._column(())
        if stage == 0:
            count = len(self.to["far"])
            for k in range(count):
                sender = self.to["far_index"][count - 1 - k]
                self._arrived(self.at(sender, row, column), k)
            self._go(near, near, 3, self.to[self.first])
            self._go(near, near, 4, self.to[self.second])
            if self.shared:
                self._go(near, near, 6, self.to["core"])
        if stage == 1:
            got = self._column((self.first,))
            self._arrived(got, 3)
            self._go(got, got, 5, self.to[self.second])
            if self.shared:
                self._go(got, got, 7, self.to["core"])
        if stage == 2:
            for k, names in ((4, (self.second,)), (5, (self.first, self.second))):
                got = self._column(names)
                self._arrived(got, k)
                if self.shared:
                    self._go(got, got, 4 + k, self.to["core"])
        if stage == 3 and self.shared:
            for k, names in enumerate(
                ((), (self.first,), (self.second,), (self.first, self.second))
            ):
                self._arrived(self._other(names), 6 + k)

    def _other(self, names):
        keep, self.at = self.at, self.shared
        ref = self._column(names)
        self.at = keep
        return ref

    def finish(self):
        for copy in self.started:
            copy.wait_send()


class GatherNear(Gather):
    def start(self):
        far, row, column = self.where
        mine = self.at(far, row, column)
        self._go(self.own, mine, 0, self.to[self.first])
        self._go(self.own, mine, 1, self.to[self.second])

    def _near(self, names):
        far, row, column = self.where
        return self.at(
            far, 1 - row if "row" in names else row, 1 - column if "column" in names else column
        )

    def step(self, stage):
        far = self.where[0]
        all_of = slice(None)
        count = len(self.to["far"])
        if stage == 0:
            got = self._near((self.first,))
            self._arrived(got, 0)
            self._go(got, got, 2, self.to[self.second])
        if stage == 1:
            self._arrived(self._near((self.second,)), 1)
            self._arrived(self._near((self.first, self.second)), 2)
            plane = self.at(far, all_of, all_of)
            for k, device in enumerate(self.to["far"]):
                self._go(plane, plane, 3 + k, device)
            if self.shared:
                self._go(plane, plane, 3 + count, self.to["core"])
        if stage == 2:
            for k in range(count):
                plane = self.at(self.to["far_index"][count - 1 - k], all_of, all_of)
                self._arrived(plane, 3 + k)
                if self.shared:
                    self._go(plane, plane, 4 + count + k, self.to["core"])
        if stage == 3 and self.shared:
            self._arrived(self.shared(far, all_of, all_of), 3 + count)
            for k in range(count):
                plane = self.shared(self.to["far_index"][count - 1 - k], all_of, all_of)
                self._arrived(plane, 4 + count + k)


def transposed(left, right):
    return lax.dot_general(left, right, (((0,), (0,)), ((), ())), preferred_element_type=F32)


def against(left, right):
    return lax.dot_general(left, right, (((1,), (1,)), ((), ())), preferred_element_type=F32)


def plain(left, right):
    return lax.dot_general(left, right, (((1,), (0,)), ((), ())), preferred_element_type=F32)


def over_rows(count, tile, work):
    def one(t, carry):
        work(pl.ds(pl.multiple_of(t * tile, tile), tile))
        return carry

    lax.fori_loop(0, count // tile, one, 0)


class Vectors:
    def __init__(self, to, held, arrived, send, recv, order):
        self.to, self.held, self.arrived, self.sems, self.order = to, held, arrived, (send, recv), order
        self.flying, self.slot = [], 0

    def _go(self, k):
        name = self.order[k]
        for device in self.to["far"] if name == "far" else [self.to[name]]:
            slot = self.slot
            copy = pltpu.make_async_remote_copy(
                self.held.at[k], self.arrived.at[slot], self.sems[0].at[slot], self.sems[1].at[slot],
                device_id=device, device_id_type=MESH,
            )
            copy.start()
            self.flying.append((slot, copy))
            self.slot += 1

    def _take(self, k):
        value = self.held[k]
        for slot, copy in self.flying:
            copy.wait()
            value = value + self.arrived[slot]
        self.flying = []
        return value

    def start(self):
        self._go(0)

    def step(self, k):
        self.held[k] = self._take(k - 1)
        self._go(k)

    def result(self):
        return self._take(3)


def attention_forward(pairs, queries, keys, values, valid, probs, mixed, first_lane, turned):
    for pair in range(*pairs):
        lanes = slice(pair * 128, pair * 128 + 128)
        query, key, value = queries[:, lanes] * LOW(HEAD ** (-0.5)), keys[:, lanes], values[:, lanes]
        outs = []
        for j in range(2):
            part = slice(j * HEAD, (j + 1) * HEAD)
            scores = against(key[:, part], query[:, part]) if turned else against(query[:, part], key[:, part])
            if valid is not None:
                scores = jnp.where(lax.broadcasted_iota(jnp.int32, scores.shape, 1) < valid[0, 0], scores, -1e30)
            axis = 0 if turned else 1
            expon = jnp.exp(scores - jnp.max(scores, axis=axis, keepdims=True))
            prob = (expon * (1.0 / jnp.sum(expon, axis=axis, keepdims=True))).astype(LOW)
            probs[pair * 2 + j] = prob
            outs.append((transposed if turned else plain)(prob, value[:, part]))
        mixed[:, pl.ds(pl.multiple_of(first_lane + pair * 128, 128), 128)] = jnp.concatenate(outs, axis=1).astype(LOW)


def norm_parts(values):
    centre = values - jnp.mean(values, axis=-1, keepdims=True)
    factor = lax.rsqrt(jnp.mean(centre * centre, axis=-1, keepdims=True) + epsilon)
    return centre * factor, factor


def norm_backward(unit, factor, gain, delta):
    scaled = delta * gain
    return factor * (scaled - jnp.mean(scaled, axis=-1, keepdims=True) - unit * jnp.mean(scaled * unit, axis=-1, keepdims=True))


def total_rows(values):
    return jnp.sum(values, axis=0, keepdims=True)


def gather_kernel(far_count, proj_in, maps_in, expand_in, shrink_in, bias_in, gain_in, shift_in, shrink_bias_in, expand_bias_in, length,
                  tokens, rows_in, token_cot, memory_cot,
                  proj_o, maps_o, expand_o, shrink_o, table_o, hidden_o, middle_full_o, d_branch_x_o,
                  inputs_o, memory_o, qp_o, kp_o, vp_o, qu_o, ku_o, vu_o,
                  probs_p_o, probs_u_o, mixed_p_o, mixed_u_o, packed_o, new_memory_o, middle_sum_o,
                  slope_o, d_sum2_o, d_branch_o, new_tokens_o, d_sum0_o, grad_table_o,
                  inputs, memory, qp, kp, vp, qu, ku, vu, probs_p, probs_u, mixed_p, mixed_u, packed, new_memory, middle_sum,
                  slope, d_sum2, d_branch, new_tokens, d_sum0, grad_table,
                  memory_sum, middle, middle_low, hidden, cot, expand_w, shrink_w,
                  weights, map_p, map_u, table, own_vec, vec, vec_all,
                  proj_f, maps_f, expand_f, shrink_f, proj, maps, expand, shrink,
                  send, recv, local, out_sems, cross_send, cross_recv, raw_local, raw_send, raw_recv):
    seq, core = lax.axis_index("seq"), lax.axis_index("mem")
    where = place(seq)
    far, row, column = where
    to = peers(seq, core, far_count)
    wide = maps.shape[-1]
    width = 2 * wide
    own_tokens, own_rows = tokens.shape[0], rows_in.shape[0]

    def cols(which, start=0):
        return pl.ds(pl.multiple_of(which * expand.shape[-1] + start, 128), wide)

    def span(which):
        return pl.ds(pl.multiple_of(which * wide, 128), wide)

    copies, stores = [], []

    def keep(source, target):
        copy = pltpu.make_async_copy(source, target, local.at[len(copies)])
        copy.start()
        copies.append(copy)
        return copy

    def store(source, target):
        copy = pltpu.make_async_copy(source, target, out_sems.at[len(stores)])
        copy.start()
        stores.append(copy)

    own_t = pl.ds(pl.multiple_of(core * own_tokens, 128), own_tokens)
    own_m = pl.ds(pl.multiple_of(core * own_rows, 128), own_rows)
    raw = []
    for n, (source, target) in enumerate(((proj_in, proj_f), (maps_in, maps_f), (expand_in, expand_f), (shrink_in, shrink_f))):
        count, size = source.shape[-2], source.shape[-1] // 2
        place_rows = pl.ds(pl.multiple_of(core * count, 8), count)
        mine, theirs = (pl.ds(pl.multiple_of(which * size, 128), size) for which in (core, 1 - core))
        lead = (slice(None),) * (len(source.shape) - 2)
        raw.append((n, source.at[lead + (slice(None), mine)], source.at[lead + (slice(None), theirs)], target.at[lead + (place_rows,)]))
    for n, own, other, target in raw:
        pltpu.make_async_copy(own, target, raw_local.at[n]).start()
    device = 2 * seq + core
    own_vec[...] = jnp.zeros_like(own_vec)
    for first_row, source in ((0, bias_in), (6, gain_in), (9, shift_in), (12, shrink_bias_in), (16, expand_bias_in)):
        own_vec[first_row : first_row + source.shape[0], 0 : source.shape[1]] = source[...]
    small, large = bias_in.shape[1], expand_bias_in.shape[1]

    def window(start):
        return lax.min(lax.div(start, 128), 2 * wide // 128 - 2)

    offsets = (small * device, lax.rem(large * device, 2 * wide))
    moved = [pltpu.roll(own_vec[k : k + 16 - k // 2], offsets[n] - 128 * window(offsets[n]), 1) for n, k in enumerate((0, 16))]
    vec[...] = jnp.concatenate([moved[0], moved[1], jnp.zeros_like(moved[1])], axis=0).astype(LOW)

    units = []

    def add(first, own, at, shared, kind=Gather):
        k = len(units)
        units.append(kind(where, to, first, own, at, shared, (send.at[k], recv.at[k])))

    def add_proj(first, p):
        add(first, proj.at[p], lambda f, r, c: proj_o.at[p, f, r, c], None)

    def add_map(first, p):
        add(first, maps.at[p], lambda f, r, c: maps_o.at[p, f, r, c, :, span(core)],
            lambda f, r, c: maps_o.at[p, f, r, c, :, span(1 - core)])

    def add_expand(first, k):
        add(first, expand.at[:, pl.ds(k * wide, wide)], lambda f, r, c: expand_o.at[f, r, c, :, cols(core, k * wide)],
            lambda f, r, c: expand_o.at[f, r, c, :, cols(1 - core, k * wide)])

    def add_shrink(first, k):
        rows = shrink.shape[0] // 4
        part = pl.ds(k * rows, rows)
        add(first, shrink.at[part], lambda f, r, c: shrink_o.at[f, r, c, part, span(core)],
            lambda f, r, c: shrink_o.at[f, r, c, part, span(1 - core)], GatherNear if k >= 2 else Gather)

    add("column", vec, lambda f, r, c: vec_all.at[core, f, r, c], lambda f, r, c: vec_all.at[1 - core, f, r, c])
    for first, second in (
        ((add_proj, 0), (add_proj, 1)), ((add_proj, 2), (add_map, 0)), ((add_proj, 4), (add_proj, 5)), ((add_proj, 3), (add_map, 1)),
        ((add_expand, 0), (add_expand, 1)), ((add_expand, 2), (add_expand, 3)), ((add_shrink, 0), (add_shrink, 1)), ((add_shrink, 2), (add_shrink, 3)),
    ):
        first[0]("column", first[1])
        second[0]("row", second[1])

    def cross(k, source, target):
        copy = pltpu.make_async_remote_copy(source, target, cross_send.at[k], cross_recv.at[k], device_id=to["core"], device_id_type=MESH)
        copy.start()
        return copy

    greet(to["far"] + [to["column"], to["row"], to["core"]])
    for n, own, other, target in raw:
        pltpu.make_async_remote_copy(other, target, raw_send.at[n], raw_recv.at[n], device_id=to["core"], device_id_type=MESH).start()
    crossed = [cross(0, tokens, inputs.at[own_t]), cross(1, rows_in, memory.at[own_m]), cross(4, memory_cot, cot.at[own_m])]
    keep(vec, vec_all.at[core, far, row, column])
    units[0].start()
    targets = (
        (proj_f, proj, proj_o.at[:, far, row, column]),
        (maps_f, maps, maps_o.at[:, far, row, column, :, span(core)]),
        (expand_f, expand, expand_o.at[far, row, column, :, pl.ds(pl.multiple_of(core * expand.shape[-1], 128), expand.shape[-1])]),
        (shrink_f, shrink, shrink_o.at[far, row, column, :, span(core)]),
    )
    groups = ((1, 2, 3), (4, 5, 6, 7, 8), (9, 10, 11, 12), (13, 14, 15, 16))
    for (n, own, other, target), (wide_block, block, place_of), group in zip(raw, targets, groups):
        pltpu.make_async_copy(own, target, raw_local.at[n]).wait()
        pltpu.make_async_remote_copy(other, target, raw_send.at[n], raw_recv.at[n], device_id=to["core"], device_id_type=MESH).wait()
        block[...] = wide_block[...].astype(LOW)
        keep(block, place_of)
        for index in group:
            units[index].start()
    keep(tokens, inputs.at[own_t])
    keep(rows_in, memory.at[own_m])
    keep(memory_cot, cot.at[own_m])
    for copy in copies:
        copy.wait()
    lanes = [units[1:3]] + [units[k:k + 2] for k in range(3, len(units), 2)]
    lanes[0] = [units[0]] + lanes[0]
    late = lanes.pop()
    plan = [(t + stage, -stage, lane, stage) for t, lane in enumerate(lanes) for stage in range(4)]
    plan += [(time, -9, late, stage) for stage, time in enumerate((0.5, 2.5, len(lanes) + 0.5, len(lanes) + 2.5))]
    plan = sorted(plan, key=lambda step: step[:2])
    taken = [0]

    def advance(until):
        while taken[0] < len(plan) and plan[taken[0]][0] <= until:
            time, rank, lane, stage = plan[taken[0]]
            taken[0] += 1
            for unit in lane:
                unit.step(stage)

    fetched = {}

    def fetch_proj(p):
        size = proj_o.shape[-2]
        copy = pltpu.make_async_copy(proj_o.at[p], weights.at[p], local.at[8 + p])
        copy.start()
        fetched[p] = copy

    def fetch_map(p, target):
        copy = pltpu.make_async_copy(maps_o.at[p], target, local.at[14 + p])
        copy.start()
        fetched[6 + p] = copy

    def weight(p):
        return weights[p].reshape(-1, wide)

    def project(p, source, target, bias):
        fetched[p].wait()

        def one(piece):
            value = plain(source[piece], weight(p))
            if bias is not None:
                value = value + table[bias : bias + 1, span(core)]
            target[piece] = value.astype(LOW)

        over_rows(source.shape[0], 256, one)

    def gain(k):
        return table[6 + k : 7 + k]

    def shift(k):
        return table[9 + k : 10 + k]

    advance(2)
    for copy in crossed:
        copy.wait()
    store(inputs, inputs_o)
    store(memory, memory_o)
    fetch_proj(0)
    fetch_proj(1)
    project(1, inputs, kp, None)
    advance(3)
    fetch_proj(2)
    table[...] = jnp.zeros_like(table)
    for k in range(8 * far_count):
        block = vec_all[k % 2, k // 8, (k // 4) % 2, (k // 2) % 2].astype(F32)
        for rows, start, at in ((slice(0, 16), small * k, slice(0, 16)), (16, (large * k) % width, 13 + large * k // width)):
            first = 128 * min(start // 128, width // 128 - 2)
            if at == slice(0, 16):
                table[0:13, first : first + 256] += block[0:13]
            else:
                table[at : at + 1, first : first + 256] += block[16:17]
    store(table, table_o)
    project(0, memory, qp, 0)
    project(2, inputs, vp, 1)
    attention_forward((0, 1), qp, kp, vp, length, probs_p, mixed_p, core * wide, False)
    advance(3.5)
    attention_forward((1, 3), qp, kp, vp, length, probs_p, mixed_p, core * wide, False)
    packing = cross(2, mixed_p.at[:, span(core)], mixed_p.at[:, span(core)])
    advance(4)
    fetch_map(0, map_p)
    fetch_proj(4)
    fetch_proj(5)
    packing.wait_send()
    pltpu.make_async_remote_copy(mixed_p.at[:, span(1 - core)], mixed_p.at[:, span(1 - core)], cross_send.at[2], cross_recv.at[2],
                                 device_id=to["core"], device_id_type=MESH).wait_recv()
    fetched[6].wait()
    for source, target in ((qp, qp_o), (kp, kp_o), (vp, vp_o), (probs_p, probs_p_o), (mixed_p, mixed_p_o)):
        store(source, target)
    value = plain(mixed_p[...], map_p[...].reshape(-1, 2 * wide)) + table[2:3]
    packed[...] = value.astype(LOW)
    memory_sum[...] = memory[...].astype(F32) + value
    project(4, packed, ku, None)
    project(5, packed, vu, 4)
    unit, factor = norm_parts(memory_sum[...])
    memory_sum[...] = unit
    d_sum0[...] = norm_backward(unit, factor, gain(0), cot[...].astype(F32))
    unit, delta = memory_sum[own_m], memory_cot[...].astype(F32)
    new_memory[...] = unit * gain(0) + shift(0)
    grad_table[...] = jnp.zeros_like(grad_table)
    grad_table[6:7] = total_rows(delta * unit)
    grad_table[9:10] = total_rows(delta)
    advance(5)
    fetch_proj(3)
    for source, target in ((packed, packed_o), (d_sum0, d_sum0_o), (new_memory, new_memory_o), (ku, ku_o), (vu, vu_o)):
        store(source, target)
    project(3, inputs, qu, 3)
    attention_forward((0, 1), qu, ku, vu, None, probs_u, mixed_u, core * wide, True)
    advance(6)
    fetch_map(1, map_u)
    attention_forward((1, 3), qu, ku, vu, None, probs_u, mixed_u, core * wide, True)
    unpacking = cross(3, mixed_u.at[:, span(core)], mixed_u.at[:, span(core)])
    advance(7)
    unpacking.wait_send()
    pltpu.make_async_remote_copy(mixed_u.at[:, span(1 - core)], mixed_u.at[:, span(1 - core)], cross_send.at[3], cross_recv.at[3],
                                 device_id=to["core"], device_id_type=MESH).wait_recv()
    for source, target in ((qu, qu_o), (probs_u, probs_u_o), (mixed_u, mixed_u_o)):
        store(source, target)
    fetched[7].wait()

    def attended(t, carry):
        here = pl.ds(pl.multiple_of(t * 256, 256), 256)
        there = pl.ds(pl.multiple_of(core * own_tokens + t * 256, 256), 256)
        value = plain(mixed_u[there], map_u[...].reshape(-1, 2 * wide)) + table[5:6]
        value = tokens[here].astype(F32) + value
        middle_sum[here] = value
        value = norm_parts(value)[0] * gain(1) + shift(1)
        middle[here] = value
        middle_low[here] = value.astype(LOW)
        return carry

    lax.fori_loop(0, own_tokens // 256, attended, 0)
    store(middle_sum, middle_sum_o)
    store(middle_low, middle_full_o.at[own_t])
    sent = [cross(5, middle_low, middle_full_o.at[own_t])]
    tall = 2 * wide
    first_bias = 13

    def widen(n):
        columns = pl.ds(n * tall, tall)
        fetched[8 + n].wait()
        value = plain(middle_low[...], expand_w[:, :, :, :, columns].reshape(-1, tall)) + table[first_bias + n : first_bias + n + 1]
        share = 0.5 + 0.5 * lax.erf(value * 0.5**0.5)
        hidden[:, columns] = (value * share).astype(LOW)
        slope[:, columns] = (share + value * (0.3989422804014327 * jnp.exp(-0.5 * value * value))).astype(LOW)
        store(hidden.at[:, columns], hidden_o.at[own_t, columns])
        sent.append(cross(6 + n, hidden.at[:, columns], hidden_o.at[own_t, columns]))

    def fetch_expand(n):
        columns = pl.ds(n * tall, tall)
        copy = pltpu.make_async_copy(expand_o.at[:, :, :, :, columns], expand_w.at[:, :, :, :, columns], local.at[16 + n])
        copy.start()
        fetched[8 + n] = copy

    fetch_expand(0)
    fetch_expand(2)
    widen(0)
    advance(7.5)
    widen(2)
    advance(8)
    fetch_expand(1)
    fetch_expand(3)
    widen(1)
    advance(8.5)
    widen(3)
    store(slope, slope_o)
    advance(99)
    last = pltpu.make_async_copy(shrink_o, shrink_w, local.at[20])
    last.start()
    last.wait()

    def narrow(t, carry):
        here = pl.ds(pl.multiple_of(t * 256, 256), 256)
        value = middle[here] + (plain(hidden[here], shrink_w[...].reshape(-1, 2 * wide)) + table[12:13])
        unit, factor = norm_parts(value)
        live = core * own_tokens + t * 256 + lax.broadcasted_iota(jnp.int32, (256, 1), 0) < length[0, 0]
        new_tokens[here] = jnp.where(live, unit * gain(2) + shift(2), 0.0)
        delta = jnp.where(live, token_cot[here].astype(F32), 0.0)
        grad_table[8:9] += total_rows(delta * unit)
        grad_table[11:12] += total_rows(delta)
        value = norm_backward(unit, factor, gain(2), delta)
        d_sum2[here] = value
        value = value.astype(LOW)
        d_branch[here] = value
        grad_table[12:13] += total_rows(value.astype(F32))
        return carry

    lax.fori_loop(0, own_tokens // 256, narrow, 0)
    sent.append(cross(10, d_branch.at[:, span(1 - core)], d_branch_x_o.at[own_t]))
    store(d_branch.at[:, span(core)], d_branch_x_o.at[own_t])
    for source, target in ((d_sum2, d_sum2_o), (d_branch, d_branch_o), (new_tokens, new_tokens_o), (grad_table, grad_table_o)):
        store(source, target)
    for copy in sent:
        copy.wait()
    for copy in stores:
        copy.wait()
    for unit in units:
        unit.finish()


def gather_chips(far_count, weights, vectors, length, tokens, memory, token_cot, memory_cot):
    grid = (far_count, 2, 2)
    width, hidden = weights[0].shape[-1], weights[2].shape[-1]
    rows, wide = 2 * weights[0].shape[1], width // 2
    blocks = ((6, rows, wide), (2, rows, wide), (rows, hidden // 2), (2 * weights[3].shape[0], wide))
    table = (24, width)
    own_tokens, own_rows = tokens.shape[0], memory.shape[0]
    all_tokens, all_rows = 2 * own_tokens, 2 * own_rows
    count = wide // HEAD
    passed = (
        ((6,) + grid + (rows, wide), LOW),
        ((2,) + grid + (rows, width), LOW),
        (grid + (rows, hidden), LOW),
        (grid + (blocks[3][0], width), LOW),
        (table, F32),
        ((all_tokens, hidden), LOW),
        ((all_tokens, width), LOW),
        ((all_tokens, wide), LOW),
    )
    kept = (
        ((all_tokens, width), LOW),
        ((all_rows, width), LOW),
        ((all_rows, wide), LOW),
        ((all_tokens, wide), LOW),
        ((all_tokens, wide), LOW),
        ((all_tokens, wide), LOW),
        ((all_rows, wide), LOW),
        ((all_rows, wide), LOW),
        ((count, all_rows, all_tokens), LOW),
        ((count, all_rows, all_tokens), LOW),
        ((all_rows, width), LOW),
        ((all_tokens, width), LOW),
        ((all_rows, width), LOW),
        ((own_rows, width), F32),
        ((own_tokens, width), F32),
        ((own_tokens, hidden), LOW),
        ((own_tokens, width), F32),
        ((own_tokens, width), LOW),
        ((own_tokens, width), F32),
        ((all_rows, width), F32),
        (table, F32),
    )
    inner = (
        ((all_rows, width), F32),
        ((own_tokens, width), F32),
        ((own_tokens, width), LOW),
        ((own_tokens, hidden), LOW),
        ((all_rows, width), LOW),
        passed[2],
        passed[3],
        passed[0],
        (passed[1][0][1:], LOW),
        (passed[1][0][1:], LOW),
        (table, F32),
        ((24, 256), F32),
        ((32, 256), LOW),
        ((2,) + grid + (32, 256), LOW),
    ) + tuple((block, F32) for block in blocks) + tuple((block, LOW) for block in blocks)
    any_space = pl.BlockSpec(memory_space=pl.ANY)
    return pl.pallas_call(
        functools.partial(gather_kernel, far_count),
        out_shape=[jax.ShapeDtypeStruct(*entry) for entry in passed + kept],
        in_specs=[any_space] * 4
        + [pl.BlockSpec(memory_space=pltpu.VMEM)] * 5
        + [pl.BlockSpec(memory_space=pltpu.SMEM)]
        + [pl.BlockSpec(memory_space=pltpu.VMEM)] * 4,
        out_specs=[any_space] * (len(passed) + len(kept)),
        scratch_shapes=[pltpu.VMEM(*entry) for entry in kept + inner]
        + [
            pltpu.SemaphoreType.DMA((17, 10)),
            pltpu.SemaphoreType.DMA((17, 10)),
            pltpu.SemaphoreType.DMA((21,)),
            pltpu.SemaphoreType.DMA((32,)),
            pltpu.SemaphoreType.DMA((11,)),
            pltpu.SemaphoreType.DMA((11,)),
            pltpu.SemaphoreType.DMA((4,)),
            pltpu.SemaphoreType.DMA((4,)),
            pltpu.SemaphoreType.DMA((4,)),
        ],
        compiler_params=pltpu.CompilerParams(
            collective_id=0, has_side_effects=True, vmem_limit_bytes=62 << 20
        ),
        name="gather_and_forward",
    )(*weights, *vectors, length, tokens, memory, token_cot, memory_cot)


class Reduce:
    def __init__(self, where, to, first, at, half_in, quarter_in, far_in, sems):
        self.where, self.to, self.at = where, to, at
        self.half_in, self.quarter_in, self.far_in = half_in, quarter_in, far_in
        self.first, self.second = first, ("row" if first == "column" else "column")
        self.send, self.recv = sems

    def _copy(self, source, target, k, device):
        return pltpu.make_async_remote_copy(
            source, target, self.send.at[k], self.recv.at[k], device_id=device, device_id_type=MESH
        )

    def _go(self, *args):
        self._copy(*args).start()

    def _arrived(self, ref, k):
        self._copy(ref, ref, k, self.to["core"]).wait_recv()

    def _column(self, near):
        far, row, column = self.where
        row, column = (
            (1 - row if "row" in near else row),
            (1 - column if "column" in near else column),
        )
        return self.at(slice(None), row, column)

    def start(self):
        for k, names in ((1, (self.first, self.second)), (0, (self.second,))):
            self._go(self._column(names), self.half_in.at[k], k, self.to[self.second])

    def _add(self, target, other):
        for k in range(target.shape[0]):
            target[k] = (target[k].astype(F32) + other[k].astype(F32)).astype(LOW)

    def step(self, stage):
        count = len(self.to["far"])
        own, near = self._column(()), self._column((self.first,))
        if stage == 0:
            self._arrived(self.half_in.at[1], 1)
            self._add(near, self.half_in.at[1])
            self._go(near, self.quarter_in, 2, self.to[self.first])
            self._arrived(self.half_in.at[0], 0)
            self._add(own, self.half_in.at[0])
        if stage == 1:
            self._arrived(self.quarter_in, 2)
            self._add(own, self.quarter_in)
            for k, device in enumerate(self.to["far"]):
                self._go(own.at[self.to["far_index"][k]], self.far_in.at[k], 3 + k, device)
        if stage == 2:
            for k in range(count):
                self._arrived(self.far_in.at[k], 3 + k)

    def result(self):
        value = self._column(())[self.where[0]].astype(F32)
        for k in range(len(self.to["far"])):
            value = value + self.far_in[k].astype(F32)
        return value

    def finish(self):
        refs = [self.half_in.at[0], self.half_in.at[1], self.quarter_in]
        refs += [self.far_in.at[k] for k in range(len(self.to["far"]))]
        for k, ref in enumerate(refs):
            self._copy(ref, ref, k, self.to["core"]).wait_send()


def attention_backward(pairs, queries, keys, values, probs, mixed, d_query, d_key, d_value, turned):
    scale = HEAD ** (-0.5)
    for pair in range(*pairs):
        lanes = slice(pair * 128, pair * 128 + 128)
        query, delta = queries[:, lanes], mixed[:, lanes]
        key, value = keys[:, lanes], values[:, lanes]
        by_query, by_key = (transposed, plain) if turned else (plain, transposed)
        parts = ([], [], [])
        for j in range(2):
            part = slice(j * HEAD, (j + 1) * HEAD)
            prob_low = probs[pair * 2 + j]
            prob = prob_low.astype(F32)
            d_prob = against(value[:, part], delta[:, part]) if turned else against(delta[:, part], value[:, part])
            row_delta = jnp.sum(d_prob * prob, axis=0 if turned else 1, keepdims=True)
            d_score = (prob * (d_prob - row_delta)).astype(LOW)
            parts[0].append(by_query(d_score, key[:, part]))
            parts[1].append(by_key(d_score, query[:, part]))
            parts[2].append(by_key(prob_low, delta[:, part]))
        d_query[:, lanes] = (jnp.concatenate(parts[0], axis=1) * scale).astype(LOW)
        d_key[:, lanes] = (jnp.concatenate(parts[1], axis=1) * scale).astype(LOW)
        d_value[:, lanes] = jnp.concatenate(parts[2], axis=1).astype(LOW)


def reduce_kernel(far_count, table, vectors_in, hidden_h, d_branch_x_h, d_branch_h, slope_h, expand_h, shrink_h, middle_h, d_sum2_h, middle_sum_h,
                  mixed_u_h, mixed_p_h, inputs_h, memory_h, qu_h, ku_h, vu_h, qp_h, kp_h, vp_h, probs_u_h, probs_p_h, packed_h, d_sum0_h, proj_h, maps_h,
                  proj_o, maps_o, expand_o, shrink_o, vec_o, tokens_o, memory_o,
                  half_in, quarter_in, far_in, vec_sum, vec_in, sums,
                  grads, expand_grads, shrink_grads, d_hidden_x, d_unpacked, d_sum1, partial, partial_in, wide_out, wide_in, rows_out, rows_in,
                  send, recv, last_send, last_recv, last_local, in_sems, cross_send, cross_recv, vec_send, vec_recv):
    seq, core = lax.axis_index("seq"), lax.axis_index("mem")
    where = place(seq)
    to = peers(seq, core, far_count)
    wide = proj_h.shape[-1]
    width = 2 * wide
    rows = proj_o.shape[-2] * 2
    part = rows // 2
    own_rows = d_sum1.shape[0]
    mem_rows = packed_h.shape[0] // 2
    units, ends = [], []

    def span(which, start=0, whole=None):
        return pl.ds(pl.multiple_of(which * (whole or wide) + start, 128), wide)

    loads = {}

    def fetch(name, source, target):
        copy = pltpu.make_async_copy(source, target, in_sems.at[len(loads)])
        copy.start()
        loads[name] = copy

    def need(*names):
        for name in names:
            loads[name].wait()

    def below(refs):
        for name, source, target in refs:
            fetch(name, source, target)

    fetch("vectors", vectors_in, vec_sum.at[0])

    def add(at, end):
        k = len(units)
        first = "column" if k % 2 == 0 else "row"
        units.append(Reduce(where, to, first, at, half_in.at[k], quarter_in.at[k], far_in.at[k], (send.at[k], recv.at[k])))
        ends.append(end)

    def add_expand(k):
        add(lambda f, r, c: expand_grads.at[k, f, r, c],
            lambda which: expand_o.at[:, span(which, k * wide, expand_o.shape[-1] // 2)])

    def add_shrink(k):
        add(lambda f, r, c: shrink_grads.at[f, r, c, pl.ds(k * rows, rows)], None)

    def add_map(p):
        add(lambda f, r, c: grads.at[6 + p, f, r, c], lambda which: maps_o.at[p, :, span(which)])

    def add_proj(p):
        add(lambda f, r, c: grads.at[p, f, r, c], lambda which: proj_o.at[p, :, span(which)])

    for k in range(4):
        add_shrink(k)
    for k in range(4):
        add_expand(k)
    for make, p in ((add_map, 1), (add_proj, 3), (add_proj, 4), (add_proj, 5), (add_map, 0), (add_proj, 0), (add_proj, 1), (add_proj, 2)):
        make(p)

    greet(to["far"] + [to["column"], to["row"], to["core"]])
    bias_sums = Vectors(to, vec_sum, vec_in, vec_send, vec_recv, ("core", "column", "row", "far"))
    lanes = [units[k:k + 2] for k in range(0, 16, 2)]
    final = []
    index = {id(unit): k for k, unit in enumerate(units)}

    def close(unit):
        k = index[id(unit)]
        sums[k] = unit.result()
        if ends[k] is None:
            owner = k // 2
            row = pl.ds((k % 2) * rows, rows)

            @pl.when(core == owner)
            def _():
                local = pltpu.make_async_copy(sums.at[k], shrink_o.at[row, span(core)], last_local.at[k])
                local.start()
                local.wait()
                pltpu.make_async_remote_copy(sums.at[k], shrink_o.at[row, span(1 - core)], last_send.at[k], last_recv.at[k],
                                             device_id=to["core"], device_id_type=MESH).wait_recv()

            @pl.when(core != owner)
            def _():
                copy = pltpu.make_async_remote_copy(sums.at[k], shrink_o.at[row, span(core)], last_send.at[k], last_recv.at[k],
                                                    device_id=to["core"], device_id_type=MESH)
                copy.start()
                copy.wait_send()
            return
        own = sums.at[k, pl.ds(pl.multiple_of(core * part, 8), part)]
        other = sums.at[k, pl.ds(pl.multiple_of((1 - core) * part, 8), part)]
        local = pltpu.make_async_copy(own, ends[k](core), last_local.at[k])
        local.start()
        copy = pltpu.make_async_remote_copy(other, ends[k](core), last_send.at[k], last_recv.at[k],
                                            device_id=to["core"], device_id_type=MESH)
        copy.start()
        final.append((local, copy, ends[k](1 - core), k))

    def advance(t):
        if 2 <= t + 1 < len(lanes):
            for unit in lanes[t + 1]:
                unit.start()
        for stage in range(3):
            if 0 <= t - stage < len(lanes):
                for unit in lanes[t - stage]:
                    unit.step(stage)
                    if stage == 2:
                        close(unit)

    def weight_grad(slot, left, right):
        def one(piece, carry):
            value = transposed(left[:, pl.ds(pl.multiple_of(piece * wide, 128), wide)], right).astype(LOW)
            count = wide // rows
            for b in range(count):
                grads[slot, piece * (count // 4) + b // 4, (b // 2) % 2, b % 2] = value[b * rows : (b + 1) * rows]
            return carry

        lax.fori_loop(0, left.shape[1] // wide, one, 0)

    def put_bias(row, values):
        vec_sum[0, row : row + 1, span(core)] = jnp.sum(values.astype(F32), axis=0, keepdims=True)

    def cross(k, source, target):
        copy = pltpu.make_async_remote_copy(source, target, cross_send.at[k], cross_recv.at[k], device_id=to["core"], device_id_type=MESH)
        copy.start()
        return copy

    hidden = hidden_h.shape[1]
    quarter = hidden // 4
    own = pl.ds(pl.multiple_of(core * own_rows, 128), own_rows)
    other = pl.ds(pl.multiple_of((1 - core) * own_rows, 128), own_rows)

    def shrink_gradient(tiles, d_branch_x, d_branch, shrink_w, slope):
        below((("d_branch_x", d_branch_x_h, d_branch_x),))
        ready = []
        for n in range(4):
            copy = pltpu.make_async_copy(hidden_h.at[:, pl.ds(n * quarter, quarter)], tiles.at[n % 2], in_sems.at[30 + n])
            ready.append(copy)
        ready[0].start()
        ready[1].start()
        below((("d_branch", d_branch_h, d_branch), ("shrink", shrink_h, shrink_w), ("slope", slope_h, slope)))
        need("d_branch_x")
        tall = shrink_grads.shape[3]
        for n in range(4):
            ready[n].wait()
            value = transposed(tiles[n % 2], d_branch_x[...]).astype(LOW)
            for b in range(quarter // tall):
                block = n * (quarter // tall) + b
                shrink_grads[block // 4, (block // 2) % 2, block % 2] = value[b * tall : (b + 1) * tall]
            if n + 2 < 4:
                ready[n + 2].start()
        for lane in lanes[:2]:
            for unit in lane:
                unit.start()
        need("d_branch", "shrink", "slope", "vectors")
        sent = []
        for k in range(4):
            which = 1 - core if k < 2 else core
            piece = which * 2 + k % 2
            columns = pl.ds(pl.multiple_of(piece * quarter, 128), quarter)
            here = pl.ds((k % 2) * quarter, quarter)
            value = against(d_branch[...], shrink_w[pl.ds(piece * (quarter // tall), quarter // tall)].reshape(quarter, width))
            value = (value * slope[:, columns].astype(F32)).astype(LOW)
            slope[:, columns] = value
            vec_sum[0, pl.ds(13 + piece, 1), :] = total_rows(value.astype(F32))
            if k < 2:
                sent.append(cross(3 + k, slope.at[:, columns], d_hidden_x.at[own, here]))
            else:
                d_hidden_x[own, here] = value
            if k == 1:
                advance(0)
        for copy in sent:
            copy.wait()

    def expand_gradient(middle, expand_w, d_sum2, middle_sum, d_hidden):
        below((("middle", middle_h, middle), ("expand", expand_h, expand_w), ("d_sum2", d_sum2_h, d_sum2), ("middle_sum", middle_sum_h, middle_sum)))
        need("middle")

        def one(k, carry):
            value = transposed(middle[...], d_hidden_x[:, pl.ds(pl.multiple_of(k * wide, 128), wide)]).astype(LOW)
            for b in range(width // rows):
                expand_grads[k, b // 4, (b // 2) % 2, b % 2] = value[b * rows : (b + 1) * rows]
            return carry

        lax.fori_loop(0, 4, one, 0)
        advance(1)
        need("expand", "d_sum2", "middle_sum")
        vec_sum[0, 5:6] = jnp.zeros((1, width), F32)
        vec_sum[0, 7:8] = jnp.zeros((1, width), F32)
        vec_sum[0, 10:11] = jnp.zeros((1, width), F32)

        def two(t, carry):
            here = pl.ds(pl.multiple_of(t * 256, 256), 256)
            delta = d_sum2[here] + against(d_hidden[here], expand_w[...].reshape(width, hidden))
            unit, factor = norm_parts(middle_sum[here])
            vec_sum[0, 7:8] += total_rows(delta * unit)
            vec_sum[0, 10:11] += total_rows(delta)
            delta = norm_backward(unit, factor, table[7:8], delta)
            d_sum1[here] = delta
            low = delta.astype(LOW)
            d_unpacked[pl.ds(pl.multiple_of(core * own_rows + t * 256, 256), 256)] = low
            vec_sum[0, 5:6] += total_rows(low.astype(F32))
            return carry

        lax.fori_loop(0, own_rows // 256, two, 0)
        return cross(5, d_unpacked.at[own], d_unpacked.at[own])

    def feed_forward(slope):
        like = lambda ref: pltpu.VMEM(ref.shape, ref.dtype)
        pl.run_scoped(
            lambda *refs: shrink_gradient(*refs, slope),
            pltpu.VMEM((2, hidden_h.shape[0], quarter), LOW), like(d_branch_x_h), like(d_branch_h), like(shrink_h),
        )
        pl.run_scoped(
            lambda *refs: expand_gradient(*refs, slope).wait(),
            like(middle_h), like(expand_h), like(d_sum2_h), like(middle_sum_h),
        )

    pl.run_scoped(feed_forward, pltpu.VMEM(slope_h.shape, LOW))

    def attention(map_u, map_p, mixed_u, mixed_p, inputs, memory, qu, ku, vu, qp, kp, vp, probs, packed, d_sum0, weights,
                  d_mixed, d_query, d_key, d_value, d_token_key, d_token_value, d_packed):
        mine = pl.ds(pl.multiple_of(core * wide, 128), wide)
        below((
            ("map_u", maps_h.at[1, mine], map_u), ("mixed_u", mixed_u_h, mixed_u), ("qu", qu_h, qu), ("ku", ku_h, ku), ("vu", vu_h, vu), ("probs_u", probs_u_h, probs),
            ("inputs", inputs_h, inputs), ("packed", packed_h, packed), ("weights", proj_h, weights), ("d_sum0", d_sum0_h, d_sum0),
            ("map_p", maps_h.at[0, mine], map_p), ("mixed_p", mixed_p_h, mixed_p), ("qp", qp_h, qp), ("kp", kp_h, kp), ("vp", vp_h, vp), ("memory", memory_h, memory),
        ))
        need("map_u")

        def from_map_u(piece):
            d_mixed[piece] = against(d_unpacked[piece], map_u[...]).astype(LOW)

        over_rows(d_unpacked.shape[0], 512, from_map_u)
        need("mixed_u")
        weight_grad(7, mixed_u, d_unpacked[:, span(core)])
        need("qu", "ku", "vu", "probs_u")
        unpack = (qu, ku, vu, probs, d_mixed, d_query, d_key, d_value, True)
        attention_backward((0, 1), *unpack)
        advance(2)
        attention_backward((1, 3), *unpack)
        below((("probs_p", probs_p_h, probs),))
        need("inputs", "packed", "weights", "d_sum0")
        partial[...] = against(d_key[...], weights[4]) + against(d_value[...], weights[5])
        packing = cross(0, partial, partial_in)
        weight_grad(3, inputs, d_query[...])
        weight_grad(4, packed, d_key[...])
        weight_grad(5, packed, d_value[...])
        put_bias(3, d_query[...])
        put_bias(4, d_value[...])
        advance(3)
        wide_out[...] = against(d_query[other], weights[3])
        tokens_o[...] = d_sum1[...] + against(d_query[own], weights[3])

        packing.wait()
        d_packed[...] = (d_sum0[...] + (partial[...] + partial_in[...])).astype(LOW)
        need("map_p", "mixed_p")
        d_mixed_p = d_mixed.at[pl.ds(0, 2 * mem_rows)]
        d_mixed_p[...] = against(d_packed[...], map_p[...]).astype(LOW)
        weight_grad(6, mixed_p, d_packed[:, span(core)])
        vec_sum[0, 2:3, :] = total_rows(d_packed[pl.ds(pl.multiple_of(core * mem_rows, 128), mem_rows)].astype(F32))
        need("qp", "kp", "vp", "probs_p")
        pack = (qp, kp, vp, probs, d_mixed_p, d_key, d_token_key, d_token_value, False)
        attention_backward((0, 1), *pack)
        advance(4)
        attention_backward((1, 3), *pack)
        need("memory")
        weight_grad(0, memory, d_key[...])
        advance(5)
        weight_grad(1, inputs, d_token_key[...])
        weight_grad(2, inputs, d_token_value[...])
        put_bias(0, d_key[...])
        put_bias(1, d_token_value[...])
        bias_sums.start()
        advance(6)
        rows_out[...] = against(d_key[...], weights[0])
        wide_out[...] = wide_out[...] + against(d_token_key[other], weights[1]) + against(d_token_value[other], weights[2])
        own_mem = pl.ds(pl.multiple_of(core * mem_rows, 128), mem_rows)
        other_mem = pl.ds(pl.multiple_of((1 - core) * mem_rows, 128), mem_rows)
        token_terms = cross(1, wide_out, wide_in)
        memory_terms = cross(2, rows_out.at[other_mem], rows_in)
        tokens_o[...] = tokens_o[...] + against(d_token_key[own], weights[1]) + against(d_token_value[own], weights[2])
        bias_sums.step(1)
        advance(7)
        memory_terms.wait()
        memory_o[...] = d_sum0[own_mem] + rows_out[own_mem] + rows_in[...]
        token_terms.wait()
        tokens_o[...] = tokens_o[...] + wide_in[...]
        bias_sums.step(2)
        advance(8)
        bias_sums.step(3)
        advance(9)
        vec_o[...] = bias_sums.result()
        for local, copy, ref, k in final:
            local.wait()
            copy.wait_send()
            pltpu.make_async_remote_copy(ref, ref, last_send.at[k], last_recv.at[k],
                                         device_id=to["core"], device_id_type=MESH).wait_recv()
        for unit in units:
            unit.finish()

    like = lambda ref: pltpu.VMEM(ref.shape, ref.dtype)
    tokens, memories = like(qu_h), like(ku_h)
    pl.run_scoped(
        attention,
        pltpu.VMEM((wide, width), LOW), pltpu.VMEM((wide, width), LOW), like(mixed_u_h), like(mixed_p_h), like(inputs_h), like(memory_h),
        tokens, memories, memories, memories, tokens, tokens, like(probs_u_h), like(packed_h), like(d_sum0_h), like(proj_h),
        tokens, tokens, memories, memories, tokens, tokens, like(packed_h),
    )


def reduce_chips(far_count, table, vectors, arrays):
    hidden_full, slope, d_sum2, inputs, memory = arrays[0], arrays[3], arrays[7], arrays[11], arrays[12]
    proj = arrays[-2]
    rows, wide = proj.shape[1] // (4 * far_count), proj.shape[2]
    part, width, hidden = rows // 2, 2 * wide, hidden_full.shape[1]
    all_tokens, own_tokens, all_rows = inputs.shape[0], slope.shape[0], memory.shape[0]
    grid = (far_count, 2, 2)
    any_space = pl.BlockSpec(memory_space=pl.ANY)
    vmem = pl.BlockSpec(memory_space=pltpu.VMEM)
    shapes = ((6, part, width), (2, part, width), (part, hidden), (hidden // (8 * far_count), width), vectors.shape, d_sum2.shape, (all_rows // 2, width))
    return pl.pallas_call(
        functools.partial(reduce_kernel, far_count),
        out_shape=[jax.ShapeDtypeStruct(shape, F32) for shape in shapes],
        in_specs=[vmem] + [any_space] * (1 + len(arrays)),
        out_specs=[vmem] * 7,
        scratch_shapes=[
            pltpu.VMEM((16, 2, far_count, rows, wide), LOW),
            pltpu.VMEM((16, far_count, rows, wide), LOW),
            pltpu.VMEM((16, far_count - 1, rows, wide), LOW),
            pltpu.VMEM((4,) + vectors.shape, F32),
            pltpu.VMEM((2 + far_count,) + vectors.shape, F32),
            pltpu.VMEM((16, rows, wide), F32),
            pltpu.VMEM((8,) + grid + (rows, wide), LOW),
            pltpu.VMEM((4,) + grid + (rows, wide), LOW),
            pltpu.VMEM(grid + (hidden // (4 * far_count), wide), LOW),
            pltpu.VMEM((all_tokens, hidden // 2), LOW),
            pltpu.VMEM((all_tokens, width), LOW),
            pltpu.VMEM((own_tokens, width), F32),
            pltpu.VMEM((all_rows, width), F32),
            pltpu.VMEM((all_rows, width), F32),
            pltpu.VMEM((own_tokens, width), F32),
            pltpu.VMEM((own_tokens, width), F32),
            pltpu.VMEM((all_rows, width), F32),
            pltpu.VMEM((all_rows // 2, width), F32),
            pltpu.SemaphoreType.DMA((16, 6)),
            pltpu.SemaphoreType.DMA((16, 6)),
            pltpu.SemaphoreType.DMA((16,)),
            pltpu.SemaphoreType.DMA((16,)),
            pltpu.SemaphoreType.DMA((16,)),
            pltpu.SemaphoreType.DMA((34,)),
            pltpu.SemaphoreType.DMA((6,)),
            pltpu.SemaphoreType.DMA((6,)),
            pltpu.SemaphoreType.DMA((2 + far_count,)),
            pltpu.SemaphoreType.DMA((2 + far_count,)),
        ],
        compiler_params=pltpu.CompilerParams(
            collective_id=1, has_side_effects=True, vmem_limit_bytes=62 << 20
        ),
        name="backward_and_sums",
    )(table, vectors, *arrays)


def norm_apply(values, gain, shift):
    centre = values - jnp.mean(values, axis=-1, keepdims=True)
    spread = jnp.mean(centre * centre, axis=-1, keepdims=True)
    return centre * lax.rsqrt(spread + epsilon) * gain + shift


def gelu_exact(values):
    return jax.nn.gelu(values, approximate=False)


def heads_of(values):
    return values.reshape(values.shape[0], values.shape[1] // HEAD, HEAD)


def scores_of(queries, keys, valid):
    scores = jnp.einsum(
        "rhd,chd->hrc", heads_of(queries), heads_of(keys), preferred_element_type=F32
    ) * HEAD ** (-0.5)
    if valid is not None:
        scores = jnp.where(valid[None, None, :], scores, -1e30)
    return scores


def attend_forward(queries, keys, values, valid):
    scores = scores_of(queries, keys, valid)
    top = jnp.max(scores, axis=-1, keepdims=True)
    expon = jnp.exp(scores - top)
    total = jnp.sum(expon, axis=-1, keepdims=True)
    probs = to_low(expon / total)
    mixed = jnp.einsum("hrc,chd->rhd", probs, heads_of(values), preferred_element_type=F32)
    return to_low(mixed.reshape(queries.shape)), top + jnp.log(total), probs


def attend_backward(queries, keys, values, valid, log_total, delta_mixed):
    probs = jnp.exp(scores_of(queries, keys, valid) - log_total)
    delta_heads = heads_of(delta_mixed)
    delta_values = jnp.einsum("hrc,rhd->chd", to_low(probs), delta_heads, preferred_element_type=F32)
    delta_probs = jnp.einsum("rhd,chd->hrc", delta_heads, heads_of(values), preferred_element_type=F32)
    row_delta = jnp.sum(delta_probs * probs, axis=-1, keepdims=True)
    score_low = to_low(probs * (delta_probs - row_delta))
    scale = HEAD ** (-0.5)
    delta_query = jnp.einsum("hrc,chd->rhd", score_low, heads_of(keys), preferred_element_type=F32) * scale
    delta_keys = jnp.einsum("hrc,rhd->chd", score_low, heads_of(queries), preferred_element_type=F32) * scale
    return (
        to_low(delta_query.reshape(queries.shape)),
        to_low(delta_keys.reshape(keys.shape)),
        to_low(delta_values.reshape(keys.shape)),
    )


def body(
    custom,
    tokens,
    memory,
    lengths,
    tokens_cotangent,
    memory_cotangent,
    projections,
    output_maps,
    expand_weight,
    shrink_weight,
    projection_bias,
    norm_gain,
    norm_bias,
    expand_bias,
    shrink_bias,
):
    share = lax.axis_index("mem")
    chips = lax.axis_size("seq")
    width = tokens.shape[1]
    hidden = expand_weight.shape[1]
    part = projections.shape[1]
    rows = 2 * part

    def block(values, axis):
        low = to_low(values)
        wide = axis + 1
        return join(half(low, share, wide), swap(half(low, 1 - share, wide)), axis)

    own_count = tokens.shape[0]
    device = 2 * lax.axis_index("seq") + share
    if custom:
        (
            proj_all, maps_all, expand_mat, shrink_mat, table, hidden_full, middle_full, d_branch_x, inputs, rows_all, pack_query, pack_keys,
            pack_values, unpack_query, unpack_keys, unpack_values, pack_probs, unpack_probs, pack_mixed, unpack_mixed, packed_low, new_memory,
            middle_sum, slope, delta_sum2, delta_branch, new_tokens, delta_sum0, vectors,
        ) = gather_chips(
            chips // 4,
            (projections, output_maps, expand_weight, shrink_weight),
            (projection_bias, norm_gain, norm_bias, shrink_bias[None], expand_bias[None]),
            lengths[None], tokens, memory, tokens_cotangent, memory_cotangent,
        )
        proj_all = proj_all.reshape(6, width, width // 2)
        maps_all = maps_all.reshape(2, width, width)
        shrink_mat = shrink_mat.reshape(chips, hidden // chips, width)
        proj_o, maps_o, expand_o, shrink_o, vec_o, tokens_grad, memory_grad = reduce_chips(
            chips // 4,
            table,
            vectors,
            (
                hidden_full, d_branch_x, delta_branch, slope, expand_mat, shrink_mat, middle_full, delta_sum2, middle_sum,
                unpack_mixed, pack_mixed, inputs, rows_all, unpack_query, unpack_keys, unpack_values,
                pack_query, pack_keys, pack_values, unpack_probs, pack_probs, packed_low, delta_sum0, proj_all, maps_all,
            ),
        )
        small = lax.dynamic_slice(vec_o, (0, device * part), (13, part))
        count = hidden // (2 * chips)
        expand_small = lax.dynamic_slice(vec_o[13 : 13 + hidden // width].reshape(-1), (device * count,), (count,))
    else:
        vectors = [to_low(v).astype(F32) for v in (projection_bias, norm_gain, norm_bias, shrink_bias[None], expand_bias)]
        blocks = (block(projections, 1), block(output_maps, 1), block(expand_weight, 0), block(shrink_weight, 0))
        length = lengths[0]
        own_valid = share * own_count + jnp.arange(own_count) < length
        all_valid = jnp.arange(2 * own_count) < length
        gather = lambda values, axis: lax.all_gather(values, "seq", axis=axis, tiled=True)
        proj_all = gather(blocks[0], 1)
        maps_all = both(gather(blocks[1], 1), 2)
        expand_mat = both(gather(blocks[2], 0), 1)
        shrink_mat = both(gather(blocks[3], 0), 1)
        table = lax.all_gather(jnp.concatenate(vectors[:4]), AXES, axis=1, tiled=True)
        line = lax.all_gather(vectors[4], AXES, axis=0, tiled=True)
        table = jnp.concatenate([table, line.reshape(-1, width)])
        biases, gains, shifts, shrink_shift = table[0:6], table[6:9], table[9:12], table[12]
        expand_shift = table[13 : 13 + hidden // width].reshape(hidden)
        bias_half = half(biases, share, 1)
        inputs, rows_all, memory_cot = both(tokens), both(memory), both(memory_cotangent)
        pack_query = to_low(matmul(rows_all, proj_all[0]) + bias_half[0])
        pack_keys = to_low(matmul(inputs, proj_all[1]))
        pack_values = to_low(matmul(inputs, proj_all[2]) + bias_half[1])
        pack_own, pack_total, pack_probs = attend_forward(pack_query, pack_keys, pack_values, all_valid)
        pack_mixed = both(pack_own, 1)
        packed = matmul(pack_mixed, maps_all[0]) + biases[2]
        packed_low = to_low(packed)
        memory_sum = rows_all.astype(F32) + packed
        new_memory = norm_apply(half(memory_sum, share, 0), gains[0], shifts[0])
        unpack_keys = to_low(matmul(packed_low, proj_all[4]))
        unpack_values = to_low(matmul(packed_low, proj_all[5]) + bias_half[4])
        unpack_query = to_low(matmul(inputs, proj_all[3]) + bias_half[3])
        unpack_own, unpack_total, unpack_probs = attend_forward(unpack_query, unpack_keys, unpack_values, None)
        unpack_mixed = both(unpack_own, 1)
        middle_sum = tokens.astype(F32) + matmul(half(unpack_mixed, share, 0), maps_all[1]) + biases[5]
        middle = norm_apply(middle_sum, gains[1], shifts[1])
        middle_low = to_low(middle)
        hidden_in = matmul(middle_low, expand_mat) + expand_shift
        hidden_low = to_low(gelu_exact(hidden_in))
        output_sum = middle + matmul(hidden_low, shrink_mat) + shrink_shift
        layer_out = norm_apply(output_sum, gains[2], shifts[2])
        new_tokens = jnp.where(own_valid[:, None], layer_out, 0.0)

        delta_out = jnp.where(own_valid[:, None], tokens_cotangent.astype(F32), 0.0)
        dropped, norm_back = jax.vjp(norm_apply, output_sum, gains[2], shifts[2])
        delta_sum2, delta_gain2, delta_shift2 = norm_back(delta_out)
        delta_branch = to_low(delta_sum2)
        delta_hidden = matmul_right(delta_branch, shrink_mat)
        dropped, gelu_back = jax.vjp(gelu_exact, hidden_in)
        delta_hidden_in = to_low(gelu_back(delta_hidden)[0])
        delta_shrink = matmul_left(
            both(hidden_low), join(half(delta_branch, share, 1), swap(half(delta_branch, 1 - share, 1)))
        )
        delta_expand = matmul_left(
            both(middle_low), join(half(delta_hidden_in, share, 1), swap(half(delta_hidden_in, 1 - share, 1)))
        )
        delta_middle = delta_sum2 + matmul_right(delta_hidden_in, expand_mat)
        dropped, norm_back = jax.vjp(norm_apply, middle_sum, gains[1], shifts[1])
        delta_sum1, delta_gain1, delta_shift1 = norm_back(delta_middle)
        delta_own = to_low(delta_sum1)
        delta_unpacked = both(delta_own)
        dropped, norm_back = jax.vjp(norm_apply, memory_sum, gains[0], shifts[0])
        delta_sum0 = norm_back(memory_cot.astype(F32))[0]
        dropped, norm_back = jax.vjp(norm_apply, half(memory_sum, share, 0), gains[0], shifts[0])
        dropped, delta_gain0, delta_shift0 = norm_back(memory_cotangent.astype(F32))
        known = [delta_gain0, delta_gain1, delta_gain2, delta_shift0, delta_shift1, delta_shift2, column_sum(delta_branch)]
        delta_map1 = matmul_left(unpack_mixed, half(delta_unpacked, share, 1))
        delta_mixed = to_low(matmul_right(delta_unpacked, half(maps_all[1], share, 0)))
        delta_uquery, delta_ukeys, delta_uvalues = attend_backward(
            unpack_query, unpack_keys, unpack_values, None, unpack_total, delta_mixed
        )
        delta_proj3 = matmul_left(inputs, delta_uquery)
        delta_proj4 = matmul_left(packed_low, delta_ukeys)
        delta_proj5 = matmul_left(packed_low, delta_uvalues)
        partial = matmul_right(delta_ukeys, proj_all[4]) + matmul_right(delta_uvalues, proj_all[5])
        delta_packed = to_low(delta_sum0 + (partial + swap(partial)))
        delta_map0 = matmul_left(pack_mixed, half(delta_packed, share, 1))
        delta_mixed = to_low(matmul_right(delta_packed, half(maps_all[0], share, 0)))
        delta_pquery, delta_pkeys, delta_pvalues = attend_backward(
            pack_query, pack_keys, pack_values, all_valid, pack_total, delta_mixed
        )
        delta_proj0 = matmul_left(rows_all, delta_pquery)
        delta_proj1 = matmul_left(inputs, delta_pkeys)
        delta_proj2 = matmul_left(inputs, delta_pvalues)
        partial = matmul_right(delta_pquery, proj_all[0])
        memory_grad = half(delta_sum0, share, 0) + half(partial, share, 0) + swap(half(partial, 1 - share, 0))
        partial = (
            matmul_right(delta_uquery, proj_all[3])
            + matmul_right(delta_pkeys, proj_all[1])
            + matmul_right(delta_pvalues, proj_all[2])
        )
        tokens_grad = delta_sum1 + half(partial, share, 0) + swap(half(partial, 1 - share, 0))

        zero = jnp.zeros((1, width // 2), F32)

        def spread(values):
            return join(values, zero[0])

        bias_grads = [
            spread(column_sum(delta_pquery)),
            spread(column_sum(delta_pvalues)),
            column_sum(half(delta_packed, share, 0)),
            spread(column_sum(delta_uquery)),
            spread(column_sum(delta_uvalues)),
            column_sum(delta_own),
        ]
        vec_grads = jnp.stack(
            bias_grads + known
        )
        vec_grads = vec_grads.reshape(13, 2 * chips, part).transpose(1, 0, 2).reshape(2 * chips, 13 * part)
        vec_grads = jnp.concatenate([vec_grads, column_sum(delta_hidden_in).reshape(2 * chips, -1)], axis=1)
        vec_grads = jnp.pad(vec_grads, ((0, 0), (0, 1024 - vec_grads.shape[1])))
        reduce = lambda values, axis: lax.psum_scatter(values, "seq", scatter_dimension=axis, tiled=True)

        def finish(values, axis):
            return join(half(values, share, axis), swap(half(values, 1 - share, axis)), axis + 1)

        proj_o = finish(reduce(jnp.stack([delta_proj0, delta_proj1, delta_proj2, delta_proj3, delta_proj4, delta_proj5]), 1), 1)
        maps_o = finish(reduce(jnp.stack([delta_map0, delta_map1]), 1), 1)
        expand_o = finish(reduce(delta_expand, 0), 0)
        shrink_o = finish(reduce(delta_shrink, 0), 0)
        vec_o = lax.psum_scatter(vec_grads, AXES, scatter_dimension=0, tiled=True).reshape(-1)
        small = vec_o[: 13 * part].reshape(13, part)
        expand_small = vec_o[13 * part : 13 * part + hidden // (2 * chips)]
    return (
        new_tokens,
        new_memory,
        tokens_grad,
        memory_grad,
        proj_o,
        maps_o,
        expand_o,
        shrink_o,
        small[0:6],
        small[6:9],
        small[9:12],
        expand_small,
        small[12],
    )


def solution(mesh):
    rows, stacked = P(AXES, None), P(None, AXES, None)
    table, line = P(None, AXES), P(AXES)
    custom = mesh.shape["seq"] == 16 and mesh.shape["mem"] == 2
    return jax.shard_map(
        functools.partial(body, custom),
        mesh=mesh,
        in_specs=(rows, rows, P("seq"), rows, rows, stacked, stacked, rows, rows, table, table, table, line, line),
        out_specs=(rows, rows, rows, rows, stacked, stacked, rows, rows, table, table, table, line, line),
        check_vma=False,
    )
```

```python
import functools

import jax
import jax.numpy as jnp
from jax import lax
from jax.experimental import pallas as pl
from jax.experimental.pallas import tpu as pltpu
from jax.sharding import PartitionSpec as P

HEAD = 64
epsilon = 1e-05
MESH = pl.DeviceIdType.MESH
LOW = jnp.bfloat16
F32 = jnp.float32
AXES = ("seq", "mem")


def matmul(left, right):
    return jnp.dot(left, right, preferred_element_type=F32)


def matmul_left(left, right):
    return lax.dot_general(left, right, (((0,), (0,)), ((), ())), preferred_element_type=F32)


def matmul_right(left, right):
    return lax.dot_general(left, right, (((1,), (1,)), ((), ())), preferred_element_type=F32)


def to_low(values):
    return values.astype(LOW)


def column_sum(values):
    return jnp.sum(values.astype(F32), axis=0)


def swap(values):
    return lax.ppermute(values, "mem", [(0, 1), (1, 0)])


def join(own, other, axis=0):
    first = lax.axis_index("mem") == 0
    return jnp.where(
        first, jnp.concatenate([own, other], axis), jnp.concatenate([other, own], axis)
    )


def both(values, axis=0):
    return join(values, swap(values), axis)


def half(values, index, axis):
    size = values.shape[axis] // 2
    return lax.dynamic_slice_in_dim(values, index * size, size, axis)


FORWARD = (
    (0, 0), (15, 0), (16, 0), (0, 1), (1, 0), (15, 1), (16, 1), (0, 2), (2, 0), (0, 3), (1, 1), (3, 0), (2, 1),
    (4, 0), (3, 1), (1, 2), "q", (5, 0), (2, 2), "k", (6, 0), (4, 1), (7, 0), (5, 1), (3, 2), "v", "pf0", (8, 0),
    "pf1", "pf2", (4, 2), (6, 1), (9, 0), "cx", (10, 0), (4, 3), (7, 1), "yp", "ln0", (5, 2), (11, 0), (12, 0),
    (6, 2), "ku", (8, 1), (9, 1), (13, 0), (10, 1), (14, 0), (11, 1), (7, 2), "qu", "uf0", "uf1", "uf2", (8, 2),
    (12, 1), "ux", (8, 3), (13, 1), (9, 2), "att", (9, 3), (15, 2), (10, 2), (15, 3), (14, 1), (10, 3), "w0", "w2",
    (12, 2), (11, 2), (12, 3), (11, 3), "w1", (13, 2), (14, 2), "w3", (16, 2), (13, 3), (14, 3), (16, 3), "nar",
)
BACKWARD = (
    (0, 0), (1, 0), "dha", (2, 0), (3, 0), "dhb", "de0", (0, 1), (1, 1), (0, 2), (1, 2), "de1", (2, 1), (3, 1),
    "dm0", (2, 2), (3, 2), (4, 0), (5, 0), "dm1", (0, 3), (1, 3), (6, 0), (7, 0), "mix", (2, 3), (3, 3), "gm1",
    (4, 1), (5, 1), (0, 4), "ua0", (4, 2), (5, 2), "ua1", (1, 4), (6, 1), (7, 1), "ua2", (2, 4), (6, 2), (7, 2),
    (8, 0), "pk", (3, 4), "g3", (4, 3), (5, 3), (9, 0), "g45", (6, 3), (7, 3), (10, 0), (11, 0), "gm0", (8, 1),
    (9, 1), (4, 4), "pa0", (5, 4), (8, 2), (9, 2), (12, 0), "pa1", (10, 1), (11, 1), (6, 4), (10, 2), "pa2", (7, 4),
    (11, 2), (9, 3), "g0", (8, 3), (13, 0), "g1", (12, 1), (14, 0), "g2", (10, 3), (9, 4), (12, 2), (15, 0), (16, 0),
    (13, 1), "tok0", (11, 3), (8, 4), (13, 2), (16, 1), "out0", (14, 1), (10, 4), (12, 3), "out1", (11, 4), (14, 2),
    (15, 1), "fin", (13, 3), (12, 4), (15, 2), (16, 2), (15, 3), (13, 4), (14, 3), (16, 3), (15, 4), (14, 4),
    (16, 4),
)


def place(seq):
    return lax.div(seq, 4), lax.rem(lax.div(seq, 2), 2), lax.rem(seq, 2)


def peers(seq, core, far_count):
    far, row, column = place(seq)
    flat = lambda f, r, c: f * 4 + r * 2 + c
    far_peers = [lax.rem(far + k, far_count) for k in range(1, far_count)]
    return {
        "far": [(flat(f, row, column), core) for f in far_peers],
        "far_index": far_peers,
        "column": (flat(far, row, 1 - column), core),
        "row": (flat(far, 1 - row, column), core),
        "core": (seq, 1 - core),
    }


def greet(targets):
    barrier = pltpu.get_barrier_semaphore()
    for target in targets:
        pl.semaphore_signal(barrier, inc=1, device_id=target, device_id_type=MESH)
    pl.semaphore_wait(barrier, len(targets))


class Gather:
    def __init__(self, where, to, first, own, at, shared, sems):
        self.where, self.to, self.own, self.at, self.shared = where, to, own, at, shared
        self.first, self.second = first, ("row" if first == "column" else "column")
        self.send, self.recv = sems
        self.started = []

    def _column(self, near):
        far, row, column = self.where
        row, column = (
            (1 - row if "row" in near else row),
            (1 - column if "column" in near else column),
        )
        return self.at(slice(None), row, column)

    def _copy(self, source, target, k, device):
        return pltpu.make_async_remote_copy(
            source, target, self.send.at[k], self.recv.at[k], device_id=device, device_id_type=MESH
        )

    def _go(self, *args):
        copy = self._copy(*args)
        copy.start()
        self.started.append(copy)

    def _arrived(self, ref, k):
        self._copy(ref, ref, k, self.to["core"]).wait_recv()

    def start(self):
        far, row, column = self.where
        mine = self.at(far, row, column)
        for k, device in enumerate(self.to["far"]):
            self._go(self.own, mine, k, device)

    def step(self, stage):
        far, row, column = self.where
        near = self._column(())
        if stage == 0:
            count = len(self.to["far"])
            for k in range(count):
                sender = self.to["far_index"][count - 1 - k]
                self._arrived(self.at(sender, row, column), k)
            self._go(near, near, 3, self.to[self.first])
            self._go(near, near, 4, self.to[self.second])
            if self.shared:
                self._go(near, near, 6, self.to["core"])
        if stage == 1:
            got = self._column((self.first,))
            self._arrived(got, 3)
            self._go(got, got, 5, self.to[self.second])
            if self.shared:
                self._go(got, got, 7, self.to["core"])
        if stage == 2:
            for k, names in ((4, (self.second,)), (5, (self.first, self.second))):
                got = self._column(names)
                self._arrived(got, k)
                if self.shared:
                    self._go(got, got, 4 + k, self.to["core"])
        if stage == 3 and self.shared:
            for k, names in enumerate(
                ((), (self.first,), (self.second,), (self.first, self.second))
            ):
                self._arrived(self._other(names), 6 + k)

    def _other(self, names):
        keep, self.at = self.at, self.shared
        ref = self._column(names)
        self.at = keep
        return ref

    def finish(self):
        for copy in self.started:
            copy.wait_send()


class GatherNear(Gather):
    def start(self):
        far, row, column = self.where
        mine = self.at(far, row, column)
        self._go(self.own, mine, 0, self.to[self.first])
        self._go(self.own, mine, 1, self.to[self.second])

    def _near(self, names):
        far, row, column = self.where
        return self.at(
            far, 1 - row if "row" in names else row, 1 - column if "column" in names else column
        )

    def step(self, stage):
        far = self.where[0]
        all_of = slice(None)
        count = len(self.to["far"])
        if stage == 0:
            got = self._near((self.first,))
            self._arrived(got, 0)
            self._go(got, got, 2, self.to[self.second])
        if stage == 1:
            self._arrived(self._near((self.second,)), 1)
            self._arrived(self._near((self.first, self.second)), 2)
            plane = self.at(far, all_of, all_of)
            for k, device in enumerate(self.to["far"]):
                self._go(plane, plane, 3 + k, device)
            if self.shared:
                self._go(plane, plane, 3 + count, self.to["core"])
        if stage == 2:
            for k in range(count):
                plane = self.at(self.to["far_index"][count - 1 - k], all_of, all_of)
                self._arrived(plane, 3 + k)
                if self.shared:
                    self._go(plane, plane, 4 + count + k, self.to["core"])
        if stage == 3 and self.shared:
            self._arrived(self.shared(far, all_of, all_of), 3 + count)
            for k in range(count):
                plane = self.shared(self.to["far_index"][count - 1 - k], all_of, all_of)
                self._arrived(plane, 4 + count + k)


def transposed(left, right):
    return lax.dot_general(left, right, (((0,), (0,)), ((), ())), preferred_element_type=F32)


def against(left, right):
    return lax.dot_general(left, right, (((1,), (1,)), ((), ())), preferred_element_type=F32)


def plain(left, right):
    return lax.dot_general(left, right, (((1,), (0,)), ((), ())), preferred_element_type=F32)


def over_rows(count, tile, work):
    def one(t, carry):
        work(pl.ds(pl.multiple_of(t * tile, tile), tile))
        return carry

    lax.fori_loop(0, count // tile, one, 0)


class Vectors:
    def __init__(self, to, held, arrived, send, recv, order):
        self.to, self.held, self.arrived, self.sems, self.order = to, held, arrived, (send, recv), order
        self.flying, self.slot = [], 0

    def _go(self, k):
        name = self.order[k]
        for device in self.to["far"] if name == "far" else [self.to[name]]:
            slot = self.slot
            copy = pltpu.make_async_remote_copy(
                self.held.at[k], self.arrived.at[slot], self.sems[0].at[slot], self.sems[1].at[slot],
                device_id=device, device_id_type=MESH,
            )
            copy.start()
            self.flying.append((slot, copy))
            self.slot += 1

    def _take(self, k):
        value = self.held[k]
        for slot, copy in self.flying:
            copy.wait()
            value = value + self.arrived[slot]
        self.flying = []
        return value

    def start(self):
        self._go(0)

    def step(self, k):
        self.held[k] = self._take(k - 1)
        self._go(k)

    def result(self):
        return self._take(3)


def attention_forward(pairs, queries, keys, values, valid, probs, mixed, first_lane, turned):
    for pair in range(*pairs):
        lanes = slice(pair * 128, pair * 128 + 128)
        query, key, value = queries[:, lanes] * LOW(HEAD ** (-0.5)), keys[:, lanes], values[:, lanes]
        outs = []
        for j in range(2):
            part = slice(j * HEAD, (j + 1) * HEAD)
            scores = against(key[:, part], query[:, part]) if turned else against(query[:, part], key[:, part])
            if valid is not None:
                scores = jnp.where(lax.broadcasted_iota(jnp.int32, scores.shape, 1) < valid[0, 0], scores, -1e30)
            axis = 0 if turned else 1
            expon = jnp.exp(scores - jnp.max(scores, axis=axis, keepdims=True))
            prob = (expon * (1.0 / jnp.sum(expon, axis=axis, keepdims=True))).astype(LOW)
            probs[pair * 2 + j] = prob
            outs.append((transposed if turned else plain)(prob, value[:, part]))
        mixed[:, pl.ds(pl.multiple_of(first_lane + pair * 128, 128), 128)] = jnp.concatenate(outs, axis=1).astype(LOW)


def norm_parts(values):
    centre = values - jnp.mean(values, axis=-1, keepdims=True)
    factor = lax.rsqrt(jnp.mean(centre * centre, axis=-1, keepdims=True) + epsilon)
    return centre * factor, factor


def norm_backward(unit, factor, gain, delta):
    scaled = delta * gain
    return factor * (scaled - jnp.mean(scaled, axis=-1, keepdims=True) - unit * jnp.mean(scaled * unit, axis=-1, keepdims=True))


def total_rows(values):
    return jnp.sum(values, axis=0, keepdims=True)


def gather_kernel(far_count, proj_in, maps_in, expand_in, shrink_in, bias_in, gain_in, shift_in, shrink_bias_in, expand_bias_in, length,
                  tokens, rows_in, token_cot, memory_cot,
                  proj_o, maps_o, expand_o, shrink_o, table_o, hidden_o, middle_full_o, d_branch_x_o,
                  inputs_o, memory_o, qp_o, kp_o, vp_o, qu_o, ku_o, vu_o,
                  probs_p_o, probs_u_o, mixed_p_o, mixed_u_o, packed_o, new_memory_o, middle_sum_o,
                  slope_o, d_sum2_o, d_branch_o, new_tokens_o, d_sum0_o, grad_table_o,
                  inputs, memory, qp, kp, vp, qu, ku, vu, probs_p, probs_u, mixed_p, mixed_u, packed, new_memory, middle_sum,
                  slope, d_sum2, d_branch, new_tokens, d_sum0, grad_table,
                  memory_sum, middle, middle_low, hidden, cot, expand_w, shrink_w,
                  weights, map_p, map_u, table, own_vec, vec, vec_all,
                  proj_f, maps_f, expand_f, shrink_f, proj, maps, expand, shrink,
                  send, recv, local, out_sems, cross_send, cross_recv, raw_local, raw_send, raw_recv):
    seq, core = lax.axis_index("seq"), lax.axis_index("mem")
    where = place(seq)
    far, row, column = where
    to = peers(seq, core, far_count)
    wide = maps.shape[-1]
    width = 2 * wide
    own_tokens, own_rows = tokens.shape[0], rows_in.shape[0]

    def cols(which, start=0):
        return pl.ds(pl.multiple_of(which * expand.shape[-1] + start, 128), wide)

    def span(which):
        return pl.ds(pl.multiple_of(which * wide, 128), wide)

    copies, stores = [], []

    def keep(source, target):
        copy = pltpu.make_async_copy(source, target, local.at[len(copies)])
        copy.start()
        copies.append(copy)
        return copy

    def store(source, target):
        copy = pltpu.make_async_copy(source, target, out_sems.at[len(stores)])
        copy.start()
        stores.append(copy)

    own_t = pl.ds(pl.multiple_of(core * own_tokens, 128), own_tokens)
    own_m = pl.ds(pl.multiple_of(core * own_rows, 128), own_rows)
    raw = []
    for n, (source, target) in enumerate(((proj_in, proj_f), (maps_in, maps_f), (expand_in, expand_f), (shrink_in, shrink_f))):
        count, size = source.shape[-2], source.shape[-1] // 2
        place_rows = pl.ds(pl.multiple_of(core * count, 8), count)
        mine, theirs = (pl.ds(pl.multiple_of(which * size, 128), size) for which in (core, 1 - core))
        lead = (slice(None),) * (len(source.shape) - 2)
        raw.append((n, source.at[lead + (slice(None), mine)], source.at[lead + (slice(None), theirs)], target.at[lead + (place_rows,)]))
    for n, own, other, target in raw:
        pltpu.make_async_copy(own, target, raw_local.at[n]).start()
    device = 2 * seq + core
    own_vec[...] = jnp.zeros_like(own_vec)
    for first_row, source in ((0, bias_in), (6, gain_in), (9, shift_in), (12, shrink_bias_in), (16, expand_bias_in)):
        own_vec[first_row : first_row + source.shape[0], 0 : source.shape[1]] = source[...]
    small, large = bias_in.shape[1], expand_bias_in.shape[1]

    def window(start):
        return lax.min(lax.div(start, 128), 2 * wide // 128 - 2)

    offsets = (small * device, lax.rem(large * device, 2 * wide))
    moved = [pltpu.roll(own_vec[k : k + 16 - k // 2], offsets[n] - 128 * window(offsets[n]), 1) for n, k in enumerate((0, 16))]
    vec[...] = jnp.concatenate([moved[0], moved[1], jnp.zeros_like(moved[1])], axis=0).astype(LOW)

    units = []

    def add(first, own, at, shared, kind=Gather):
        k = len(units)
        units.append(kind(where, to, first, own, at, shared, (send.at[k], recv.at[k])))

    def add_proj(first, p):
        add(first, proj.at[p], lambda f, r, c: proj_o.at[p, f, r, c], None)

    def add_map(first, p):
        add(first, maps.at[p], lambda f, r, c: maps_o.at[p, f, r, c, :, span(core)],
            lambda f, r, c: maps_o.at[p, f, r, c, :, span(1 - core)])

    def add_expand(first, k):
        add(first, expand.at[:, pl.ds(k * wide, wide)], lambda f, r, c: expand_o.at[f, r, c, :, cols(core, k * wide)],
            lambda f, r, c: expand_o.at[f, r, c, :, cols(1 - core, k * wide)])

    def add_shrink(first, k):
        rows = shrink.shape[0] // 4
        part = pl.ds(k * rows, rows)
        add(first, shrink.at[part], lambda f, r, c: shrink_o.at[f, r, c, part, span(core)],
            lambda f, r, c: shrink_o.at[f, r, c, part, span(1 - core)], GatherNear if k >= 2 else Gather)

    add("column", vec, lambda f, r, c: vec_all.at[core, f, r, c], lambda f, r, c: vec_all.at[1 - core, f, r, c])
    for first, second in (
        ((add_proj, 0), (add_proj, 1)), ((add_proj, 2), (add_map, 0)), ((add_proj, 4), (add_proj, 5)), ((add_proj, 3), (add_map, 1)),
        ((add_expand, 0), (add_expand, 1)), ((add_expand, 2), (add_expand, 3)), ((add_shrink, 0), (add_shrink, 1)), ((add_shrink, 2), (add_shrink, 3)),
    ):
        first[0]("column", first[1])
        second[0]("row", second[1])

    def cross(k, source, target):
        copy = pltpu.make_async_remote_copy(source, target, cross_send.at[k], cross_recv.at[k], device_id=to["core"], device_id_type=MESH)
        copy.start()
        return copy

    greet(to["far"] + [to["column"], to["row"], to["core"]])
    for n, own, other, target in raw:
        pltpu.make_async_remote_copy(other, target, raw_send.at[n], raw_recv.at[n], device_id=to["core"], device_id_type=MESH).start()
    crossed = [cross(0, tokens, inputs.at[own_t]), cross(1, rows_in, memory.at[own_m]), cross(4, memory_cot, cot.at[own_m])]
    keep(vec, vec_all.at[core, far, row, column])
    units[0].start()
    targets = (
        (proj_f, proj, proj_o.at[:, far, row, column]),
        (maps_f, maps, maps_o.at[:, far, row, column, :, span(core)]),
        (expand_f, expand, expand_o.at[far, row, column, :, pl.ds(pl.multiple_of(core * expand.shape[-1], 128), expand.shape[-1])]),
        (shrink_f, shrink, shrink_o.at[far, row, column, :, span(core)]),
    )
    groups = ((1, 2, 3), (4, 5, 6, 7, 8), (9, 10, 11, 12), (13, 14, 15, 16))
    for (n, own, other, target), (wide_block, block, place_of), group in zip(raw, targets, groups):
        pltpu.make_async_copy(own, target, raw_local.at[n]).wait()
        pltpu.make_async_remote_copy(other, target, raw_send.at[n], raw_recv.at[n], device_id=to["core"], device_id_type=MESH).wait()
        block[...] = wide_block[...].astype(LOW)
        keep(block, place_of)
        for index in group:
            units[index].start()
    keep(tokens, inputs.at[own_t])
    keep(rows_in, memory.at[own_m])
    keep(memory_cot, cot.at[own_m])
    for copy in copies:
        copy.wait()
    fetched = {}

    def fetch(key, source, target):
        copy = pltpu.make_async_copy(source, target, local.at[len(copies) + sum(len(v) for v in fetched.values())])
        copy.start()
        fetched.setdefault(key, []).append(copy)

    def need(*keys):
        for key in keys:
            for copy in fetched[key]:
                copy.wait()

    tall = width
    names = ("vec", "p0", "p1", "p2", "m0", "p4", "p5", "p3", "m1", "e0", "e1", "e2", "e3", "s0", "s1", "s2", "s3")

    def complete(name):
        k = int(name[1]) if name != "vec" else 0
        if name[0] == "p":
            fetch(name, proj_o.at[k], weights.at[k])
        elif name[0] == "m":
            fetch(name, maps_o.at[k], (map_p, map_u)[k])
        elif name[0] == "e":
            for side in range(2):
                columns = pl.ds(side * expand.shape[-1] + k * wide, wide)
                fetch(name, expand_o.at[:, :, :, :, columns], expand_w.at[:, :, :, :, columns])
        elif name[0] == "s":
            rows = shrink.shape[0] // 4
            part = pl.ds(k * rows, rows)
            fetch(name, shrink_o.at[:, :, :, part], shrink_w.at[:, :, :, part])

    def weight(p):
        return weights[p].reshape(-1, wide)

    def project(p, source, target, bias):
        need("p" + str(p))

        def one(piece):
            value = plain(source[piece], weight(p))
            if bias is not None:
                value = value + table[bias : bias + 1, span(core)]
            target[piece] = value.astype(LOW)

        over_rows(source.shape[0], min(512, source.shape[0]), one)

    def gain(k):
        return table[6 + k : 7 + k]

    def shift(k):
        return table[9 + k : 10 + k]

    def from_other(k, ref):
        copy = pltpu.make_async_remote_copy(ref, ref, cross_send.at[k], cross_recv.at[k], device_id=to["core"], device_id_type=MESH)
        copy.wait_send()
        copy.wait_recv()

    def make_k():
        crossed[0].wait()
        project(1, inputs, kp, None)
        store(inputs, inputs_o)

    def make_q():
        table[...] = jnp.zeros_like(table)
        for k in range(8 * far_count):
            block = vec_all[k % 2, k // 8, (k // 4) % 2, (k // 2) % 2].astype(F32)
            for count, row, start in ((13, 0, small * k), (1, 13 + large * k // width, (large * k) % width)):
                first = 128 * min(start // 128, width // 128 - 2)
                from_row = 0 if count == 13 else 16
                table[row : row + count, first : first + 256] += block[from_row : from_row + count]
        store(table, table_o)
        crossed[1].wait()
        project(0, memory, qp, 0)
        store(memory, memory_o)

    def make_packed():
        from_other(2, mixed_p.at[:, span(core)])
        need("m0")
        for source, target in ((qp, qp_o), (kp, kp_o), (vp, vp_o), (probs_p, probs_p_o), (mixed_p, mixed_p_o)):
            store(source, target)
        value = plain(mixed_p[...], map_p[...].reshape(-1, width)) + table[2:3]
        packed[...] = value.astype(LOW)
        memory_sum[...] = memory[...].astype(F32) + value

    def make_memory():
        crossed[2].wait()
        unit, factor = norm_parts(memory_sum[...])
        memory_sum[...] = unit
        d_sum0[...] = norm_backward(unit, factor, gain(0), cot[...].astype(F32))
        unit, delta = memory_sum[own_m], memory_cot[...].astype(F32)
        new_memory[...] = unit * gain(0) + shift(0)
        grad_table[...] = jnp.zeros_like(grad_table)
        grad_table[6:7] = total_rows(delta * unit)
        grad_table[9:10] = total_rows(delta)
        for source, target in ((packed, packed_o), (d_sum0, d_sum0_o), (new_memory, new_memory_o)):
            store(source, target)

    def make_unpack():
        project(4, packed, ku, None)
        project(5, packed, vu, 4)
        store(ku, ku_o)
        store(vu, vu_o)

    sent = []

    def make_middle():
        from_other(3, mixed_u.at[:, span(core)])
        need("m1")
        for source, target in ((qu, qu_o), (probs_u, probs_u_o), (mixed_u, mixed_u_o)):
            store(source, target)

        def attended(t, carry):
            here = pl.ds(pl.multiple_of(t * 256, 256), 256)
            there = pl.ds(pl.multiple_of(core * own_tokens + t * 256, 256), 256)
            value = plain(mixed_u[there], map_u[...].reshape(-1, width)) + table[5:6]
            value = tokens[here].astype(F32) + value
            middle_sum[here] = value
            value = norm_parts(value)[0] * gain(1) + shift(1)
            middle[here] = value
            middle_low[here] = value.astype(LOW)
            return carry

        lax.fori_loop(0, own_tokens // 256, attended, 0)
        store(middle_sum, middle_sum_o)
        store(middle_low, middle_full_o.at[own_t])
        sent.append(cross(5, middle_low, middle_full_o.at[own_t]))

    def widen(n):
        columns = pl.ds(n * tall, tall)
        if n < 2:
            need("e" + str(2 * n), "e" + str(2 * n + 1))
        value = plain(middle_low[...], expand_w[:, :, :, :, columns].reshape(-1, tall)) + table[13 + n : 14 + n]
        share = 0.5 + 0.5 * lax.erf(value * 0.5**0.5)
        hidden[:, columns] = (value * share).astype(LOW)
        slope[:, columns] = (share + value * (0.3989422804014327 * jnp.exp(-0.5 * value * value))).astype(LOW)
        store(hidden.at[:, columns], hidden_o.at[own_t, columns])
        store(slope.at[:, columns], slope_o.at[:, columns])
        sent.append(cross(6 + n, hidden.at[:, columns], hidden_o.at[own_t, columns]))

    def narrow(t, carry):
        here = pl.ds(pl.multiple_of(t * 256, 256), 256)
        value = middle[here] + (plain(hidden[here], shrink_w[...].reshape(-1, width)) + table[12:13])
        unit, factor = norm_parts(value)
        live = core * own_tokens + t * 256 + lax.broadcasted_iota(jnp.int32, (256, 1), 0) < length[0, 0]
        new_tokens[here] = jnp.where(live, unit * gain(2) + shift(2), 0.0)
        delta = jnp.where(live, token_cot[here].astype(F32), 0.0)
        grad_table[8:9] += total_rows(delta * unit)
        grad_table[11:12] += total_rows(delta)
        value = norm_backward(unit, factor, gain(2), delta)
        d_sum2[here] = value
        value = value.astype(LOW)
        d_branch[here] = value
        grad_table[12:13] += total_rows(value.astype(F32))
        return carry

    def make_tokens():
        need("s0", "s1", "s2", "s3")
        lax.fori_loop(0, own_tokens // 256, narrow, 0)
        sent.append(cross(10, d_branch.at[:, span(1 - core)], d_branch_x_o.at[own_t]))
        store(d_branch.at[:, span(core)], d_branch_x_o.at[own_t])
        for source, target in ((d_sum2, d_sum2_o), (d_branch, d_branch_o), (new_tokens, new_tokens_o), (grad_table, grad_table_o)):
            store(source, target)

    work = {
        "k": make_k,
        "q": make_q,
        "v": lambda: project(2, inputs, vp, 1),
        "cx": lambda: cross(2, mixed_p.at[:, span(core)], mixed_p.at[:, span(core)]),
        "yp": make_packed,
        "ln0": make_memory,
        "ku": make_unpack,
        "qu": lambda: project(3, inputs, qu, 3),
        "ux": lambda: cross(3, mixed_u.at[:, span(core)], mixed_u.at[:, span(core)]),
        "att": make_middle,
        "nar": make_tokens,
    }
    for n in range(3):
        work["pf" + str(n)] = functools.partial(attention_forward, (n, n + 1), qp, kp, vp, length, probs_p, mixed_p, core * wide, False)
        work["uf" + str(n)] = functools.partial(attention_forward, (n, n + 1), qu, ku, vu, None, probs_u, mixed_u, core * wide, True)
    for n in range(4):
        work["w" + str(n)] = functools.partial(widen, n)
    for item in FORWARD:
        if isinstance(item, str):
            work[item]()
            continue
        index, stage = item
        units[index].step(stage)
        if stage == (3 if units[index].shared else 2):
            complete(names[index])
    for copy in sent:
        copy.wait()
    for copy in stores:
        copy.wait()
    for unit in units:
        unit.finish()


def gather_chips(far_count, weights, vectors, length, tokens, memory, token_cot, memory_cot):
    grid = (far_count, 2, 2)
    width, hidden = weights[0].shape[-1], weights[2].shape[-1]
    rows, wide = 2 * weights[0].shape[1], width // 2
    blocks = ((6, rows, wide), (2, rows, wide), (rows, hidden // 2), (2 * weights[3].shape[0], wide))
    table = (24, width)
    own_tokens, own_rows = tokens.shape[0], memory.shape[0]
    all_tokens, all_rows = 2 * own_tokens, 2 * own_rows
    count = wide // HEAD
    passed = (
        ((6,) + grid + (rows, wide), LOW),
        ((2,) + grid + (rows, width), LOW),
        (grid + (rows, hidden), LOW),
        (grid + (blocks[3][0], width), LOW),
        (table, F32),
        ((all_tokens, hidden), LOW),
        ((all_tokens, width), LOW),
        ((all_tokens, wide), LOW),
    )
    kept = (
        ((all_tokens, width), LOW),
        ((all_rows, width), LOW),
        ((all_rows, wide), LOW),
        ((all_tokens, wide), LOW),
        ((all_tokens, wide), LOW),
        ((all_tokens, wide), LOW),
        ((all_rows, wide), LOW),
        ((all_rows, wide), LOW),
        ((count, all_rows, all_tokens), LOW),
        ((count, all_rows, all_tokens), LOW),
        ((all_rows, width), LOW),
        ((all_tokens, width), LOW),
        ((all_rows, width), LOW),
        ((own_rows, width), F32),
        ((own_tokens, width), F32),
        ((own_tokens, hidden), LOW),
        ((own_tokens, width), F32),
        ((own_tokens, width), LOW),
        ((own_tokens, width), F32),
        ((all_rows, width), F32),
        (table, F32),
    )
    inner = (
        ((all_rows, width), F32),
        ((own_tokens, width), F32),
        ((own_tokens, width), LOW),
        ((own_tokens, hidden), LOW),
        ((all_rows, width), LOW),
        passed[2],
        passed[3],
        passed[0],
        (passed[1][0][1:], LOW),
        (passed[1][0][1:], LOW),
        (table, F32),
        ((24, 256), F32),
        ((32, 256), LOW),
        ((2,) + grid + (32, 256), LOW),
    ) + tuple((block, F32) for block in blocks) + tuple((block, LOW) for block in blocks)
    any_space = pl.BlockSpec(memory_space=pl.ANY)
    return pl.pallas_call(
        functools.partial(gather_kernel, far_count),
        out_shape=[jax.ShapeDtypeStruct(*entry) for entry in passed + kept],
        in_specs=[any_space] * 4
        + [pl.BlockSpec(memory_space=pltpu.VMEM)] * 5
        + [pl.BlockSpec(memory_space=pltpu.SMEM)]
        + [pl.BlockSpec(memory_space=pltpu.VMEM)] * 4,
        out_specs=[any_space] * (len(passed) + len(kept)),
        scratch_shapes=[pltpu.VMEM(*entry) for entry in kept + inner]
        + [
            pltpu.SemaphoreType.DMA((17, 10)),
            pltpu.SemaphoreType.DMA((17, 10)),
            pltpu.SemaphoreType.DMA((28,)),
            pltpu.SemaphoreType.DMA((36,)),
            pltpu.SemaphoreType.DMA((11,)),
            pltpu.SemaphoreType.DMA((11,)),
            pltpu.SemaphoreType.DMA((4,)),
            pltpu.SemaphoreType.DMA((4,)),
            pltpu.SemaphoreType.DMA((4,)),
        ],
        compiler_params=pltpu.CompilerParams(
            collective_id=0, has_side_effects=True, vmem_limit_bytes=62 << 20
        ),
        name="gather_and_forward",
    )(*weights, *vectors, length, tokens, memory, token_cot, memory_cot)


class Reduce:
    def __init__(self, where, to, first, at, half_in, quarter_in, far_in, sems):
        self.where, self.to, self.at = where, to, at
        self.half_in, self.quarter_in, self.far_in = half_in, quarter_in, far_in
        self.first, self.second = first, ("row" if first == "column" else "column")
        self.send, self.recv = sems

    def _copy(self, source, target, k, device):
        return pltpu.make_async_remote_copy(
            source, target, self.send.at[k], self.recv.at[k], device_id=device, device_id_type=MESH
        )

    def _go(self, *args):
        self._copy(*args).start()

    def _arrived(self, ref, k):
        self._copy(ref, ref, k, self.to["core"]).wait_recv()

    def _column(self, near):
        far, row, column = self.where
        row, column = (
            (1 - row if "row" in near else row),
            (1 - column if "column" in near else column),
        )
        return self.at(slice(None), row, column)

    def start(self):
        for k, names in ((1, (self.first, self.second)), (0, (self.second,))):
            self._go(self._column(names), self.half_in.at[k], k, self.to[self.second])

    def _add(self, target, other):
        for k in range(target.shape[0]):
            target[k] = (target[k].astype(F32) + other[k].astype(F32)).astype(LOW)

    def step(self, stage):
        count = len(self.to["far"])
        own, near = self._column(()), self._column((self.first,))
        if stage == 0:
            self.start()
        if stage == 1:
            self._arrived(self.half_in.at[1], 1)
            self._add(near, self.half_in.at[1])
            self._go(near, self.quarter_in, 2, self.to[self.first])
        if stage == 2:
            self._arrived(self.half_in.at[0], 0)
            self._add(own, self.half_in.at[0])
        if stage == 3:
            self._arrived(self.quarter_in, 2)
            self._add(own, self.quarter_in)
            for k, device in enumerate(self.to["far"]):
                self._go(own.at[self.to["far_index"][k]], self.far_in.at[k], 3 + k, device)
        if stage == 4:
            for k in range(count):
                self._arrived(self.far_in.at[k], 3 + k)

    def result(self):
        value = self._column(())[self.where[0]].astype(F32)
        for k in range(len(self.to["far"])):
            value = value + self.far_in[k].astype(F32)
        return value

    def finish(self):
        refs = [self.half_in.at[0], self.half_in.at[1], self.quarter_in]
        refs += [self.far_in.at[k] for k in range(len(self.to["far"]))]
        for k, ref in enumerate(refs):
            self._copy(ref, ref, k, self.to["core"]).wait_send()


def attention_backward(pairs, queries, keys, values, probs, mixed, d_query, d_key, d_value, turned):
    scale = HEAD ** (-0.5)
    for pair in range(*pairs):
        lanes = slice(pair * 128, pair * 128 + 128)
        query, delta = queries[:, lanes], mixed[:, lanes]
        key, value = keys[:, lanes], values[:, lanes]
        by_query, by_key = (transposed, plain) if turned else (plain, transposed)
        parts = ([], [], [])
        for j in range(2):
            part = slice(j * HEAD, (j + 1) * HEAD)
            prob_low = probs[pair * 2 + j]
            prob = prob_low.astype(F32)
            d_prob = against(value[:, part], delta[:, part]) if turned else against(delta[:, part], value[:, part])
            row_delta = jnp.sum(d_prob * prob, axis=0 if turned else 1, keepdims=True)
            d_score = (prob * (d_prob - row_delta)).astype(LOW)
            parts[0].append(by_query(d_score, key[:, part]))
            parts[1].append(by_key(d_score, query[:, part]))
            parts[2].append(by_key(prob_low, delta[:, part]))
        d_query[:, lanes] = (jnp.concatenate(parts[0], axis=1) * scale).astype(LOW)
        d_key[:, lanes] = (jnp.concatenate(parts[1], axis=1) * scale).astype(LOW)
        d_value[:, lanes] = jnp.concatenate(parts[2], axis=1).astype(LOW)


def reduce_kernel(far_count, table, vectors_in, hidden_h, d_branch_x_h, d_branch_h, slope_h, expand_h, shrink_h, middle_h, d_sum2_h, middle_sum_h,
                  mixed_u_h, mixed_p_h, inputs_h, memory_h, qu_h, ku_h, vu_h, qp_h, kp_h, vp_h, probs_u_h, probs_p_h, packed_h, d_sum0_h, proj_h, maps_h,
                  proj_o, maps_o, expand_o, shrink_o, vec_o, tokens_o, memory_o,
                  half_in, quarter_in, far_in, vec_sum, vec_in, sums,
                  grads, expand_grads, shrink_grads, d_hidden_x, d_unpacked, d_sum1, partial, partial_in, wide_out, wide_in, rows_out, rows_in,
                  send, recv, last_send, last_recv, last_local, in_sems, cross_send, cross_recv, vec_send, vec_recv):
    seq, core = lax.axis_index("seq"), lax.axis_index("mem")
    where = place(seq)
    to = peers(seq, core, far_count)
    wide = proj_h.shape[-1]
    width = 2 * wide
    rows = proj_o.shape[-2] * 2
    part = rows // 2
    own_rows = d_sum1.shape[0]
    mem_rows = packed_h.shape[0] // 2
    units, ends = [], []

    def span(which, start=0, whole=None):
        return pl.ds(pl.multiple_of(which * (whole or wide) + start, 128), wide)

    loads = {}

    def fetch(name, source, target):
        copy = pltpu.make_async_copy(source, target, in_sems.at[len(loads)])
        copy.start()
        loads[name] = copy

    def need(*names):
        for name in names:
            loads[name].wait()

    def below(refs):
        for name, source, target in refs:
            fetch(name, source, target)

    fetch("vectors", vectors_in, vec_sum.at[0])

    def add(at, end):
        k = len(units)
        first = "column" if k % 2 == 0 else "row"
        units.append(Reduce(where, to, first, at, half_in.at[k], quarter_in.at[k], far_in.at[k], (send.at[k], recv.at[k])))
        ends.append(end)

    def add_expand(k):
        add(lambda f, r, c: expand_grads.at[k, f, r, c],
            lambda which: expand_o.at[:, span(which, k * wide, expand_o.shape[-1] // 2)])

    def add_shrink(k):
        add(lambda f, r, c: shrink_grads.at[f, r, c, pl.ds(k * rows, rows)], None)

    def add_map(p):
        add(lambda f, r, c: grads.at[6 + p, f, r, c], lambda which: maps_o.at[p, :, span(which)])

    def add_proj(p):
        add(lambda f, r, c: grads.at[p, f, r, c], lambda which: proj_o.at[p, :, span(which)])

    for k in range(4):
        add_shrink(k)
    for k in range(4):
        add_expand(k)
    for make, p in ((add_map, 1), (add_proj, 3), (add_proj, 4), (add_proj, 5), (add_map, 0), (add_proj, 0), (add_proj, 1), (add_proj, 2)):
        make(p)

    greet(to["far"] + [to["column"], to["row"], to["core"]])
    bias_sums = Vectors(to, vec_sum, vec_in, vec_send, vec_recv, ("core", "column", "row", "far"))

    def last(k, source, target):
        return pltpu.make_async_remote_copy(source, target, last_send.at[k], last_recv.at[k], device_id=to["core"], device_id_type=MESH)

    def close(k, start):
        if ends[k] is None:
            owner = k // 2
            row = pl.ds((k % 2) * rows, rows)

            @pl.when(core == owner)
            def _():
                local = pltpu.make_async_copy(sums.at[k], shrink_o.at[row, span(core)], last_local.at[k])
                if start:
                    local.start()
                else:
                    local.wait()
                    last(k, sums.at[k], shrink_o.at[row, span(1 - core)]).wait_recv()

            @pl.when(core != owner)
            def _():
                copy = last(k, sums.at[k], shrink_o.at[row, span(core)])
                if start:
                    copy.start()
                else:
                    copy.wait_send()

            return
        own = sums.at[k, pl.ds(pl.multiple_of(core * part, 8), part)]
        other = sums.at[k, pl.ds(pl.multiple_of((1 - core) * part, 8), part)]
        local = pltpu.make_async_copy(own, ends[k](core), last_local.at[k])
        copy = last(k, other, ends[k](core))
        if start:
            local.start()
            copy.start()
        else:
            local.wait()
            copy.wait_send()
            last(k, ends[k](1 - core), ends[k](1 - core)).wait_recv()

    place_in_plan = [0]

    def turn(name):
        while place_in_plan[0] < len(BACKWARD):
            item = BACKWARD[place_in_plan[0]]
            place_in_plan[0] += 1
            if isinstance(item, str):
                if item != name:
                    raise ValueError(item)
                return
            index, stage = item
            if index == 16:
                if stage == 0:
                    bias_sums.start()
                elif stage < 4:
                    bias_sums.step(stage)
                else:
                    vec_o[...] = bias_sums.result()
                continue
            units[index].step(stage)
            if stage == 4:
                sums[index] = units[index].result()
                close(index, True)

    def weight_grad(slot, left, right):
        def one(piece, carry):
            value = transposed(left[:, pl.ds(pl.multiple_of(piece * wide, 128), wide)], right).astype(LOW)
            count = wide // rows
            for b in range(count):
                grads[slot, piece * (count // 4) + b // 4, (b // 2) % 2, b % 2] = value[b * rows : (b + 1) * rows]
            return carry

        lax.fori_loop(0, left.shape[1] // wide, one, 0)

    def put_bias(row, values):
        vec_sum[0, row : row + 1, span(core)] = jnp.sum(values.astype(F32), axis=0, keepdims=True)

    def cross(k, source, target):
        copy = pltpu.make_async_remote_copy(source, target, cross_send.at[k], cross_recv.at[k], device_id=to["core"], device_id_type=MESH)
        copy.start()
        return copy

    hidden = hidden_h.shape[1]
    quarter = hidden // 4
    own = pl.ds(pl.multiple_of(core * own_rows, 128), own_rows)
    other = pl.ds(pl.multiple_of((1 - core) * own_rows, 128), own_rows)

    def shrink_gradient(tiles, d_branch_x, d_branch, shrink_w, slope):
        below((("d_branch_x", d_branch_x_h, d_branch_x),))
        ready = []
        for n in range(4):
            copy = pltpu.make_async_copy(hidden_h.at[:, pl.ds(n * quarter, quarter)], tiles.at[n % 2], in_sems.at[30 + n])
            ready.append(copy)
        ready[0].start()
        ready[1].start()
        below((("d_branch", d_branch_h, d_branch), ("shrink", shrink_h, shrink_w), ("slope", slope_h, slope)))
        need("d_branch_x")
        tall = shrink_grads.shape[3]
        for n in range(4):
            ready[n].wait()
            value = transposed(tiles[n % 2], d_branch_x[...]).astype(LOW)
            for b in range(quarter // tall):
                block = n * (quarter // tall) + b
                shrink_grads[block // 4, (block // 2) % 2, block % 2] = value[b * tall : (b + 1) * tall]
            if n + 2 < 4:
                ready[n + 2].start()
        need("d_branch", "shrink", "slope", "vectors")
        sent = []
        for k in range(4):
            if k % 2 == 0:
                turn("dha" if k == 0 else "dhb")
            which = 1 - core if k < 2 else core
            piece = which * 2 + k % 2
            columns = pl.ds(pl.multiple_of(piece * quarter, 128), quarter)
            here = pl.ds((k % 2) * quarter, quarter)
            value = against(d_branch[...], shrink_w[pl.ds(piece * (quarter // tall), quarter // tall)].reshape(quarter, width))
            value = (value * slope[:, columns].astype(F32)).astype(LOW)
            slope[:, columns] = value
            vec_sum[0, pl.ds(13 + piece, 1), :] = total_rows(value.astype(F32))
            if k < 2:
                sent.append(cross(3 + k, slope.at[:, columns], d_hidden_x.at[own, here]))
            else:
                d_hidden_x[own, here] = value
        for copy in sent:
            copy.wait()

    def expand_gradient(middle, expand_w, d_sum2, middle_sum, d_hidden):
        below((("middle", middle_h, middle), ("expand", expand_h, expand_w), ("d_sum2", d_sum2_h, d_sum2), ("middle_sum", middle_sum_h, middle_sum)))
        need("middle")

        def one(k, carry):
            value = transposed(middle[...], d_hidden_x[:, pl.ds(pl.multiple_of(k * wide, 128), wide)]).astype(LOW)
            for b in range(width // rows):
                expand_grads[k, b // 4, (b // 2) % 2, b % 2] = value[b * rows : (b + 1) * rows]
            return carry

        turn("de0")
        lax.fori_loop(0, 2, one, 0)
        turn("de1")
        lax.fori_loop(2, 4, one, 0)
        need("expand", "d_sum2", "middle_sum")
        vec_sum[0, 5:6] = jnp.zeros((1, width), F32)
        vec_sum[0, 7:8] = jnp.zeros((1, width), F32)
        vec_sum[0, 10:11] = jnp.zeros((1, width), F32)

        def two(t, carry):
            here = pl.ds(pl.multiple_of(t * 256, 256), 256)
            delta = d_sum2[here] + against(d_hidden[here], expand_w[...].reshape(width, hidden))
            unit, factor = norm_parts(middle_sum[here])
            vec_sum[0, 7:8] += total_rows(delta * unit)
            vec_sum[0, 10:11] += total_rows(delta)
            delta = norm_backward(unit, factor, table[7:8], delta)
            d_sum1[here] = delta
            low = delta.astype(LOW)
            d_unpacked[pl.ds(pl.multiple_of(core * own_rows + t * 256, 256), 256)] = low
            vec_sum[0, 5:6] += total_rows(low.astype(F32))
            return carry

        turn("dm0")
        lax.fori_loop(0, own_rows // 512, two, 0)
        turn("dm1")
        lax.fori_loop(own_rows // 512, own_rows // 256, two, 0)
        return cross(5, d_unpacked.at[own], d_unpacked.at[own])

    def feed_forward(slope):
        like = lambda ref: pltpu.VMEM(ref.shape, ref.dtype)
        pl.run_scoped(
            lambda *refs: shrink_gradient(*refs, slope),
            pltpu.VMEM((2, hidden_h.shape[0], quarter), LOW), like(d_branch_x_h), like(d_branch_h), like(shrink_h),
        )
        pl.run_scoped(
            lambda *refs: expand_gradient(*refs, slope).wait(),
            like(middle_h), like(expand_h), like(d_sum2_h), like(middle_sum_h),
        )

    pl.run_scoped(feed_forward, pltpu.VMEM(slope_h.shape, LOW))

    def attention(map_u, map_p, mixed_u, mixed_p, inputs, memory, qu, ku, vu, qp, kp, vp, probs, packed, d_sum0, weights,
                  d_mixed, d_query, d_key, d_value, d_token_key, d_token_value, d_packed):
        mine = pl.ds(pl.multiple_of(core * wide, 128), wide)
        below((
            ("map_u", maps_h.at[1, mine], map_u), ("mixed_u", mixed_u_h, mixed_u), ("qu", qu_h, qu), ("ku", ku_h, ku), ("vu", vu_h, vu), ("probs_u", probs_u_h, probs),
            ("inputs", inputs_h, inputs), ("packed", packed_h, packed), ("weights", proj_h, weights), ("d_sum0", d_sum0_h, d_sum0),
            ("map_p", maps_h.at[0, mine], map_p), ("mixed_p", mixed_p_h, mixed_p), ("qp", qp_h, qp), ("kp", kp_h, kp), ("vp", vp_h, vp), ("memory", memory_h, memory),
        ))
        need("map_u")

        def from_map_u(piece):
            d_mixed[piece] = against(d_unpacked[piece], map_u[...]).astype(LOW)

        turn("mix")
        over_rows(d_unpacked.shape[0], 512, from_map_u)
        need("mixed_u")
        turn("gm1")
        weight_grad(7, mixed_u, d_unpacked[:, span(core)])
        need("qu", "ku", "vu", "probs_u")
        for n in range(3):
            turn("ua" + str(n))
            attention_backward((n, n + 1), qu, ku, vu, probs, d_mixed, d_query, d_key, d_value, True)
        below((("probs_p", probs_p_h, probs),))
        need("inputs", "packed", "weights", "d_sum0")
        turn("pk")
        partial[...] = against(d_key[...], weights[4]) + against(d_value[...], weights[5])
        packing = cross(0, partial, partial_in)
        turn("g3")
        weight_grad(3, inputs, d_query[...])
        turn("g45")
        weight_grad(4, packed, d_key[...])
        weight_grad(5, packed, d_value[...])
        put_bias(3, d_query[...])
        put_bias(4, d_value[...])

        turn("gm0")
        packing.wait()
        d_packed[...] = (d_sum0[...] + (partial[...] + partial_in[...])).astype(LOW)
        need("map_p", "mixed_p")
        d_mixed_p = d_mixed.at[pl.ds(0, 2 * mem_rows)]
        d_mixed_p[...] = against(d_packed[...], map_p[...]).astype(LOW)
        weight_grad(6, mixed_p, d_packed[:, span(core)])
        vec_sum[0, 2:3, :] = total_rows(d_packed[pl.ds(pl.multiple_of(core * mem_rows, 128), mem_rows)].astype(F32))
        need("qp", "kp", "vp", "probs_p")
        for n in range(3):
            turn("pa" + str(n))
            attention_backward((n, n + 1), qp, kp, vp, probs, d_mixed_p, d_key, d_token_key, d_token_value, False)
        need("memory")
        turn("g0")
        weight_grad(0, memory, d_key[...])
        turn("g1")
        weight_grad(1, inputs, d_token_key[...])
        turn("g2")
        weight_grad(2, inputs, d_token_value[...])
        put_bias(0, d_key[...])
        put_bias(1, d_token_value[...])
        turn("tok0")
        own_mem = pl.ds(pl.multiple_of(core * mem_rows, 128), mem_rows)
        other_mem = pl.ds(pl.multiple_of((1 - core) * mem_rows, 128), mem_rows)
        rows_out[...] = against(d_key[...], weights[0])
        memory_terms = cross(2, rows_out.at[other_mem], rows_in)
        wide_out[...] = against(d_query[other], weights[3]) + against(d_token_key[other], weights[1]) + against(d_token_value[other], weights[2])
        token_terms = cross(1, wide_out, wide_in)
        turn("out0")
        tokens_o[...] = d_sum1[...] + against(d_query[own], weights[3])
        turn("out1")
        tokens_o[...] = tokens_o[...] + against(d_token_key[own], weights[1]) + against(d_token_value[own], weights[2])
        turn("fin")
        memory_terms.wait()
        memory_o[...] = d_sum0[own_mem] + rows_out[own_mem] + rows_in[...]
        token_terms.wait()
        tokens_o[...] = tokens_o[...] + wide_in[...]
        turn(None)
        for k in range(len(units)):
            close(k, False)
        for unit in units:
            unit.finish()

    like = lambda ref: pltpu.VMEM(ref.shape, ref.dtype)
    tokens, memories = like(qu_h), like(ku_h)
    pl.run_scoped(
        attention,
        pltpu.VMEM((wide, width), LOW), pltpu.VMEM((wide, width), LOW), like(mixed_u_h), like(mixed_p_h), like(inputs_h), like(memory_h),
        tokens, memories, memories, memories, tokens, tokens, like(probs_u_h), like(packed_h), like(d_sum0_h), like(proj_h),
        tokens, tokens, memories, memories, tokens, tokens, like(packed_h),
    )


def reduce_chips(far_count, table, vectors, arrays):
    hidden_full, slope, d_sum2, inputs, memory = arrays[0], arrays[3], arrays[7], arrays[11], arrays[12]
    proj = arrays[-2]
    rows, wide = proj.shape[1] // (4 * far_count), proj.shape[2]
    part, width, hidden = rows // 2, 2 * wide, hidden_full.shape[1]
    all_tokens, own_tokens, all_rows = inputs.shape[0], slope.shape[0], memory.shape[0]
    grid = (far_count, 2, 2)
    any_space = pl.BlockSpec(memory_space=pl.ANY)
    vmem = pl.BlockSpec(memory_space=pltpu.VMEM)
    shapes = ((6, part, width), (2, part, width), (part, hidden), (hidden // (8 * far_count), width), vectors.shape, d_sum2.shape, (all_rows // 2, width))
    return pl.pallas_call(
        functools.partial(reduce_kernel, far_count),
        out_shape=[jax.ShapeDtypeStruct(shape, F32) for shape in shapes],
        in_specs=[vmem] + [any_space] * (1 + len(arrays)),
        out_specs=[vmem] * 7,
        scratch_shapes=[
            pltpu.VMEM((16, 2, far_count, rows, wide), LOW),
            pltpu.VMEM((16, far_count, rows, wide), LOW),
            pltpu.VMEM((16, far_count - 1, rows, wide), LOW),
            pltpu.VMEM((4,) + vectors.shape, F32),
            pltpu.VMEM((2 + far_count,) + vectors.shape, F32),
            pltpu.VMEM((16, rows, wide), F32),
            pltpu.VMEM((8,) + grid + (rows, wide), LOW),
            pltpu.VMEM((4,) + grid + (rows, wide), LOW),
            pltpu.VMEM(grid + (hidden // (4 * far_count), wide), LOW),
            pltpu.VMEM((all_tokens, hidden // 2), LOW),
            pltpu.VMEM((all_tokens, width), LOW),
            pltpu.VMEM((own_tokens, width), F32),
            pltpu.VMEM((all_rows, width), F32),
            pltpu.VMEM((all_rows, width), F32),
            pltpu.VMEM((own_tokens, width), F32),
            pltpu.VMEM((own_tokens, width), F32),
            pltpu.VMEM((all_rows, width), F32),
            pltpu.VMEM((all_rows // 2, width), F32),
            pltpu.SemaphoreType.DMA((16, 6)),
            pltpu.SemaphoreType.DMA((16, 6)),
            pltpu.SemaphoreType.DMA((16,)),
            pltpu.SemaphoreType.DMA((16,)),
            pltpu.SemaphoreType.DMA((16,)),
            pltpu.SemaphoreType.DMA((34,)),
            pltpu.SemaphoreType.DMA((6,)),
            pltpu.SemaphoreType.DMA((6,)),
            pltpu.SemaphoreType.DMA((2 + far_count,)),
            pltpu.SemaphoreType.DMA((2 + far_count,)),
        ],
        compiler_params=pltpu.CompilerParams(
            collective_id=1, has_side_effects=True, vmem_limit_bytes=62 << 20
        ),
        name="backward_and_sums",
    )(table, vectors, *arrays)


def norm_apply(values, gain, shift):
    centre = values - jnp.mean(values, axis=-1, keepdims=True)
    spread = jnp.mean(centre * centre, axis=-1, keepdims=True)
    return centre * lax.rsqrt(spread + epsilon) * gain + shift


def gelu_exact(values):
    return jax.nn.gelu(values, approximate=False)


def heads_of(values):
    return values.reshape(values.shape[0], values.shape[1] // HEAD, HEAD)


def scores_of(queries, keys, valid):
    scores = jnp.einsum(
        "rhd,chd->hrc", heads_of(queries), heads_of(keys), preferred_element_type=F32
    ) * HEAD ** (-0.5)
    if valid is not None:
        scores = jnp.where(valid[None, None, :], scores, -1e30)
    return scores


def attend_forward(queries, keys, values, valid):
    scores = scores_of(queries, keys, valid)
    top = jnp.max(scores, axis=-1, keepdims=True)
    expon = jnp.exp(scores - top)
    total = jnp.sum(expon, axis=-1, keepdims=True)
    probs = to_low(expon / total)
    mixed = jnp.einsum("hrc,chd->rhd", probs, heads_of(values), preferred_element_type=F32)
    return to_low(mixed.reshape(queries.shape)), top + jnp.log(total), probs


def attend_backward(queries, keys, values, valid, log_total, delta_mixed):
    probs = jnp.exp(scores_of(queries, keys, valid) - log_total)
    delta_heads = heads_of(delta_mixed)
    delta_values = jnp.einsum("hrc,rhd->chd", to_low(probs), delta_heads, preferred_element_type=F32)
    delta_probs = jnp.einsum("rhd,chd->hrc", delta_heads, heads_of(values), preferred_element_type=F32)
    row_delta = jnp.sum(delta_probs * probs, axis=-1, keepdims=True)
    score_low = to_low(probs * (delta_probs - row_delta))
    scale = HEAD ** (-0.5)
    delta_query = jnp.einsum("hrc,chd->rhd", score_low, heads_of(keys), preferred_element_type=F32) * scale
    delta_keys = jnp.einsum("hrc,rhd->chd", score_low, heads_of(queries), preferred_element_type=F32) * scale
    return (
        to_low(delta_query.reshape(queries.shape)),
        to_low(delta_keys.reshape(keys.shape)),
        to_low(delta_values.reshape(keys.shape)),
    )


def body(
    custom,
    tokens,
    memory,
    lengths,
    tokens_cotangent,
    memory_cotangent,
    projections,
    output_maps,
    expand_weight,
    shrink_weight,
    projection_bias,
    norm_gain,
    norm_bias,
    expand_bias,
    shrink_bias,
):
    share = lax.axis_index("mem")
    chips = lax.axis_size("seq")
    width = tokens.shape[1]
    hidden = expand_weight.shape[1]
    part = projections.shape[1]
    rows = 2 * part

    def block(values, axis):
        low = to_low(values)
        wide = axis + 1
        return join(half(low, share, wide), swap(half(low, 1 - share, wide)), axis)

    own_count = tokens.shape[0]
    device = 2 * lax.axis_index("seq") + share
    if custom:
        (
            proj_all, maps_all, expand_mat, shrink_mat, table, hidden_full, middle_full, d_branch_x, inputs, rows_all, pack_query, pack_keys,
            pack_values, unpack_query, unpack_keys, unpack_values, pack_probs, unpack_probs, pack_mixed, unpack_mixed, packed_low, new_memory,
            middle_sum, slope, delta_sum2, delta_branch, new_tokens, delta_sum0, vectors,
        ) = gather_chips(
            chips // 4,
            (projections, output_maps, expand_weight, shrink_weight),
            (projection_bias, norm_gain, norm_bias, shrink_bias[None], expand_bias[None]),
            lengths[None], tokens, memory, tokens_cotangent, memory_cotangent,
        )
        proj_all = proj_all.reshape(6, width, width // 2)
        maps_all = maps_all.reshape(2, width, width)
        shrink_mat = shrink_mat.reshape(chips, hidden // chips, width)
        proj_o, maps_o, expand_o, shrink_o, vec_o, tokens_grad, memory_grad = reduce_chips(
            chips // 4,
            table,
            vectors,
            (
                hidden_full, d_branch_x, delta_branch, slope, expand_mat, shrink_mat, middle_full, delta_sum2, middle_sum,
                unpack_mixed, pack_mixed, inputs, rows_all, unpack_query, unpack_keys, unpack_values,
                pack_query, pack_keys, pack_values, unpack_probs, pack_probs, packed_low, delta_sum0, proj_all, maps_all,
            ),
        )
        small = lax.dynamic_slice(vec_o, (0, device * part), (13, part))
        count = hidden // (2 * chips)
        expand_small = lax.dynamic_slice(vec_o[13 : 13 + hidden // width].reshape(-1), (device * count,), (count,))
    else:
        vectors = [to_low(v).astype(F32) for v in (projection_bias, norm_gain, norm_bias, shrink_bias[None], expand_bias)]
        blocks = (block(projections, 1), block(output_maps, 1), block(expand_weight, 0), block(shrink_weight, 0))
        length = lengths[0]
        own_valid = share * own_count + jnp.arange(own_count) < length
        all_valid = jnp.arange(2 * own_count) < length
        gather = lambda values, axis: lax.all_gather(values, "seq", axis=axis, tiled=True)
        proj_all = gather(blocks[0], 1)
        maps_all = both(gather(blocks[1], 1), 2)
        expand_mat = both(gather(blocks[2], 0), 1)
        shrink_mat = both(gather(blocks[3], 0), 1)
        table = lax.all_gather(jnp.concatenate(vectors[:4]), AXES, axis=1, tiled=True)
        line = lax.all_gather(vectors[4], AXES, axis=0, tiled=True)
        table = jnp.concatenate([table, line.reshape(-1, width)])
        biases, gains, shifts, shrink_shift = table[0:6], table[6:9], table[9:12], table[12]
        expand_shift = table[13 : 13 + hidden // width].reshape(hidden)
        bias_half = half(biases, share, 1)
        inputs, rows_all, memory_cot = both(tokens), both(memory), both(memory_cotangent)
        pack_query = to_low(matmul(rows_all, proj_all[0]) + bias_half[0])
        pack_keys = to_low(matmul(inputs, proj_all[1]))
        pack_values = to_low(matmul(inputs, proj_all[2]) + bias_half[1])
        pack_own, pack_total, pack_probs = attend_forward(pack_query, pack_keys, pack_values, all_valid)
        pack_mixed = both(pack_own, 1)
        packed = matmul(pack_mixed, maps_all[0]) + biases[2]
        packed_low = to_low(packed)
        memory_sum = rows_all.astype(F32) + packed
        new_memory = norm_apply(half(memory_sum, share, 0), gains[0], shifts[0])
        unpack_keys = to_low(matmul(packed_low, proj_all[4]))
        unpack_values = to_low(matmul(packed_low, proj_all[5]) + bias_half[4])
        unpack_query = to_low(matmul(inputs, proj_all[3]) + bias_half[3])
        unpack_own, unpack_total, unpack_probs = attend_forward(unpack_query, unpack_keys, unpack_values, None)
        unpack_mixed = both(unpack_own, 1)
        middle_sum = tokens.astype(F32) + matmul(half(unpack_mixed, share, 0), maps_all[1]) + biases[5]
        middle = norm_apply(middle_sum, gains[1], shifts[1])
        middle_low = to_low(middle)
        hidden_in = matmul(middle_low, expand_mat) + expand_shift
        hidden_low = to_low(gelu_exact(hidden_in))
        output_sum = middle + matmul(hidden_low, shrink_mat) + shrink_shift
        layer_out = norm_apply(output_sum, gains[2], shifts[2])
        new_tokens = jnp.where(own_valid[:, None], layer_out, 0.0)

        delta_out = jnp.where(own_valid[:, None], tokens_cotangent.astype(F32), 0.0)
        dropped, norm_back = jax.vjp(norm_apply, output_sum, gains[2], shifts[2])
        delta_sum2, delta_gain2, delta_shift2 = norm_back(delta_out)
        delta_branch = to_low(delta_sum2)
        delta_hidden = matmul_right(delta_branch, shrink_mat)
        dropped, gelu_back = jax.vjp(gelu_exact, hidden_in)
        delta_hidden_in = to_low(gelu_back(delta_hidden)[0])
        delta_shrink = matmul_left(
            both(hidden_low), join(half(delta_branch, share, 1), swap(half(delta_branch, 1 - share, 1)))
        )
        delta_expand = matmul_left(
            both(middle_low), join(half(delta_hidden_in, share, 1), swap(half(delta_hidden_in, 1 - share, 1)))
        )
        delta_middle = delta_sum2 + matmul_right(delta_hidden_in, expand_mat)
        dropped, norm_back = jax.vjp(norm_apply, middle_sum, gains[1], shifts[1])
        delta_sum1, delta_gain1, delta_shift1 = norm_back(delta_middle)
        delta_own = to_low(delta_sum1)
        delta_unpacked = both(delta_own)
        dropped, norm_back = jax.vjp(norm_apply, memory_sum, gains[0], shifts[0])
        delta_sum0 = norm_back(memory_cot.astype(F32))[0]
        dropped, norm_back = jax.vjp(norm_apply, half(memory_sum, share, 0), gains[0], shifts[0])
        dropped, delta_gain0, delta_shift0 = norm_back(memory_cotangent.astype(F32))
        known = [delta_gain0, delta_gain1, delta_gain2, delta_shift0, delta_shift1, delta_shift2, column_sum(delta_branch)]
        delta_map1 = matmul_left(unpack_mixed, half(delta_unpacked, share, 1))
        delta_mixed = to_low(matmul_right(delta_unpacked, half(maps_all[1], share, 0)))
        delta_uquery, delta_ukeys, delta_uvalues = attend_backward(
            unpack_query, unpack_keys, unpack_values, None, unpack_total, delta_mixed
        )
        delta_proj3 = matmul_left(inputs, delta_uquery)
        delta_proj4 = matmul_left(packed_low, delta_ukeys)
        delta_proj5 = matmul_left(packed_low, delta_uvalues)
        partial = matmul_right(delta_ukeys, proj_all[4]) + matmul_right(delta_uvalues, proj_all[5])
        delta_packed = to_low(delta_sum0 + (partial + swap(partial)))
        delta_map0 = matmul_left(pack_mixed, half(delta_packed, share, 1))
        delta_mixed = to_low(matmul_right(delta_packed, half(maps_all[0], share, 0)))
        delta_pquery, delta_pkeys, delta_pvalues = attend_backward(
            pack_query, pack_keys, pack_values, all_valid, pack_total, delta_mixed
        )
        delta_proj0 = matmul_left(rows_all, delta_pquery)
        delta_proj1 = matmul_left(inputs, delta_pkeys)
        delta_proj2 = matmul_left(inputs, delta_pvalues)
        partial = matmul_right(delta_pquery, proj_all[0])
        memory_grad = half(delta_sum0, share, 0) + half(partial, share, 0) + swap(half(partial, 1 - share, 0))
        partial = (
            matmul_right(delta_uquery, proj_all[3])
            + matmul_right(delta_pkeys, proj_all[1])
            + matmul_right(delta_pvalues, proj_all[2])
        )
        tokens_grad = delta_sum1 + half(partial, share, 0) + swap(half(partial, 1 - share, 0))

        zero = jnp.zeros((1, width // 2), F32)

        def spread(values):
            return join(values, zero[0])

        bias_grads = [
            spread(column_sum(delta_pquery)),
            spread(column_sum(delta_pvalues)),
            column_sum(half(delta_packed, share, 0)),
            spread(column_sum(delta_uquery)),
            spread(column_sum(delta_uvalues)),
            column_sum(delta_own),
        ]
        vec_grads = jnp.stack(
            bias_grads + known
        )
        vec_grads = vec_grads.reshape(13, 2 * chips, part).transpose(1, 0, 2).reshape(2 * chips, 13 * part)
        vec_grads = jnp.concatenate([vec_grads, column_sum(delta_hidden_in).reshape(2 * chips, -1)], axis=1)
        vec_grads = jnp.pad(vec_grads, ((0, 0), (0, 1024 - vec_grads.shape[1])))
        reduce = lambda values, axis: lax.psum_scatter(values, "seq", scatter_dimension=axis, tiled=True)

        def finish(values, axis):
            return join(half(values, share, axis), swap(half(values, 1 - share, axis)), axis + 1)

        proj_o = finish(reduce(jnp.stack([delta_proj0, delta_proj1, delta_proj2, delta_proj3, delta_proj4, delta_proj5]), 1), 1)
        maps_o = finish(reduce(jnp.stack([delta_map0, delta_map1]), 1), 1)
        expand_o = finish(reduce(delta_expand, 0), 0)
        shrink_o = finish(reduce(delta_shrink, 0), 0)
        vec_o = lax.psum_scatter(vec_grads, AXES, scatter_dimension=0, tiled=True).reshape(-1)
        small = vec_o[: 13 * part].reshape(13, part)
        expand_small = vec_o[13 * part : 13 * part + hidden // (2 * chips)]
    return (
        new_tokens,
        new_memory,
        tokens_grad,
        memory_grad,
        proj_o,
        maps_o,
        expand_o,
        shrink_o,
        small[0:6],
        small[6:9],
        small[9:12],
        expand_small,
        small[12],
    )


def solution(mesh):
    rows, stacked = P(AXES, None), P(None, AXES, None)
    table, line = P(None, AXES), P(AXES)
    custom = mesh.shape["seq"] == 16 and mesh.shape["mem"] == 2
    return jax.shard_map(
        functools.partial(body, custom),
        mesh=mesh,
        in_specs=(rows, rows, P("seq"), rows, rows, stacked, stacked, rows, rows, table, table, table, line, line),
        out_specs=(rows, rows, rows, rows, stacked, stacked, rows, rows, table, table, table, line, line),
        check_vma=False,
    )
```

```python
import functools

import jax
import jax.numpy as jnp
from jax import lax
from jax.experimental import pallas as pl
from jax.experimental.pallas import tpu as pltpu
from jax.sharding import PartitionSpec as P

HEAD = 64
epsilon = 1e-05
MESH = pl.DeviceIdType.MESH
LOW = jnp.bfloat16
F32 = jnp.float32
AXES = ("seq", "mem")


def matmul(left, right):
    return jnp.dot(left, right, preferred_element_type=F32)


def matmul_left(left, right):
    return lax.dot_general(left, right, (((0,), (0,)), ((), ())), preferred_element_type=F32)


def matmul_right(left, right):
    return lax.dot_general(left, right, (((1,), (1,)), ((), ())), preferred_element_type=F32)


def to_low(values):
    return values.astype(LOW)


def column_sum(values):
    return jnp.sum(values.astype(F32), axis=0)


def swap(values):
    return lax.ppermute(values, "mem", [(0, 1), (1, 0)])


def join(own, other, axis=0):
    first = lax.axis_index("mem") == 0
    return jnp.where(
        first, jnp.concatenate([own, other], axis), jnp.concatenate([other, own], axis)
    )


def both(values, axis=0):
    return join(values, swap(values), axis)


def half(values, index, axis):
    size = values.shape[axis] // 2
    return lax.dynamic_slice_in_dim(values, index * size, size, axis)


FORWARD = (
    (0, 0), (15, 0), (16, 0), (0, 1), (15, 1), (1, 0), (16, 1), (0, 2), (0, 3), (2, 0), (1, 1), (3, 0), (2, 1),
    (1, 2), "q", (3, 1), (4, 0), (2, 2), "k", (5, 0), (3, 2), "v", "pf0", (4, 1), (6, 0), "pf1", (5, 1), "pf2", "cx",
    (7, 0), (4, 2), (6, 1), (4, 3), "yp", (5, 2), (8, 0), "ln0", (7, 1), (9, 0), (6, 2), "ku", (8, 1), (10, 0),
    (7, 2), "qu", "uf0", (9, 1), (11, 0), "uf1", "uf2", (8, 2), (10, 1), (12, 0), "ux", (8, 3), (9, 2), "att",
    (9, 3), (11, 1), (13, 0), (10, 2), (12, 1), (14, 0), (10, 3), "w0", "w2", (11, 2), (13, 1), (11, 3), (12, 2),
    (14, 1), (12, 3), "w1", "w3", (13, 2), (14, 2), (13, 3), (14, 3), (15, 2), (15, 3), (16, 2), (16, 3), "nar",
)
BACKWARD = (
    (0, 0), (1, 0), "dha", "dhb", (2, 0), (3, 0), "de0", (0, 1), (1, 1), "de1", (0, 2), (1, 2), "dm0", (2, 1),
    (3, 1), "dm1", (2, 2), (3, 2), (4, 0), (5, 0), "mix", (1, 3), (0, 3), "gm1", "ua0", (2, 3), (3, 3), "ua1",
    (6, 0), (7, 0), (4, 1), (5, 1), "ua2", (1, 4), "pk", (4, 2), (5, 2), "g3", (0, 4), "g45", (6, 1), (7, 1), "gm0",
    (2, 4), (6, 2), (7, 2), "pa0", (8, 0), (5, 3), (4, 3), (9, 0), "pa1", (3, 4), "pa2", (6, 3), (7, 3), (10, 0),
    (11, 0), "g0", (8, 1), (9, 1), (5, 4), "g12", (8, 2), (9, 2), (16, 0), "tok0", (4, 4), (16, 1), "out0", (10, 1),
    (11, 1), "out1", "fin", (6, 4), (10, 2), (11, 2), (12, 0), (9, 3), (8, 3), (13, 0), (7, 4), (16, 2), (11, 3),
    (10, 3), (9, 4), (14, 0), (12, 1), (13, 1), (12, 2), (8, 4), (15, 0), (16, 3), (13, 2), (14, 1), (12, 3),
    (11, 4), (14, 2), (15, 1), (10, 4), (13, 3), (15, 2), (15, 3), (14, 3), (16, 4), (12, 4), (13, 4), (15, 4),
    (14, 4),
)


def place(seq):
    return lax.div(seq, 4), lax.rem(lax.div(seq, 2), 2), lax.rem(seq, 2)


def peers(seq, core, far_count):
    far, row, column = place(seq)
    flat = lambda f, r, c: f * 4 + r * 2 + c
    far_peers = [lax.rem(far + k, far_count) for k in range(1, far_count)]
    return {
        "far": [(flat(f, row, column), core) for f in far_peers],
        "far_index": far_peers,
        "column": (flat(far, row, 1 - column), core),
        "row": (flat(far, 1 - row, column), core),
        "core": (seq, 1 - core),
    }


def greet(targets):
    barrier = pltpu.get_barrier_semaphore()
    for target in targets:
        pl.semaphore_signal(barrier, inc=1, device_id=target, device_id_type=MESH)
    pl.semaphore_wait(barrier, len(targets))


class Gather:
    def __init__(self, where, to, first, own, at, shared, sems):
        self.where, self.to, self.own, self.at, self.shared = where, to, own, at, shared
        self.first, self.second = first, ("row" if first == "column" else "column")
        self.send, self.recv = sems
        self.started = []

    def _column(self, near):
        far, row, column = self.where
        row, column = (
            (1 - row if "row" in near else row),
            (1 - column if "column" in near else column),
        )
        return self.at(slice(None), row, column)

    def _copy(self, source, target, k, device):
        return pltpu.make_async_remote_copy(
            source, target, self.send.at[k], self.recv.at[k], device_id=device, device_id_type=MESH
        )

    def _go(self, *args):
        copy = self._copy(*args)
        copy.start()
        self.started.append(copy)

    def _arrived(self, ref, k):
        self._copy(ref, ref, k, self.to["core"]).wait_recv()

    def start(self):
        far, row, column = self.where
        mine = self.at(far, row, column)
        for k, device in enumerate(self.to["far"]):
            self._go(self.own, mine, k, device)

    def step(self, stage):
        far, row, column = self.where
        near = self._column(())
        if stage == 0:
            count = len(self.to["far"])
            for k in range(count):
                sender = self.to["far_index"][count - 1 - k]
                self._arrived(self.at(sender, row, column), k)
            self._go(near, near, 3, self.to[self.first])
            self._go(near, near, 4, self.to[self.second])
            if self.shared:
                self._go(near, near, 6, self.to["core"])
        if stage == 1:
            got = self._column((self.first,))
            self._arrived(got, 3)
            self._go(got, got, 5, self.to[self.second])
            if self.shared:
                self._go(got, got, 7, self.to["core"])
        if stage == 2:
            for k, names in ((4, (self.second,)), (5, (self.first, self.second))):
                got = self._column(names)
                self._arrived(got, k)
                if self.shared:
                    self._go(got, got, 4 + k, self.to["core"])
        if stage == 3 and self.shared:
            for k, names in enumerate(
                ((), (self.first,), (self.second,), (self.first, self.second))
            ):
                self._arrived(self._other(names), 6 + k)

    def _other(self, names):
        keep, self.at = self.at, self.shared
        ref = self._column(names)
        self.at = keep
        return ref

    def finish(self):
        for copy in self.started:
            copy.wait_send()


class GatherNear(Gather):
    def start(self):
        far, row, column = self.where
        mine = self.at(far, row, column)
        self._go(self.own, mine, 0, self.to[self.first])
        self._go(self.own, mine, 1, self.to[self.second])

    def _near(self, names):
        far, row, column = self.where
        return self.at(
            far, 1 - row if "row" in names else row, 1 - column if "column" in names else column
        )

    def step(self, stage):
        far = self.where[0]
        all_of = slice(None)
        count = len(self.to["far"])
        if stage == 0:
            got = self._near((self.first,))
            self._arrived(got, 0)
            self._go(got, got, 2, self.to[self.second])
        if stage == 1:
            self._arrived(self._near((self.second,)), 1)
            self._arrived(self._near((self.first, self.second)), 2)
            plane = self.at(far, all_of, all_of)
            for k, device in enumerate(self.to["far"]):
                self._go(plane, plane, 3 + k, device)
            if self.shared:
                self._go(plane, plane, 3 + count, self.to["core"])
        if stage == 2:
            for k in range(count):
                plane = self.at(self.to["far_index"][count - 1 - k], all_of, all_of)
                self._arrived(plane, 3 + k)
                if self.shared:
                    self._go(plane, plane, 4 + count + k, self.to["core"])
        if stage == 3 and self.shared:
            self._arrived(self.shared(far, all_of, all_of), 3 + count)
            for k in range(count):
                plane = self.shared(self.to["far_index"][count - 1 - k], all_of, all_of)
                self._arrived(plane, 4 + count + k)


def transposed(left, right):
    return lax.dot_general(left, right, (((0,), (0,)), ((), ())), preferred_element_type=F32)


def against(left, right):
    return lax.dot_general(left, right, (((1,), (1,)), ((), ())), preferred_element_type=F32)


def plain(left, right):
    return lax.dot_general(left, right, (((1,), (0,)), ((), ())), preferred_element_type=F32)


def over_rows(count, tile, work):
    def one(t, carry):
        work(pl.ds(pl.multiple_of(t * tile, tile), tile))
        return carry

    lax.fori_loop(0, count // tile, one, 0)


class Vectors:
    def __init__(self, to, held, arrived, send, recv, order):
        self.to, self.held, self.arrived, self.sems, self.order = to, held, arrived, (send, recv), order
        self.flying, self.slot = [], 0

    def _go(self, k):
        name = self.order[k]
        for device in self.to["far"] if name == "far" else [self.to[name]]:
            slot = self.slot
            copy = pltpu.make_async_remote_copy(
                self.held.at[k], self.arrived.at[slot], self.sems[0].at[slot], self.sems[1].at[slot],
                device_id=device, device_id_type=MESH,
            )
            copy.start()
            self.flying.append((slot, copy))
            self.slot += 1

    def _take(self, k):
        value = self.held[k]
        for slot, copy in self.flying:
            copy.wait()
            value = value + self.arrived[slot]
        self.flying = []
        return value

    def start(self):
        self._go(0)

    def step(self, k):
        self.held[k] = self._take(k - 1)
        self._go(k)

    def result(self):
        return self._take(3)


def attention_forward(pairs, queries, keys, values, valid, probs, mixed, first_lane, turned):
    for pair in range(*pairs):
        lanes = slice(pair * 128, pair * 128 + 128)
        query, key, value = queries[:, lanes] * LOW(HEAD ** (-0.5)), keys[:, lanes], values[:, lanes]
        outs = []
        for j in range(2):
            part = slice(j * HEAD, (j + 1) * HEAD)
            scores = against(key[:, part], query[:, part]) if turned else against(query[:, part], key[:, part])
            if valid is not None:
                scores = jnp.where(lax.broadcasted_iota(jnp.int32, scores.shape, 1) < valid[0, 0], scores, -1e30)
            axis = 0 if turned else 1
            expon = jnp.exp(scores - jnp.max(scores, axis=axis, keepdims=True))
            prob = (expon * (1.0 / jnp.sum(expon, axis=axis, keepdims=True))).astype(LOW)
            probs[pair * 2 + j] = prob
            outs.append((transposed if turned else plain)(prob, value[:, part]))
        mixed[:, pl.ds(pl.multiple_of(first_lane + pair * 128, 128), 128)] = jnp.concatenate(outs, axis=1).astype(LOW)


def norm_parts(values):
    centre = values - jnp.mean(values, axis=-1, keepdims=True)
    factor = lax.rsqrt(jnp.mean(centre * centre, axis=-1, keepdims=True) + epsilon)
    return centre * factor, factor


def norm_backward(unit, factor, gain, delta):
    scaled = delta * gain
    return factor * (scaled - jnp.mean(scaled, axis=-1, keepdims=True) - unit * jnp.mean(scaled * unit, axis=-1, keepdims=True))


def total_rows(values):
    return jnp.sum(values, axis=0, keepdims=True)


def gather_kernel(far_count, proj_in, maps_in, expand_in, shrink_in, bias_in, gain_in, shift_in, shrink_bias_in, expand_bias_in, length,
                  tokens, rows_in, token_cot_in, memory_cot,
                  proj_o, maps_o, expand_o, shrink_o, table_o, hidden_o, middle_full_o, d_branch_x_o,
                  inputs_o, memory_o, qp_o, kp_o, vp_o, qu_o, ku_o, vu_o,
                  probs_p_o, probs_u_o, mixed_p_o, mixed_u_o, packed_o, new_memory_o, middle_sum_o,
                  slope_o, d_sum2_o, d_branch_o, new_tokens_o, d_sum0_o, grad_table_o,
                  inputs, memory, qp, kp, vp, qu, ku, vu, probs_p, probs_u, mixed_p, mixed_u, packed, new_memory, middle_sum,
                  slope, d_sum2, d_branch, new_tokens, d_sum0, grad_table,
                  memory_sum, middle, middle_low, hidden, cot, expand_w, shrink_w,
                  weights, map_p, map_u, token_cot, table, own_vec, vec, vec_all,
                  proj_f, maps_f, expand_f, shrink_f, proj, maps, expand, shrink,
                  send, recv, local, out_sems, cross_send, cross_recv, raw_local, raw_send, raw_recv):
    seq, core = lax.axis_index("seq"), lax.axis_index("mem")
    where = place(seq)
    far, row, column = where
    to = peers(seq, core, far_count)
    wide = maps.shape[-1]
    width = 2 * wide
    own_tokens, own_rows = tokens.shape[0], rows_in.shape[0]

    def cols(which, start=0):
        return pl.ds(pl.multiple_of(which * expand.shape[-1] + start, 128), wide)

    def span(which):
        return pl.ds(pl.multiple_of(which * wide, 128), wide)

    copies, stores = [], []

    def keep(source, target):
        copy = pltpu.make_async_copy(source, target, local.at[len(copies)])
        copy.start()
        copies.append(copy)
        return copy

    def store(source, target):
        copy = pltpu.make_async_copy(source, target, out_sems.at[len(stores)])
        copy.start()
        stores.append(copy)

    own_t = pl.ds(pl.multiple_of(core * own_tokens, 128), own_tokens)
    own_m = pl.ds(pl.multiple_of(core * own_rows, 128), own_rows)
    raw = []
    for n, (source, target) in enumerate(((proj_in, proj_f), (maps_in, maps_f), (expand_in, expand_f), (shrink_in, shrink_f))):
        count, size = source.shape[-2], source.shape[-1] // 2
        place_rows = pl.ds(pl.multiple_of(core * count, 8), count)
        mine, theirs = (pl.ds(pl.multiple_of(which * size, 128), size) for which in (core, 1 - core))
        lead = (slice(None),) * (len(source.shape) - 2)
        raw.append((n, source.at[lead + (slice(None), mine)], source.at[lead + (slice(None), theirs)], target.at[lead + (place_rows,)]))
    for n, own, other, target in raw:
        pltpu.make_async_copy(own, target, raw_local.at[n]).start()
    keep(tokens, inputs.at[own_t])
    keep(rows_in, memory.at[own_m])
    keep(memory_cot, cot.at[own_m])
    keep(token_cot_in, token_cot)
    device = 2 * seq + core
    own_vec[...] = jnp.zeros_like(own_vec)
    for first_row, source in ((0, bias_in), (6, gain_in), (9, shift_in), (12, shrink_bias_in), (16, expand_bias_in)):
        own_vec[first_row : first_row + source.shape[0], 0 : source.shape[1]] = source[...]
    small, large = bias_in.shape[1], expand_bias_in.shape[1]

    def window(start):
        return lax.min(lax.div(start, 128), 2 * wide // 128 - 2)

    offsets = (small * device, lax.rem(large * device, 2 * wide))
    moved = [pltpu.roll(own_vec[k : k + 16 - k // 2], offsets[n] - 128 * window(offsets[n]), 1) for n, k in enumerate((0, 16))]
    vec[...] = jnp.concatenate([moved[0], moved[1], jnp.zeros_like(moved[1])], axis=0).astype(LOW)

    units = []

    def add(first, own, at, shared, kind=Gather):
        k = len(units)
        units.append(kind(where, to, first, own, at, shared, (send.at[k], recv.at[k])))

    def add_proj(first, p):
        add(first, proj.at[p], lambda f, r, c: proj_o.at[p, f, r, c], None)

    def add_map(first, p):
        add(first, maps.at[p], lambda f, r, c: maps_o.at[p, f, r, c, :, span(core)],
            lambda f, r, c: maps_o.at[p, f, r, c, :, span(1 - core)])

    def add_expand(first, k):
        add(first, expand.at[:, pl.ds(k * wide, wide)], lambda f, r, c: expand_o.at[f, r, c, :, cols(core, k * wide)],
            lambda f, r, c: expand_o.at[f, r, c, :, cols(1 - core, k * wide)])

    def add_shrink(first, k):
        rows = shrink.shape[0] // 4
        part = pl.ds(k * rows, rows)
        add(first, shrink.at[part], lambda f, r, c: shrink_o.at[f, r, c, part, span(core)],
            lambda f, r, c: shrink_o.at[f, r, c, part, span(1 - core)], GatherNear if k >= 2 else Gather)

    add("column", vec, lambda f, r, c: vec_all.at[core, f, r, c], lambda f, r, c: vec_all.at[1 - core, f, r, c])
    for first, second in (
        ((add_proj, 0), (add_proj, 1)), ((add_proj, 2), (add_map, 0)), ((add_proj, 4), (add_proj, 5)), ((add_proj, 3), (add_map, 1)),
        ((add_expand, 0), (add_expand, 1)), ((add_expand, 2), (add_expand, 3)), ((add_shrink, 0), (add_shrink, 1)), ((add_shrink, 2), (add_shrink, 3)),
    ):
        first[0]("column", first[1])
        second[0]("row", second[1])

    def cross(k, source, target):
        copy = pltpu.make_async_remote_copy(source, target, cross_send.at[k], cross_recv.at[k], device_id=to["core"], device_id_type=MESH)
        copy.start()
        return copy

    greet(to["far"] + [to["column"], to["row"], to["core"]])
    for n, own, other, target in raw:
        pltpu.make_async_remote_copy(other, target, raw_send.at[n], raw_recv.at[n], device_id=to["core"], device_id_type=MESH).start()
    crossed = [cross(0, tokens, inputs.at[own_t]), cross(1, rows_in, memory.at[own_m]), cross(4, memory_cot, cot.at[own_m])]
    keep(vec, vec_all.at[core, far, row, column])
    units[0].start()
    targets = (
        (proj_f, proj, proj_o.at[:, far, row, column]),
        (maps_f, maps, maps_o.at[:, far, row, column, :, span(core)]),
        (expand_f, expand, expand_o.at[far, row, column, :, pl.ds(pl.multiple_of(core * expand.shape[-1], 128), expand.shape[-1])]),
        (shrink_f, shrink, shrink_o.at[far, row, column, :, span(core)]),
    )
    groups = ((1, 2, 3), (4, 5, 6, 7, 8), (9, 10, 11, 12), (13, 14, 15, 16))
    for (n, own, other, target), (wide_block, block, place_of), group in zip(raw, targets, groups):
        pltpu.make_async_copy(own, target, raw_local.at[n]).wait()
        pltpu.make_async_remote_copy(other, target, raw_send.at[n], raw_recv.at[n], device_id=to["core"], device_id_type=MESH).wait()
        block[...] = wide_block[...].astype(LOW)
        keep(block, place_of)
        for index in group:
            units[index].start()
    for copy in copies:
        copy.wait()
    fetched = {}

    def fetch(key, source, target):
        copy = pltpu.make_async_copy(source, target, local.at[len(copies) + sum(len(v) for v in fetched.values())])
        copy.start()
        fetched.setdefault(key, []).append(copy)

    def need(*keys):
        for key in keys:
            for copy in fetched[key]:
                copy.wait()

    tall = width
    names = ("vec", "p0", "p1", "p2", "m0", "p4", "p5", "p3", "m1", "e0", "e1", "e2", "e3", "s0", "s1", "s2", "s3")

    def complete(name):
        k = int(name[1]) if name != "vec" else 0
        if name[0] == "p":
            fetch(name, proj_o.at[k], weights.at[k])
        elif name[0] == "m":
            fetch(name, maps_o.at[k], (map_p, map_u)[k])
        elif name[0] == "e":
            for side in range(2):
                columns = pl.ds(side * expand.shape[-1] + k * wide, wide)
                fetch(name, expand_o.at[:, :, :, :, columns], expand_w.at[:, :, :, :, columns])
        elif name[0] == "s":
            rows = shrink.shape[0] // 4
            part = pl.ds(k * rows, rows)
            fetch(name, shrink_o.at[:, :, :, part], shrink_w.at[:, :, :, part])

    def weight(p):
        return weights[p].reshape(-1, wide)

    def project(p, source, target, bias):
        need("p" + str(p))

        def one(piece):
            value = plain(source[piece], weight(p))
            if bias is not None:
                value = value + table[bias : bias + 1, span(core)]
            target[piece] = value.astype(LOW)

        one(slice(None))

    def gain(k):
        return table[6 + k : 7 + k]

    def shift(k):
        return table[9 + k : 10 + k]

    def from_other(k, ref):
        copy = pltpu.make_async_remote_copy(ref, ref, cross_send.at[k], cross_recv.at[k], device_id=to["core"], device_id_type=MESH)
        copy.wait_send()
        copy.wait_recv()

    def make_k():
        crossed[0].wait()
        project(1, inputs, kp, None)
        store(inputs, inputs_o)

    def make_q():
        table[...] = jnp.zeros_like(table)
        for k in range(8 * far_count):
            block = vec_all[k % 2, k // 8, (k // 4) % 2, (k // 2) % 2].astype(F32)
            for count, row, start in ((13, 0, small * k), (1, 13 + large * k // width, (large * k) % width)):
                first = 128 * min(start // 128, width // 128 - 2)
                from_row = 0 if count == 13 else 16
                table[row : row + count, first : first + 256] += block[from_row : from_row + count]
        store(table, table_o)
        crossed[1].wait()
        project(0, memory, qp, 0)
        store(memory, memory_o)

    def make_packed():
        from_other(2, mixed_p.at[:, span(core)])
        need("m0")
        for source, target in ((qp, qp_o), (kp, kp_o), (vp, vp_o), (probs_p, probs_p_o), (mixed_p, mixed_p_o)):
            store(source, target)
        value = plain(mixed_p[...], map_p[...].reshape(-1, width)) + table[2:3]
        packed[...] = value.astype(LOW)
        memory_sum[...] = memory[...].astype(F32) + value

    def make_memory():
        crossed[2].wait()
        unit, factor = norm_parts(memory_sum[...])
        memory_sum[...] = unit
        d_sum0[...] = norm_backward(unit, factor, gain(0), cot[...].astype(F32))
        unit, delta = memory_sum[own_m], cot[own_m].astype(F32)
        new_memory[...] = unit * gain(0) + shift(0)
        grad_table[...] = jnp.zeros_like(grad_table)
        grad_table[6:7] = total_rows(delta * unit)
        grad_table[9:10] = total_rows(delta)
        for source, target in ((packed, packed_o), (d_sum0, d_sum0_o), (new_memory, new_memory_o)):
            store(source, target)

    def make_unpack():
        project(4, packed, ku, None)
        project(5, packed, vu, 4)
        store(ku, ku_o)
        store(vu, vu_o)

    sent = []

    def make_middle():
        from_other(3, mixed_u.at[:, span(core)])
        need("m1")
        for source, target in ((qu, qu_o), (probs_u, probs_u_o), (mixed_u, mixed_u_o)):
            store(source, target)

        def attended(t, carry):
            here = pl.ds(pl.multiple_of(t * 256, 256), 256)
            there = pl.ds(pl.multiple_of(core * own_tokens + t * 256, 256), 256)
            value = plain(mixed_u[there], map_u[...].reshape(-1, width)) + table[5:6]
            value = inputs[there].astype(F32) + value
            middle_sum[here] = value
            value = norm_parts(value)[0] * gain(1) + shift(1)
            middle[here] = value
            middle_low[here] = value.astype(LOW)
            return carry

        lax.fori_loop(0, own_tokens // 256, attended, 0)
        store(middle_sum, middle_sum_o)
        store(middle_low, middle_full_o.at[own_t])
        sent.append(cross(5, middle_low, middle_full_o.at[own_t]))

    def widen(n):
        columns = pl.ds(n * tall, tall)
        if n < 2:
            need("e" + str(2 * n), "e" + str(2 * n + 1))
        value = plain(middle_low[...], expand_w[:, :, :, :, columns].reshape(-1, tall)) + table[13 + n : 14 + n]
        share = 0.5 + 0.5 * lax.erf(value * 0.5**0.5)
        hidden[:, columns] = (value * share).astype(LOW)
        slope[:, columns] = (share + value * (0.3989422804014327 * jnp.exp(-0.5 * value * value))).astype(LOW)
        store(hidden.at[:, columns], hidden_o.at[own_t, columns])
        store(slope.at[:, columns], slope_o.at[:, columns])
        sent.append(cross(6 + n, hidden.at[:, columns], hidden_o.at[own_t, columns]))

    def narrow(t, carry):
        here = pl.ds(pl.multiple_of(t * 256, 256), 256)
        value = middle[here] + (plain(hidden[here], shrink_w[...].reshape(-1, width)) + table[12:13])
        unit, factor = norm_parts(value)
        live = core * own_tokens + t * 256 + lax.broadcasted_iota(jnp.int32, (256, 1), 0) < length[0, 0]
        new_tokens[here] = jnp.where(live, unit * gain(2) + shift(2), 0.0)
        delta = jnp.where(live, token_cot[here].astype(F32), 0.0)
        grad_table[8:9] += total_rows(delta * unit)
        grad_table[11:12] += total_rows(delta)
        value = norm_backward(unit, factor, gain(2), delta)
        d_sum2[here] = value
        value = value.astype(LOW)
        d_branch[here] = value
        grad_table[12:13] += total_rows(value.astype(F32))
        return carry

    def make_tokens():
        need("s0", "s1", "s2", "s3")
        lax.fori_loop(0, own_tokens // 256, narrow, 0)
        sent.append(cross(10, d_branch.at[:, span(1 - core)], d_branch_x_o.at[own_t]))
        store(d_branch.at[:, span(core)], d_branch_x_o.at[own_t])
        for source, target in ((d_sum2, d_sum2_o), (d_branch, d_branch_o), (new_tokens, new_tokens_o), (grad_table, grad_table_o)):
            store(source, target)

    work = {
        "k": make_k,
        "q": make_q,
        "v": lambda: project(2, inputs, vp, 1),
        "cx": lambda: cross(2, mixed_p.at[:, span(core)], mixed_p.at[:, span(core)]),
        "yp": make_packed,
        "ln0": make_memory,
        "ku": make_unpack,
        "qu": lambda: project(3, inputs, qu, 3),
        "ux": lambda: cross(3, mixed_u.at[:, span(core)], mixed_u.at[:, span(core)]),
        "att": make_middle,
        "nar": make_tokens,
    }
    for n in range(3):
        work["pf" + str(n)] = functools.partial(attention_forward, (n, n + 1), qp, kp, vp, length, probs_p, mixed_p, core * wide, False)
        work["uf" + str(n)] = functools.partial(attention_forward, (n, n + 1), qu, ku, vu, None, probs_u, mixed_u, core * wide, True)
    for n in range(4):
        work["w" + str(n)] = functools.partial(widen, n)
    for item in FORWARD:
        if isinstance(item, str):
            work[item]()
            continue
        index, stage = item
        units[index].step(stage)
        if stage == (3 if units[index].shared else 2):
            complete(names[index])
    for copy in sent:
        copy.wait()
    for copy in stores:
        copy.wait()
    for unit in units:
        unit.finish()


def gather_chips(far_count, weights, vectors, length, tokens, memory, token_cot, memory_cot):
    grid = (far_count, 2, 2)
    width, hidden = weights[0].shape[-1], weights[2].shape[-1]
    rows, wide = 2 * weights[0].shape[1], width // 2
    blocks = ((6, rows, wide), (2, rows, wide), (rows, hidden // 2), (2 * weights[3].shape[0], wide))
    table = (24, width)
    own_tokens, own_rows = tokens.shape[0], memory.shape[0]
    all_tokens, all_rows = 2 * own_tokens, 2 * own_rows
    count = wide // HEAD
    passed = (
        ((6,) + grid + (rows, wide), LOW),
        ((2,) + grid + (rows, width), LOW),
        (grid + (rows, hidden), LOW),
        (grid + (blocks[3][0], width), LOW),
        (table, F32),
        ((all_tokens, hidden), LOW),
        ((all_tokens, width), LOW),
        ((all_tokens, wide), LOW),
    )
    kept = (
        ((all_tokens, width), LOW),
        ((all_rows, width), LOW),
        ((all_rows, wide), LOW),
        ((all_tokens, wide), LOW),
        ((all_tokens, wide), LOW),
        ((all_tokens, wide), LOW),
        ((all_rows, wide), LOW),
        ((all_rows, wide), LOW),
        ((count, all_rows, all_tokens), LOW),
        ((count, all_rows, all_tokens), LOW),
        ((all_rows, width), LOW),
        ((all_tokens, width), LOW),
        ((all_rows, width), LOW),
        ((own_rows, width), F32),
        ((own_tokens, width), F32),
        ((own_tokens, hidden), LOW),
        ((own_tokens, width), F32),
        ((own_tokens, width), LOW),
        ((own_tokens, width), F32),
        ((all_rows, width), F32),
        (table, F32),
    )
    inner = (
        ((all_rows, width), F32),
        ((own_tokens, width), F32),
        ((own_tokens, width), LOW),
        ((own_tokens, hidden), LOW),
        ((all_rows, width), LOW),
        passed[2],
        passed[3],
        passed[0],
        (passed[1][0][1:], LOW),
        (passed[1][0][1:], LOW),
        ((own_tokens, width), LOW),
        (table, F32),
        ((24, 256), F32),
        ((32, 256), LOW),
        ((2,) + grid + (32, 256), LOW),
    ) + tuple((block, F32) for block in blocks) + tuple((block, LOW) for block in blocks)
    any_space = pl.BlockSpec(memory_space=pl.ANY)
    return pl.pallas_call(
        functools.partial(gather_kernel, far_count),
        out_shape=[jax.ShapeDtypeStruct(*entry) for entry in passed + kept],
        in_specs=[any_space] * 4
        + [pl.BlockSpec(memory_space=pltpu.VMEM)] * 5
        + [pl.BlockSpec(memory_space=pltpu.SMEM)]
        + [any_space] * 4,
        out_specs=[any_space] * (len(passed) + len(kept)),
        scratch_shapes=[pltpu.VMEM(*entry) for entry in kept + inner]
        + [
            pltpu.SemaphoreType.DMA((17, 10)),
            pltpu.SemaphoreType.DMA((17, 10)),
            pltpu.SemaphoreType.DMA((29,)),
            pltpu.SemaphoreType.DMA((36,)),
            pltpu.SemaphoreType.DMA((11,)),
            pltpu.SemaphoreType.DMA((11,)),
            pltpu.SemaphoreType.DMA((4,)),
            pltpu.SemaphoreType.DMA((4,)),
            pltpu.SemaphoreType.DMA((4,)),
        ],
        compiler_params=pltpu.CompilerParams(
            collective_id=0, has_side_effects=True, vmem_limit_bytes=62 << 20
        ),
        name="gather_and_forward",
    )(*weights, *vectors, length, tokens, memory, token_cot, memory_cot)


class Reduce:
    def __init__(self, where, to, first, at, half_in, quarter_in, far_in, sems):
        self.where, self.to, self.at = where, to, at
        self.half_in, self.quarter_in, self.far_in = half_in, quarter_in, far_in
        self.first, self.second = first, ("row" if first == "column" else "column")
        self.send, self.recv = sems

    def _copy(self, source, target, k, device):
        return pltpu.make_async_remote_copy(
            source, target, self.send.at[k], self.recv.at[k], device_id=device, device_id_type=MESH
        )

    def _go(self, *args):
        self._copy(*args).start()

    def _arrived(self, ref, k):
        self._copy(ref, ref, k, self.to["core"]).wait_recv()

    def _column(self, near):
        far, row, column = self.where
        row, column = (
            (1 - row if "row" in near else row),
            (1 - column if "column" in near else column),
        )
        return self.at(slice(None), row, column)

    def start(self):
        for k, names in ((1, (self.first, self.second)), (0, (self.second,))):
            self._go(self._column(names), self.half_in.at[k], k, self.to[self.second])

    def _add(self, target, other):
        for k in range(target.shape[0]):
            target[k] = (target[k].astype(F32) + other[k].astype(F32)).astype(LOW)

    def step(self, stage):
        count = len(self.to["far"])
        own, near = self._column(()), self._column((self.first,))
        if stage == 0:
            self.start()
        if stage == 1:
            self._arrived(self.half_in.at[1], 1)
            self._add(near, self.half_in.at[1])
            self._go(near, self.quarter_in, 2, self.to[self.first])
        if stage == 2:
            self._arrived(self.half_in.at[0], 0)
            self._add(own, self.half_in.at[0])
        if stage == 3:
            self._arrived(self.quarter_in, 2)
            self._add(own, self.quarter_in)
            for k, device in enumerate(self.to["far"]):
                self._go(own.at[self.to["far_index"][k]], self.far_in.at[k], 3 + k, device)
        if stage == 4:
            for k in range(count):
                self._arrived(self.far_in.at[k], 3 + k)

    def result(self):
        value = self._column(())[self.where[0]].astype(F32)
        for k in range(len(self.to["far"])):
            value = value + self.far_in[k].astype(F32)
        return value

    def finish(self):
        refs = [self.half_in.at[0], self.half_in.at[1], self.quarter_in]
        refs += [self.far_in.at[k] for k in range(len(self.to["far"]))]
        for k, ref in enumerate(refs):
            self._copy(ref, ref, k, self.to["core"]).wait_send()


def attention_backward(pairs, queries, keys, values, probs, mixed, d_query, d_key, d_value, turned):
    scale = HEAD ** (-0.5)
    for pair in range(*pairs):
        lanes = slice(pair * 128, pair * 128 + 128)
        query, delta = queries[:, lanes], mixed[:, lanes]
        key, value = keys[:, lanes], values[:, lanes]
        by_query, by_key = (transposed, plain) if turned else (plain, transposed)
        parts = ([], [], [])
        for j in range(2):
            part = slice(j * HEAD, (j + 1) * HEAD)
            prob_low = probs[pair * 2 + j]
            prob = prob_low.astype(F32)
            d_prob = against(value[:, part], delta[:, part]) if turned else against(delta[:, part], value[:, part])
            row_delta = jnp.sum(d_prob * prob, axis=0 if turned else 1, keepdims=True)
            d_score = (prob * (d_prob - row_delta)).astype(LOW)
            parts[0].append(by_query(d_score, key[:, part]))
            parts[1].append(by_key(d_score, query[:, part]))
            parts[2].append(by_key(prob_low, delta[:, part]))
        d_query[:, lanes] = (jnp.concatenate(parts[0], axis=1) * scale).astype(LOW)
        d_key[:, lanes] = (jnp.concatenate(parts[1], axis=1) * scale).astype(LOW)
        d_value[:, lanes] = jnp.concatenate(parts[2], axis=1).astype(LOW)


def reduce_kernel(far_count, table, vectors_in, hidden_h, d_branch_x_h, d_branch_h, slope_h, expand_h, shrink_h, middle_h, d_sum2_h, middle_sum_h,
                  mixed_u_h, mixed_p_h, inputs_h, memory_h, qu_h, ku_h, vu_h, qp_h, kp_h, vp_h, probs_u_h, probs_p_h, packed_h, d_sum0_h, proj_h, maps_h,
                  proj_o, maps_o, expand_o, shrink_o, vec_o, tokens_o, memory_o,
                  half_in, quarter_in, far_in, vec_sum, vec_in, sums,
                  grads, expand_grads, shrink_grads, d_hidden_x, d_unpacked, d_sum1, partial, partial_in, wide_out, wide_in, rows_out, rows_in,
                  send, recv, last_send, last_recv, last_local, in_sems, cross_send, cross_recv, vec_send, vec_recv):
    seq, core = lax.axis_index("seq"), lax.axis_index("mem")
    where = place(seq)
    to = peers(seq, core, far_count)
    wide = proj_h.shape[-1]
    width = 2 * wide
    rows = proj_o.shape[-2] * 2
    part = rows // 2
    own_rows = d_sum1.shape[0]
    mem_rows = packed_h.shape[0] // 2
    units, ends = [], []

    def span(which, start=0, whole=None):
        return pl.ds(pl.multiple_of(which * (whole or wide) + start, 128), wide)

    loads = {}

    def fetch(name, source, target):
        loads[name] = (source, target, len(loads))
        pltpu.make_async_copy(source, target, in_sems.at[len(loads) - 1]).start()

    def need(*names):
        for name in names:
            source, target, index = loads[name]
            pltpu.make_async_copy(source, target, in_sems.at[index]).wait()

    def below(refs):
        for name, source, target in refs:
            fetch(name, source, target)

    fetch("vectors", vectors_in, vec_sum.at[0])

    def add(at, end):
        k = len(units)
        first = "column" if k % 2 == 0 else "row"
        units.append(Reduce(where, to, first, at, half_in.at[k], quarter_in.at[k], far_in.at[k], (send.at[k], recv.at[k])))
        ends.append(end)

    def add_expand(k):
        add(lambda f, r, c: expand_grads.at[k, f, r, c],
            lambda which: expand_o.at[:, span(which, k * wide, expand_o.shape[-1] // 2)])

    def add_shrink(k):
        add(lambda f, r, c: shrink_grads.at[f, r, c, pl.ds(k * rows, rows)], None)

    def add_map(p):
        add(lambda f, r, c: grads.at[6 + p, f, r, c], lambda which: maps_o.at[p, :, span(which)])

    def add_proj(p):
        add(lambda f, r, c: grads.at[p, f, r, c], lambda which: proj_o.at[p, :, span(which)])

    for k in range(4):
        add_shrink(k)
    for k in range(4):
        add_expand(k)
    for make, p in ((add_map, 1), (add_proj, 3), (add_proj, 4), (add_proj, 5), (add_map, 0), (add_proj, 0), (add_proj, 1), (add_proj, 2)):
        make(p)

    bias_sums = Vectors(to, vec_sum, vec_in, vec_send, vec_recv, ("core", "column", "row", "far"))

    def last(k, source, target):
        return pltpu.make_async_remote_copy(source, target, last_send.at[k], last_recv.at[k], device_id=to["core"], device_id_type=MESH)

    def close(k, start):
        if ends[k] is None:
            owner = k // 2
            row = pl.ds((k % 2) * rows, rows)

            @pl.when(core == owner)
            def _():
                local = pltpu.make_async_copy(sums.at[k], shrink_o.at[row, span(core)], last_local.at[k])
                if start:
                    local.start()
                else:
                    local.wait()
                    last(k, sums.at[k], shrink_o.at[row, span(1 - core)]).wait_recv()

            @pl.when(core != owner)
            def _():
                copy = last(k, sums.at[k], shrink_o.at[row, span(core)])
                if start:
                    copy.start()
                else:
                    copy.wait_send()

            return
        own = sums.at[k, pl.ds(pl.multiple_of(core * part, 8), part)]
        other = sums.at[k, pl.ds(pl.multiple_of((1 - core) * part, 8), part)]
        local = pltpu.make_async_copy(own, ends[k](core), last_local.at[k])
        copy = last(k, other, ends[k](core))
        if start:
            local.start()
            copy.start()
        else:
            local.wait()
            copy.wait_send()
            last(k, ends[k](1 - core), ends[k](1 - core)).wait_recv()

    place_in_plan = [0]

    def turn(name):
        while place_in_plan[0] < len(BACKWARD):
            item = BACKWARD[place_in_plan[0]]
            place_in_plan[0] += 1
            if isinstance(item, str):
                if item != name:
                    raise ValueError(item)
                return
            index, stage = item
            if index == 16:
                if stage == 0:
                    bias_sums.start()
                elif stage < 4:
                    bias_sums.step(stage)
                else:
                    vec_o[...] = bias_sums.result()
                continue
            units[index].step(stage)
            if stage == 4:
                sums[index] = units[index].result()
                close(index, True)

    def weight_grad(slots, left, *rights):
        right = rights[0] if len(rights) == 1 else jnp.concatenate(rights, axis=1)
        value = transposed(left[...], right).astype(LOW)
        for k, slot in enumerate(slots):
            grads[slot] = value[:, k * wide : (k + 1) * wide].reshape(grads.shape[1:])

    def put_bias(row, values):
        vec_sum[0, row : row + 1, span(core)] = jnp.sum(values.astype(F32), axis=0, keepdims=True)

    def cross(k, source, target):
        copy = pltpu.make_async_remote_copy(source, target, cross_send.at[k], cross_recv.at[k], device_id=to["core"], device_id_type=MESH)
        copy.start()
        return copy

    hidden = hidden_h.shape[1]
    quarter = hidden // 4
    own = pl.ds(pl.multiple_of(core * own_rows, 128), own_rows)
    other = pl.ds(pl.multiple_of((1 - core) * own_rows, 128), own_rows)

    def shrink_gradient(tiles, d_branch_x, d_branch, shrink_w, slope, middle):
        below((("d_branch_x", d_branch_x_h, d_branch_x),))
        ready = []
        for n in range(4):
            copy = pltpu.make_async_copy(hidden_h.at[:, pl.ds(n * quarter, quarter)], tiles.at[n % 2], in_sems.at[30 + n])
            ready.append(copy)
        ready[0].start()
        ready[1].start()
        below((("d_branch", d_branch_h, d_branch), ("shrink", shrink_h, shrink_w), ("slope", slope_h, slope), ("middle", middle_h, middle)))
        tall = shrink_grads.shape[3]
        greet(to["far"] + [to["column"], to["row"], to["core"]])
        need("d_branch_x")
        for n in range(4):
            ready[n].wait()
            value = transposed(tiles[n % 2], d_branch_x[...]).astype(LOW)
            for b in range(quarter // tall):
                block = n * (quarter // tall) + b
                shrink_grads[block // 4, (block // 2) % 2, block % 2] = value[b * tall : (b + 1) * tall]
            if n + 2 < 4:
                ready[n + 2].start()
        need("d_branch", "shrink", "slope", "vectors")
        sent = []
        for k in range(4):
            if k % 2 == 0:
                turn("dha" if k == 0 else "dhb")
            which = 1 - core if k < 2 else core
            piece = which * 2 + k % 2
            columns = pl.ds(pl.multiple_of(piece * quarter, 128), quarter)
            here = pl.ds((k % 2) * quarter, quarter)
            value = against(d_branch[...], shrink_w[pl.ds(piece * (quarter // tall), quarter // tall)].reshape(quarter, width))
            value = (value * slope[:, columns].astype(F32)).astype(LOW)
            slope[:, columns] = value
            vec_sum[0, pl.ds(13 + piece, 1), :] = total_rows(value.astype(F32))
            if k < 2:
                sent.append(cross(3 + k, slope.at[:, columns], d_hidden_x.at[own, here]))
            else:
                d_hidden_x[own, here] = value
        for copy in sent:
            copy.wait()

    def expand_gradient(expand_w, d_sum2, middle_sum, d_hidden, middle):
        below((("expand", expand_h, expand_w), ("d_sum2", d_sum2_h, d_sum2), ("middle_sum", middle_sum_h, middle_sum)))
        need("middle")

        def one(k):
            value = transposed(middle[...], d_hidden_x[:, k * width : (k + 1) * width]).astype(LOW)
            for j in range(2):
                expand_grads[2 * k + j] = value[:, j * wide : (j + 1) * wide].reshape(expand_grads.shape[1:])

        turn("de0")
        one(0)
        turn("de1")
        one(1)
        need("expand", "d_sum2", "middle_sum")
        vec_sum[0, 5:6] = jnp.zeros((1, width), F32)
        vec_sum[0, 7:8] = jnp.zeros((1, width), F32)
        vec_sum[0, 10:11] = jnp.zeros((1, width), F32)

        def two(t, carry):
            here = pl.ds(pl.multiple_of(t * 256, 256), 256)
            delta = d_sum2[here] + against(d_hidden[here], expand_w[...].reshape(width, hidden))
            unit, factor = norm_parts(middle_sum[here])
            vec_sum[0, 7:8] += total_rows(delta * unit)
            vec_sum[0, 10:11] += total_rows(delta)
            delta = norm_backward(unit, factor, table[7:8], delta)
            d_sum1[here] = delta
            low = delta.astype(LOW)
            d_unpacked[pl.ds(pl.multiple_of(core * own_rows + t * 256, 256), 256)] = low
            vec_sum[0, 5:6] += total_rows(low.astype(F32))
            return carry

        turn("dm0")
        lax.fori_loop(0, own_rows // 512, two, 0)
        turn("dm1")
        lax.fori_loop(own_rows // 512, own_rows // 256, two, 0)
        return cross(5, d_unpacked.at[own], d_unpacked.at[own])

    def feed_forward(slope, middle):
        like = lambda ref: pltpu.VMEM(ref.shape, ref.dtype)
        pl.run_scoped(
            lambda *refs: shrink_gradient(*refs, slope, middle),
            pltpu.VMEM((2, hidden_h.shape[0], quarter), LOW), like(d_branch_x_h), like(d_branch_h), like(shrink_h),
        )
        pl.run_scoped(
            lambda *refs: expand_gradient(*refs, slope, middle).wait(),
            like(expand_h), like(d_sum2_h), like(middle_sum_h),
        )

    pl.run_scoped(feed_forward, pltpu.VMEM(slope_h.shape, LOW), pltpu.VMEM(middle_h.shape, LOW))

    def attention(map_u, map_p, mixed_u, mixed_p, inputs, memory, qu, ku, vu, qp, kp, vp, probs, packed, d_sum0, weights,
                  d_mixed, d_query, d_key, d_value, d_token_key, d_token_value, d_packed):
        mine = pl.ds(pl.multiple_of(core * wide, 128), wide)
        below((
            ("map_u", maps_h.at[1, mine], map_u), ("mixed_u", mixed_u_h, mixed_u), ("qu", qu_h, qu), ("ku", ku_h, ku), ("vu", vu_h, vu), ("probs_u", probs_u_h, probs),
            ("inputs", inputs_h, inputs), ("packed", packed_h, packed), ("weights", proj_h, weights), ("d_sum0", d_sum0_h, d_sum0),
            ("map_p", maps_h.at[0, mine], map_p), ("mixed_p", mixed_p_h, mixed_p), ("qp", qp_h, qp), ("kp", kp_h, kp), ("vp", vp_h, vp), ("memory", memory_h, memory),
        ))
        need("map_u")

        def from_map_u(piece):
            d_mixed[piece] = against(d_unpacked[piece], map_u[...]).astype(LOW)

        turn("mix")
        from_map_u(slice(None))
        need("mixed_u")
        turn("gm1")
        weight_grad((7,), mixed_u, d_unpacked[:, span(core)])
        need("qu", "ku", "vu", "probs_u")
        for n in range(3):
            turn("ua" + str(n))
            attention_backward((n, n + 1), qu, ku, vu, probs, d_mixed, d_query, d_key, d_value, True)
        below((("probs_p", probs_p_h, probs),))
        need("inputs", "packed", "weights", "d_sum0")
        turn("pk")
        partial[...] = against(d_key[...], weights[4]) + against(d_value[...], weights[5])
        packing = cross(0, partial, partial_in)
        turn("g3")
        weight_grad((3,), inputs, d_query[...])
        turn("g45")
        weight_grad((4, 5), packed, d_key[...], d_value[...])
        put_bias(3, d_query[...])
        put_bias(4, d_value[...])

        turn("gm0")
        packing.wait()
        d_packed[...] = (d_sum0[...] + (partial[...] + partial_in[...])).astype(LOW)
        need("map_p", "mixed_p")
        d_mixed_p = d_mixed.at[pl.ds(0, 2 * mem_rows)]
        d_mixed_p[...] = against(d_packed[...], map_p[...]).astype(LOW)
        weight_grad((6,), mixed_p, d_packed[:, span(core)])
        vec_sum[0, 2:3, :] = total_rows(d_packed[pl.ds(pl.multiple_of(core * mem_rows, 128), mem_rows)].astype(F32))
        need("qp", "kp", "vp", "probs_p")
        for n in range(3):
            turn("pa" + str(n))
            attention_backward((n, n + 1), qp, kp, vp, probs, d_mixed_p, d_key, d_token_key, d_token_value, False)
        need("memory")
        turn("g0")
        weight_grad((0,), memory, d_key[...])
        turn("g12")
        weight_grad((1, 2), inputs, d_token_key[...], d_token_value[...])
        put_bias(0, d_key[...])
        put_bias(1, d_token_value[...])
        turn("tok0")
        own_mem = pl.ds(pl.multiple_of(core * mem_rows, 128), mem_rows)
        other_mem = pl.ds(pl.multiple_of((1 - core) * mem_rows, 128), mem_rows)
        rows_out[...] = against(d_key[...], weights[0])
        memory_terms = cross(2, rows_out.at[other_mem], rows_in)
        wide_out[...] = against(d_query[other], weights[3]) + against(d_token_key[other], weights[1]) + against(d_token_value[other], weights[2])
        token_terms = cross(1, wide_out, wide_in)
        turn("out0")
        tokens_o[...] = d_sum1[...] + against(d_query[own], weights[3])
        turn("out1")
        tokens_o[...] = tokens_o[...] + against(d_token_key[own], weights[1]) + against(d_token_value[own], weights[2])
        turn("fin")
        memory_terms.wait()
        memory_o[...] = d_sum0[own_mem] + rows_out[own_mem] + rows_in[...]
        token_terms.wait()
        tokens_o[...] = tokens_o[...] + wide_in[...]
        turn(None)
        for k in range(len(units)):
            close(k, False)
        for unit in units:
            unit.finish()

    like = lambda ref: pltpu.VMEM(ref.shape, ref.dtype)
    tokens, memories = like(qu_h), like(ku_h)
    pl.run_scoped(
        attention,
        pltpu.VMEM((wide, width), LOW), pltpu.VMEM((wide, width), LOW), like(mixed_u_h), like(mixed_p_h), like(inputs_h), like(memory_h),
        tokens, memories, memories, memories, tokens, tokens, like(probs_u_h), like(packed_h), like(d_sum0_h), like(proj_h),
        tokens, tokens, memories, memories, tokens, tokens, like(packed_h),
    )


def reduce_chips(far_count, table, vectors, arrays):
    hidden_full, slope, d_sum2, inputs, memory = arrays[0], arrays[3], arrays[7], arrays[11], arrays[12]
    proj = arrays[-2]
    rows, wide = proj.shape[1] // (4 * far_count), proj.shape[2]
    part, width, hidden = rows // 2, 2 * wide, hidden_full.shape[1]
    all_tokens, own_tokens, all_rows = inputs.shape[0], slope.shape[0], memory.shape[0]
    grid = (far_count, 2, 2)
    any_space = pl.BlockSpec(memory_space=pl.ANY)
    vmem = pl.BlockSpec(memory_space=pltpu.VMEM)
    shapes = ((6, part, width), (2, part, width), (part, hidden), (hidden // (8 * far_count), width), vectors.shape, d_sum2.shape, (all_rows // 2, width))
    return pl.pallas_call(
        functools.partial(reduce_kernel, far_count),
        out_shape=[jax.ShapeDtypeStruct(shape, F32) for shape in shapes],
        in_specs=[vmem] + [any_space] * (1 + len(arrays)),
        out_specs=[vmem] * 7,
        scratch_shapes=[
            pltpu.VMEM((16, 2, far_count, rows, wide), LOW),
            pltpu.VMEM((16, far_count, rows, wide), LOW),
            pltpu.VMEM((16, far_count - 1, rows, wide), LOW),
            pltpu.VMEM((4,) + vectors.shape, F32),
            pltpu.VMEM((2 + far_count,) + vectors.shape, F32),
            pltpu.VMEM((16, rows, wide), F32),
            pltpu.VMEM((8,) + grid + (rows, wide), LOW),
            pltpu.VMEM((4,) + grid + (rows, wide), LOW),
            pltpu.VMEM(grid + (hidden // (4 * far_count), wide), LOW),
            pltpu.VMEM((all_tokens, hidden // 2), LOW),
            pltpu.VMEM((all_tokens, width), LOW),
            pltpu.VMEM((own_tokens, width), F32),
            pltpu.VMEM((all_rows, width), F32),
            pltpu.VMEM((all_rows, width), F32),
            pltpu.VMEM((own_tokens, width), F32),
            pltpu.VMEM((own_tokens, width), F32),
            pltpu.VMEM((all_rows, width), F32),
            pltpu.VMEM((all_rows // 2, width), F32),
            pltpu.SemaphoreType.DMA((16, 6)),
            pltpu.SemaphoreType.DMA((16, 6)),
            pltpu.SemaphoreType.DMA((16,)),
            pltpu.SemaphoreType.DMA((16,)),
            pltpu.SemaphoreType.DMA((16,)),
            pltpu.SemaphoreType.DMA((34,)),
            pltpu.SemaphoreType.DMA((6,)),
            pltpu.SemaphoreType.DMA((6,)),
            pltpu.SemaphoreType.DMA((2 + far_count,)),
            pltpu.SemaphoreType.DMA((2 + far_count,)),
        ],
        compiler_params=pltpu.CompilerParams(
            collective_id=1, has_side_effects=True, vmem_limit_bytes=62 << 20
        ),
        name="backward_and_sums",
    )(table, vectors, *arrays)


def deliver_kernel(count, *refs):
    sources, table, targets, vectors = refs[:count], refs[count], refs[count + 1 : 2 * count + 1], refs[2 * count + 1 : 2 * count + 6]
    held, sems = refs[2 * count + 6 : 3 * count + 6], refs[3 * count + 6]
    loads = [pltpu.make_async_copy(source, hold, sems.at[0, k]) for k, (source, hold) in enumerate(zip(sources, held))]
    stores = [pltpu.make_async_copy(hold, target, sems.at[1, k]) for k, (hold, target) in enumerate(zip(held, targets))]
    for copy in loads:
        copy.start()
    device = 2 * lax.axis_index("seq") + lax.axis_index("mem")
    width = table.shape[1]
    small, large = vectors[0].shape[1], vectors[3].shape[1]
    turned = pltpu.roll(table[0:16], lax.rem(width - small * device, width), 1)[:, 0:small]
    vectors[0][...] = turned[0:6]
    vectors[1][...] = turned[6:9]
    vectors[2][...] = turned[9:12]
    vectors[4][...] = turned[12:13]
    row, column = lax.div(large * device, width), lax.rem(large * device, width)
    vectors[3][...] = pltpu.roll(table[pl.ds(13 + row, 1)], lax.rem(width - column, width), 1)[:, 0:large]
    for load, copy in zip(loads, stores):
        load.wait()
        copy.start()
    for copy in stores:
        copy.wait()


def deliver(arrays, table, part, count):
    any_space, vmem = pl.BlockSpec(memory_space=pl.ANY), pl.BlockSpec(memory_space=pltpu.VMEM)
    shapes = [array.shape for array in arrays] + [(6, part), (3, part), (3, part), (1, count), (1, part)]
    return pl.pallas_call(
        functools.partial(deliver_kernel, len(arrays)),
        out_shape=[jax.ShapeDtypeStruct(shape, F32) for shape in shapes],
        in_specs=[any_space] * len(arrays) + [vmem],
        out_specs=[any_space] * len(arrays) + [vmem] * 5,
        scratch_shapes=[pltpu.VMEM(array.shape, F32) for array in arrays] + [pltpu.SemaphoreType.DMA((2, len(arrays)))],
        compiler_params=pltpu.CompilerParams(vmem_limit_bytes=62 << 20),
        name="deliver",
    )(*arrays, table)


def norm_apply(values, gain, shift):
    centre = values - jnp.mean(values, axis=-1, keepdims=True)
    spread = jnp.mean(centre * centre, axis=-1, keepdims=True)
    return centre * lax.rsqrt(spread + epsilon) * gain + shift


def gelu_exact(values):
    return jax.nn.gelu(values, approximate=False)


def heads_of(values):
    return values.reshape(values.shape[0], values.shape[1] // HEAD, HEAD)


def scores_of(queries, keys, valid):
    scores = jnp.einsum(
        "rhd,chd->hrc", heads_of(queries), heads_of(keys), preferred_element_type=F32
    ) * HEAD ** (-0.5)
    if valid is not None:
        scores = jnp.where(valid[None, None, :], scores, -1e30)
    return scores


def attend_forward(queries, keys, values, valid):
    scores = scores_of(queries, keys, valid)
    top = jnp.max(scores, axis=-1, keepdims=True)
    expon = jnp.exp(scores - top)
    total = jnp.sum(expon, axis=-1, keepdims=True)
    probs = to_low(expon / total)
    mixed = jnp.einsum("hrc,chd->rhd", probs, heads_of(values), preferred_element_type=F32)
    return to_low(mixed.reshape(queries.shape)), top + jnp.log(total), probs


def attend_backward(queries, keys, values, valid, log_total, delta_mixed):
    probs = jnp.exp(scores_of(queries, keys, valid) - log_total)
    delta_heads = heads_of(delta_mixed)
    delta_values = jnp.einsum("hrc,rhd->chd", to_low(probs), delta_heads, preferred_element_type=F32)
    delta_probs = jnp.einsum("rhd,chd->hrc", delta_heads, heads_of(values), preferred_element_type=F32)
    row_delta = jnp.sum(delta_probs * probs, axis=-1, keepdims=True)
    score_low = to_low(probs * (delta_probs - row_delta))
    scale = HEAD ** (-0.5)
    delta_query = jnp.einsum("hrc,chd->rhd", score_low, heads_of(keys), preferred_element_type=F32) * scale
    delta_keys = jnp.einsum("hrc,rhd->chd", score_low, heads_of(queries), preferred_element_type=F32) * scale
    return (
        to_low(delta_query.reshape(queries.shape)),
        to_low(delta_keys.reshape(keys.shape)),
        to_low(delta_values.reshape(keys.shape)),
    )


def body(
    custom,
    tokens,
    memory,
    lengths,
    tokens_cotangent,
    memory_cotangent,
    projections,
    output_maps,
    expand_weight,
    shrink_weight,
    projection_bias,
    norm_gain,
    norm_bias,
    expand_bias,
    shrink_bias,
):
    share = lax.axis_index("mem")
    chips = lax.axis_size("seq")
    width = tokens.shape[1]
    hidden = expand_weight.shape[1]
    part = projections.shape[1]
    rows = 2 * part

    def block(values, axis):
        low = to_low(values)
        wide = axis + 1
        return join(half(low, share, wide), swap(half(low, 1 - share, wide)), axis)

    own_count = tokens.shape[0]
    device = 2 * lax.axis_index("seq") + share
    if custom:
        (
            proj_all, maps_all, expand_mat, shrink_mat, table, hidden_full, middle_full, d_branch_x, inputs, rows_all, pack_query, pack_keys,
            pack_values, unpack_query, unpack_keys, unpack_values, pack_probs, unpack_probs, pack_mixed, unpack_mixed, packed_low, new_memory,
            middle_sum, slope, delta_sum2, delta_branch, new_tokens, delta_sum0, vectors,
        ) = gather_chips(
            chips // 4,
            (projections, output_maps, expand_weight, shrink_weight),
            (projection_bias, norm_gain, norm_bias, shrink_bias[None], expand_bias[None]),
            lengths[None], tokens, memory, tokens_cotangent, memory_cotangent,
        )
        proj_all = proj_all.reshape(6, width, width // 2)
        maps_all = maps_all.reshape(2, width, width)
        shrink_mat = shrink_mat.reshape(chips, hidden // chips, width)
        proj_o, maps_o, expand_o, shrink_o, vec_o, tokens_grad, memory_grad = reduce_chips(
            chips // 4,
            table,
            vectors,
            (
                hidden_full, d_branch_x, delta_branch, slope, expand_mat, shrink_mat, middle_full, delta_sum2, middle_sum,
                unpack_mixed, pack_mixed, inputs, rows_all, unpack_query, unpack_keys, unpack_values,
                pack_query, pack_keys, pack_values, unpack_probs, pack_probs, packed_low, delta_sum0, proj_all, maps_all,
            ),
        )
        results = deliver(
            (new_tokens, new_memory, tokens_grad, memory_grad, proj_o, maps_o, expand_o, shrink_o), vec_o, part, hidden // (2 * chips)
        )
        return tuple(results[:11]) + (results[11][0], results[12][0])
    else:
        vectors = [to_low(v).astype(F32) for v in (projection_bias, norm_gain, norm_bias, shrink_bias[None], expand_bias)]
        blocks = (block(projections, 1), block(output_maps, 1), block(expand_weight, 0), block(shrink_weight, 0))
        length = lengths[0]
        own_valid = share * own_count + jnp.arange(own_count) < length
        all_valid = jnp.arange(2 * own_count) < length
        gather = lambda values, axis: lax.all_gather(values, "seq", axis=axis, tiled=True)
        proj_all = gather(blocks[0], 1)
        maps_all = both(gather(blocks[1], 1), 2)
        expand_mat = both(gather(blocks[2], 0), 1)
        shrink_mat = both(gather(blocks[3], 0), 1)
        table = lax.all_gather(jnp.concatenate(vectors[:4]), AXES, axis=1, tiled=True)
        line = lax.all_gather(vectors[4], AXES, axis=0, tiled=True)
        table = jnp.concatenate([table, line.reshape(-1, width)])
        biases, gains, shifts, shrink_shift = table[0:6], table[6:9], table[9:12], table[12]
        expand_shift = table[13 : 13 + hidden // width].reshape(hidden)
        bias_half = half(biases, share, 1)
        inputs, rows_all, memory_cot = both(tokens), both(memory), both(memory_cotangent)
        pack_query = to_low(matmul(rows_all, proj_all[0]) + bias_half[0])
        pack_keys = to_low(matmul(inputs, proj_all[1]))
        pack_values = to_low(matmul(inputs, proj_all[2]) + bias_half[1])
        pack_own, pack_total, pack_probs = attend_forward(pack_query, pack_keys, pack_values, all_valid)
        pack_mixed = both(pack_own, 1)
        packed = matmul(pack_mixed, maps_all[0]) + biases[2]
        packed_low = to_low(packed)
        memory_sum = rows_all.astype(F32) + packed
        new_memory = norm_apply(half(memory_sum, share, 0), gains[0], shifts[0])
        unpack_keys = to_low(matmul(packed_low, proj_all[4]))
        unpack_values = to_low(matmul(packed_low, proj_all[5]) + bias_half[4])
        unpack_query = to_low(matmul(inputs, proj_all[3]) + bias_half[3])
        unpack_own, unpack_total, unpack_probs = attend_forward(unpack_query, unpack_keys, unpack_values, None)
        unpack_mixed = both(unpack_own, 1)
        middle_sum = tokens.astype(F32) + matmul(half(unpack_mixed, share, 0), maps_all[1]) + biases[5]
        middle = norm_apply(middle_sum, gains[1], shifts[1])
        middle_low = to_low(middle)
        hidden_in = matmul(middle_low, expand_mat) + expand_shift
        hidden_low = to_low(gelu_exact(hidden_in))
        output_sum = middle + matmul(hidden_low, shrink_mat) + shrink_shift
        layer_out = norm_apply(output_sum, gains[2], shifts[2])
        new_tokens = jnp.where(own_valid[:, None], layer_out, 0.0)

        delta_out = jnp.where(own_valid[:, None], tokens_cotangent.astype(F32), 0.0)
        dropped, norm_back = jax.vjp(norm_apply, output_sum, gains[2], shifts[2])
        delta_sum2, delta_gain2, delta_shift2 = norm_back(delta_out)
        delta_branch = to_low(delta_sum2)
        delta_hidden = matmul_right(delta_branch, shrink_mat)
        dropped, gelu_back = jax.vjp(gelu_exact, hidden_in)
        delta_hidden_in = to_low(gelu_back(delta_hidden)[0])
        delta_shrink = matmul_left(
            both(hidden_low), join(half(delta_branch, share, 1), swap(half(delta_branch, 1 - share, 1)))
        )
        delta_expand = matmul_left(
            both(middle_low), join(half(delta_hidden_in, share, 1), swap(half(delta_hidden_in, 1 - share, 1)))
        )
        delta_middle = delta_sum2 + matmul_right(delta_hidden_in, expand_mat)
        dropped, norm_back = jax.vjp(norm_apply, middle_sum, gains[1], shifts[1])
        delta_sum1, delta_gain1, delta_shift1 = norm_back(delta_middle)
        delta_own = to_low(delta_sum1)
        delta_unpacked = both(delta_own)
        dropped, norm_back = jax.vjp(norm_apply, memory_sum, gains[0], shifts[0])
        delta_sum0 = norm_back(memory_cot.astype(F32))[0]
        dropped, norm_back = jax.vjp(norm_apply, half(memory_sum, share, 0), gains[0], shifts[0])
        dropped, delta_gain0, delta_shift0 = norm_back(memory_cotangent.astype(F32))
        known = [delta_gain0, delta_gain1, delta_gain2, delta_shift0, delta_shift1, delta_shift2, column_sum(delta_branch)]
        delta_map1 = matmul_left(unpack_mixed, half(delta_unpacked, share, 1))
        delta_mixed = to_low(matmul_right(delta_unpacked, half(maps_all[1], share, 0)))
        delta_uquery, delta_ukeys, delta_uvalues = attend_backward(
            unpack_query, unpack_keys, unpack_values, None, unpack_total, delta_mixed
        )
        delta_proj3 = matmul_left(inputs, delta_uquery)
        delta_proj4 = matmul_left(packed_low, delta_ukeys)
        delta_proj5 = matmul_left(packed_low, delta_uvalues)
        partial = matmul_right(delta_ukeys, proj_all[4]) + matmul_right(delta_uvalues, proj_all[5])
        delta_packed = to_low(delta_sum0 + (partial + swap(partial)))
        delta_map0 = matmul_left(pack_mixed, half(delta_packed, share, 1))
        delta_mixed = to_low(matmul_right(delta_packed, half(maps_all[0], share, 0)))
        delta_pquery, delta_pkeys, delta_pvalues = attend_backward(
            pack_query, pack_keys, pack_values, all_valid, pack_total, delta_mixed
        )
        delta_proj0 = matmul_left(rows_all, delta_pquery)
        delta_proj1 = matmul_left(inputs, delta_pkeys)
        delta_proj2 = matmul_left(inputs, delta_pvalues)
        partial = matmul_right(delta_pquery, proj_all[0])
        memory_grad = half(delta_sum0, share, 0) + half(partial, share, 0) + swap(half(partial, 1 - share, 0))
        partial = (
            matmul_right(delta_uquery, proj_all[3])
            + matmul_right(delta_pkeys, proj_all[1])
            + matmul_right(delta_pvalues, proj_all[2])
        )
        tokens_grad = delta_sum1 + half(partial, share, 0) + swap(half(partial, 1 - share, 0))

        zero = jnp.zeros((1, width // 2), F32)

        def spread(values):
            return join(values, zero[0])

        bias_grads = [
            spread(column_sum(delta_pquery)),
            spread(column_sum(delta_pvalues)),
            column_sum(half(delta_packed, share, 0)),
            spread(column_sum(delta_uquery)),
            spread(column_sum(delta_uvalues)),
            column_sum(delta_own),
        ]
        vec_grads = jnp.stack(
            bias_grads + known
        )
        vec_grads = vec_grads.reshape(13, 2 * chips, part).transpose(1, 0, 2).reshape(2 * chips, 13 * part)
        vec_grads = jnp.concatenate([vec_grads, column_sum(delta_hidden_in).reshape(2 * chips, -1)], axis=1)
        vec_grads = jnp.pad(vec_grads, ((0, 0), (0, 1024 - vec_grads.shape[1])))
        reduce = lambda values, axis: lax.psum_scatter(values, "seq", scatter_dimension=axis, tiled=True)

        def finish(values, axis):
            return join(half(values, share, axis), swap(half(values, 1 - share, axis)), axis + 1)

        proj_o = finish(reduce(jnp.stack([delta_proj0, delta_proj1, delta_proj2, delta_proj3, delta_proj4, delta_proj5]), 1), 1)
        maps_o = finish(reduce(jnp.stack([delta_map0, delta_map1]), 1), 1)
        expand_o = finish(reduce(delta_expand, 0), 0)
        shrink_o = finish(reduce(delta_shrink, 0), 0)
        vec_o = lax.psum_scatter(vec_grads, AXES, scatter_dimension=0, tiled=True).reshape(-1)
        small = vec_o[: 13 * part].reshape(13, part)
        expand_small = vec_o[13 * part : 13 * part + hidden // (2 * chips)]
    return (
        new_tokens,
        new_memory,
        tokens_grad,
        memory_grad,
        proj_o,
        maps_o,
        expand_o,
        shrink_o,
        small[0:6],
        small[6:9],
        small[9:12],
        expand_small,
        small[12],
    )


def solution(mesh):
    rows, stacked = P(AXES, None), P(None, AXES, None)
    table, line = P(None, AXES), P(AXES)
    custom = mesh.shape["seq"] == 16 and mesh.shape["mem"] == 2
    return jax.shard_map(
        functools.partial(body, custom),
        mesh=mesh,
        in_specs=(rows, rows, P("seq"), rows, rows, stacked, stacked, rows, rows, table, table, table, line, line),
        out_specs=(rows, rows, rows, rows, stacked, stacked, rows, rows, table, table, table, line, line),
        check_vma=False,
    )
```

```python
import functools

import jax
import jax.numpy as jnp
from jax import lax
from jax.experimental import pallas as pl
from jax.experimental.pallas import tpu as pltpu
from jax.sharding import PartitionSpec as P

HEAD = 64
epsilon = 1e-05
MESH = pl.DeviceIdType.MESH
LOW = jnp.bfloat16
F32 = jnp.float32
AXES = ("seq", "mem")


def matmul(left, right):
    return jnp.dot(left, right, preferred_element_type=F32)


def matmul_left(left, right):
    return lax.dot_general(left, right, (((0,), (0,)), ((), ())), preferred_element_type=F32)


def matmul_right(left, right):
    return lax.dot_general(left, right, (((1,), (1,)), ((), ())), preferred_element_type=F32)


def to_low(values):
    return values.astype(LOW)


def column_sum(values):
    return jnp.sum(values.astype(F32), axis=0)


def swap(values):
    return lax.ppermute(values, "mem", [(0, 1), (1, 0)])


def join(own, other, axis=0):
    first = lax.axis_index("mem") == 0
    return jnp.where(
        first, jnp.concatenate([own, other], axis), jnp.concatenate([other, own], axis)
    )


def both(values, axis=0):
    return join(values, swap(values), axis)


def half(values, index, axis):
    size = values.shape[axis] // 2
    return lax.dynamic_slice_in_dim(values, index * size, size, axis)


FORWARD = (
    (0, 0), (15, 0), (16, 0), (0, 1), (15, 1), (1, 0), (16, 1), (0, 2), (0, 3), (2, 0), (1, 1), (3, 0), (2, 1),
    (1, 2), 1, (3, 1), (4, 0), (2, 2), 0, (5, 0), (3, 2), 2, 11, (4, 1), (6, 0), 13, (5, 1), 15, 3,
    (7, 0), (4, 2), (6, 1), (4, 3), 4, (5, 2), (8, 0), 5, (7, 1), (9, 0), (6, 2), 6, (8, 1), (10, 0),
    (7, 2), 7, 12, (9, 1), (11, 0), 14, 16, (8, 2), (10, 1), (12, 0), 8, (8, 3), (9, 2), 9,
    (9, 3), (11, 1), (13, 0), (10, 2), (12, 1), (14, 0), (10, 3), 17, 19, (11, 2), (13, 1), (11, 3), (12, 2),
    (14, 1), (12, 3), 18, 20, (13, 2), (14, 2), (13, 3), (14, 3), (15, 2), (15, 3), (16, 2), (16, 3), 10,
)
BACKWARD = (
    (0, 0), (1, 0), (2, 0), (3, 0), 0, 0, 0, (2, 1), (3, 1), 0, (4, 0), (5, 0), (2, 2), (3, 2),
    0, 0, (2, 3), (3, 3), (6, 0), (7, 0), 0, (4, 1), (5, 1), 0, (0, 1), (4, 2), (5, 2), 0, 0,
    (6, 1), (7, 1), 0, 0, (6, 2), (7, 2), 0, 0, (9, 0), (4, 3), (5, 3), 0, (0, 2), (8, 0), 0,
    (1, 1), (6, 3), (7, 3), 0, (9, 1), 0, (8, 1), (2, 4), (9, 2), 0, (0, 3), (8, 2), (10, 0), (11, 0),
    (1, 2), (3, 4), 0, (9, 3), (16, 0), 0, (8, 3), (4, 4), (16, 1), 0, (10, 1), (11, 1), 0,
    (5, 4), 0, (10, 2), (1, 3), (11, 2), (12, 0), (13, 0), (16, 2), (6, 4), (11, 3), (10, 3), (7, 4), (12, 1),
    (13, 1), (12, 2), (9, 4), (13, 2), (14, 0), (15, 0), (16, 3), (8, 4), (12, 3), (13, 3), (15, 1), (11, 4),
    (14, 1), (15, 2), (14, 2), (10, 4), (16, 4), (14, 3), (15, 3), (12, 4), (13, 4), (14, 4), (15, 4),
)


def place(seq):
    return lax.div(seq, 4), lax.rem(lax.div(seq, 2), 2), lax.rem(seq, 2)


def peers(seq, core, far_count):
    far, row, column = place(seq)
    flat = lambda f, r, c: f * 4 + r * 2 + c
    far_peers = [lax.rem(far + k, far_count) for k in range(1, far_count)]
    return {
        "far": [(flat(f, row, column), core) for f in far_peers],
        "far_index": far_peers,
        "column": (flat(far, row, 1 - column), core),
        "row": (flat(far, 1 - row, column), core),
        "core": (seq, 1 - core),
    }


def greet(targets):
    barrier = pltpu.get_barrier_semaphore()
    for target in targets:
        pl.semaphore_signal(barrier, inc=1, device_id=target, device_id_type=MESH)
    pl.semaphore_wait(barrier, len(targets))


class Gather:
    def __init__(self, where, to, first, own, at, shared, sems):
        self.where, self.to, self.own, self.at, self.shared = where, to, own, at, shared
        self.first, self.second = first, ("row" if first == "column" else "column")
        self.send, self.recv = sems
        self.started = []

    def _column(self, near):
        far, row, column = self.where
        row, column = (
            (1 - row if "row" in near else row),
            (1 - column if "column" in near else column),
        )
        return self.at(slice(None), row, column)

    def _copy(self, source, target, k, device):
        return pltpu.make_async_remote_copy(
            source, target, self.send.at[k], self.recv.at[k], device_id=device, device_id_type=MESH
        )

    def _go(self, *args):
        copy = self._copy(*args)
        copy.start()
        self.started.append(copy)

    def _arrived(self, ref, k):
        self._copy(ref, ref, k, self.to["core"]).wait_recv()

    def start(self):
        far, row, column = self.where
        mine = self.at(far, row, column)
        for k, device in enumerate(self.to["far"]):
            self._go(self.own, mine, k, device)

    def step(self, stage):
        far, row, column = self.where
        near = self._column(())
        if stage == 0:
            count = len(self.to["far"])
            for k in range(count):
                sender = self.to["far_index"][count - 1 - k]
                self._arrived(self.at(sender, row, column), k)
            self._go(near, near, 3, self.to[self.first])
            self._go(near, near, 4, self.to[self.second])
            if self.shared:
                self._go(near, near, 6, self.to["core"])
        if stage == 1:
            got = self._column((self.first,))
            self._arrived(got, 3)
            self._go(got, got, 5, self.to[self.second])
            if self.shared:
                self._go(got, got, 7, self.to["core"])
        if stage == 2:
            for k, names in ((4, (self.second,)), (5, (self.first, self.second))):
                got = self._column(names)
                self._arrived(got, k)
                if self.shared:
                    self._go(got, got, 4 + k, self.to["core"])
        if stage == 3 and self.shared:
            for k, names in enumerate(
                ((), (self.first,), (self.second,), (self.first, self.second))
            ):
                self._arrived(self._other(names), 6 + k)

    def _other(self, names):
        keep, self.at = self.at, self.shared
        ref = self._column(names)
        self.at = keep
        return ref

    def finish(self):
        for copy in self.started:
            copy.wait_send()


class GatherNear(Gather):
    def start(self):
        far, row, column = self.where
        mine = self.at(far, row, column)
        self._go(self.own, mine, 0, self.to[self.first])
        self._go(self.own, mine, 1, self.to[self.second])

    def _near(self, names):
        far, row, column = self.where
        return self.at(
            far, 1 - row if "row" in names else row, 1 - column if "column" in names else column
        )

    def step(self, stage):
        far = self.where[0]
        all_of = slice(None)
        count = len(self.to["far"])
        if stage == 0:
            got = self._near((self.first,))
            self._arrived(got, 0)
            self._go(got, got, 2, self.to[self.second])
        if stage == 1:
            self._arrived(self._near((self.second,)), 1)
            self._arrived(self._near((self.first, self.second)), 2)
            plane = self.at(far, all_of, all_of)
            for k, device in enumerate(self.to["far"]):
                self._go(plane, plane, 3 + k, device)
            if self.shared:
                self._go(plane, plane, 3 + count, self.to["core"])
        if stage == 2:
            for k in range(count):
                plane = self.at(self.to["far_index"][count - 1 - k], all_of, all_of)
                self._arrived(plane, 3 + k)
                if self.shared:
                    self._go(plane, plane, 4 + count + k, self.to["core"])
        if stage == 3 and self.shared:
            self._arrived(self.shared(far, all_of, all_of), 3 + count)
            for k in range(count):
                plane = self.shared(self.to["far_index"][count - 1 - k], all_of, all_of)
                self._arrived(plane, 4 + count + k)


def transposed(left, right):
    return lax.dot_general(left, right, (((0,), (0,)), ((), ())), preferred_element_type=F32)


def against(left, right):
    return lax.dot_general(left, right, (((1,), (1,)), ((), ())), preferred_element_type=F32)


def plain(left, right):
    return lax.dot_general(left, right, (((1,), (0,)), ((), ())), preferred_element_type=F32)


def over_rows(count, tile, work):
    def one(t, carry):
        work(pl.ds(pl.multiple_of(t * tile, tile), tile))
        return carry

    lax.fori_loop(0, count // tile, one, 0)


class Vectors:
    def __init__(self, to, held, arrived, send, recv, order):
        self.to, self.held, self.arrived, self.sems, self.order = to, held, arrived, (send, recv), order
        self.flying, self.slot = [], 0

    def _go(self, k):
        name = self.order[k]
        for device in self.to["far"] if name == "far" else [self.to[name]]:
            slot = self.slot
            copy = pltpu.make_async_remote_copy(
                self.held.at[k], self.arrived.at[slot], self.sems[0].at[slot], self.sems[1].at[slot],
                device_id=device, device_id_type=MESH,
            )
            copy.start()
            self.flying.append((slot, copy))
            self.slot += 1

    def _take(self, k):
        value = self.held[k]
        for slot, copy in self.flying:
            copy.wait()
            value = value + self.arrived[slot]
        self.flying = []
        return value

    def start(self):
        self._go(0)

    def step(self, k):
        self.held[k] = self._take(k - 1)
        self._go(k)

    def scatter(self, far_in, cuts):
        self.held[3] = self._take(2)
        self.flying = []
        for k, device in enumerate(self.to["far"]):
            for n, (rows, columns) in enumerate(cuts(self.to["far_index"][k])):
                copy = pltpu.make_async_remote_copy(
                    self.held.at[3, rows, columns], far_in.at[k, rows], self.sems[0].at[3 + 2 * k + n], self.sems[1].at[3 + 2 * k + n],
                    device_id=device, device_id_type=MESH,
                )
                copy.start()
                self.flying.append(copy)

    def gathered(self, far_in, own_cuts, target):
        for copy in self.flying:
            copy.wait()
        for rows, columns in own_cuts:
            value = self.held[3, rows, columns]
            for k in range(len(self.to["far"])):
                value = value + far_in[k, rows]
            target[rows] = value


def attention_forward(pairs, queries, keys, values, valid, probs, mixed, first_lane, turned):
    for pair in range(*pairs):
        lanes = slice(pair * 128, pair * 128 + 128)
        query, key, value = queries[:, lanes] * LOW(HEAD ** (-0.5)), keys[:, lanes], values[:, lanes]
        outs = []
        for j in range(2):
            part = slice(j * HEAD, (j + 1) * HEAD)
            scores = against(key[:, part], query[:, part]) if turned else against(query[:, part], key[:, part])
            if valid is not None:
                scores = jnp.where(lax.broadcasted_iota(jnp.int32, scores.shape, 1) < valid[0, 0], scores, -1e30)
            axis = 0 if turned else 1
            expon = jnp.exp(scores - jnp.max(scores, axis=axis, keepdims=True))
            prob = (expon * (1.0 / jnp.sum(expon, axis=axis, keepdims=True))).astype(LOW)
            probs[pair * 2 + j] = prob
            outs.append((transposed if turned else plain)(prob, value[:, part]))
        mixed[:, pl.ds(pl.multiple_of(first_lane + pair * 128, 128), 128)] = jnp.concatenate(outs, axis=1).astype(LOW)


def norm_parts(values):
    centre = values - jnp.mean(values, axis=-1, keepdims=True)
    factor = lax.rsqrt(jnp.mean(centre * centre, axis=-1, keepdims=True) + epsilon)
    return centre * factor, factor


def norm_backward(unit, factor, gain, delta):
    scaled = delta * gain
    return factor * (scaled - jnp.mean(scaled, axis=-1, keepdims=True) - unit * jnp.mean(scaled * unit, axis=-1, keepdims=True))


def total_rows(values):
    return jnp.sum(values, axis=0, keepdims=True)


def gather_kernel(far_count, proj_in, maps_in, expand_in, shrink_in, bias_in, gain_in, shift_in, shrink_bias_in, expand_bias_in, length,
                  tokens, rows_in, token_cot_in, memory_cot,
                  proj_o, maps_o, expand_o, shrink_o, table_o, hidden_o, middle_full_o, d_branch_x_o,
                  inputs_o, memory_o, qp_o, kp_o, vp_o, qu_o, ku_o, vu_o,
                  probs_p_o, probs_u_o, mixed_p_o, mixed_u_o, packed_o, new_memory_o, middle_sum_o,
                  slope_o, d_sum2_o, d_branch_o, new_tokens_o, d_sum0_o, grad_table_o,
                  inputs, memory, qp, kp, vp, qu, ku, vu, probs_p, probs_u, mixed_p, mixed_u, packed, new_memory, middle_sum,
                  slope, d_sum2, d_branch, new_tokens, d_sum0, grad_table,
                  memory_sum, middle, middle_low, hidden, cot, expand_w, shrink_w,
                  weights, map_p, map_u, token_cot, table, own_vec, vec, vec_all,
                  proj_f, maps_f, expand_f, shrink_f, proj, maps, expand, shrink,
                  send, recv, local, out_sems, cross_send, cross_recv, raw_local, raw_send, raw_recv):
    seq, core = lax.axis_index("seq"), lax.axis_index("mem")
    where = place(seq)
    far, row, column = where
    to = peers(seq, core, far_count)
    wide = maps.shape[-1]
    width = 2 * wide
    own_tokens, own_rows = tokens.shape[0], rows_in.shape[0]

    def cols(which, start=0):
        return pl.ds(pl.multiple_of(which * expand.shape[-1] + start, 128), wide)

    def span(which):
        return pl.ds(pl.multiple_of(which * wide, 128), wide)

    copies, stores = [], []

    def keep(source, target):
        copy = pltpu.make_async_copy(source, target, local.at[len(copies)])
        copy.start()
        copies.append(copy)
        return copy

    def store(source, target):
        copy = pltpu.make_async_copy(source, target, out_sems.at[len(stores)])
        copy.start()
        stores.append(copy)

    own_t = pl.ds(pl.multiple_of(core * own_tokens, 128), own_tokens)
    own_m = pl.ds(pl.multiple_of(core * own_rows, 128), own_rows)
    raw = []
    for n, (source, target) in enumerate(((proj_in, proj_f), (maps_in, maps_f), (expand_in, expand_f), (shrink_in, shrink_f))):
        count, size = source.shape[-2], source.shape[-1] // 2
        place_rows = pl.ds(pl.multiple_of(core * count, 8), count)
        mine, theirs = (pl.ds(pl.multiple_of(which * size, 128), size) for which in (core, 1 - core))
        lead = (slice(None),) * (len(source.shape) - 2)
        raw.append((n, source.at[lead + (slice(None), mine)], source.at[lead + (slice(None), theirs)], target.at[lead + (place_rows,)]))
    for n, own, other, target in raw:
        pltpu.make_async_copy(own, target, raw_local.at[n]).start()
    keep(tokens, inputs.at[own_t])
    keep(rows_in, memory.at[own_m])
    keep(memory_cot, cot.at[own_m])
    keep(token_cot_in, token_cot)
    device = 2 * seq + core
    own_vec[...] = jnp.zeros_like(own_vec)
    for first_row, source in ((0, bias_in), (6, gain_in), (9, shift_in), (12, shrink_bias_in), (16, expand_bias_in)):
        own_vec[first_row : first_row + source.shape[0], 0 : source.shape[1]] = source[...]
    small, large = bias_in.shape[1], expand_bias_in.shape[1]

    def window(start):
        return lax.min(lax.div(start, 128), 2 * wide // 128 - 2)

    offsets = (small * device, lax.rem(large * device, 2 * wide))
    moved = [pltpu.roll(own_vec[k : k + 16 - k // 2], offsets[n] - 128 * window(offsets[n]), 1) for n, k in enumerate((0, 16))]
    vec[...] = jnp.concatenate([moved[0], moved[1], jnp.zeros_like(moved[1])], axis=0).astype(LOW)

    units = []

    def add(first, own, at, shared, kind=Gather):
        k = len(units)
        units.append(kind(where, to, first, own, at, shared, (send.at[k], recv.at[k])))

    def add_proj(first, p):
        add(first, proj.at[p], lambda f, r, c: proj_o.at[p, f, r, c], None)

    def add_map(first, p):
        add(first, maps.at[p], lambda f, r, c: maps_o.at[p, f, r, c, :, span(core)],
            lambda f, r, c: maps_o.at[p, f, r, c, :, span(1 - core)])

    def add_expand(first, k):
        add(first, expand.at[:, pl.ds(k * wide, wide)], lambda f, r, c: expand_o.at[f, r, c, :, cols(core, k * wide)],
            lambda f, r, c: expand_o.at[f, r, c, :, cols(1 - core, k * wide)])

    def add_shrink(first, k):
        rows = shrink.shape[0] // 4
        part = pl.ds(k * rows, rows)
        add(first, shrink.at[part], lambda f, r, c: shrink_o.at[f, r, c, part, span(core)],
            lambda f, r, c: shrink_o.at[f, r, c, part, span(1 - core)], GatherNear if k >= 2 else Gather)

    add("column", vec, lambda f, r, c: vec_all.at[core, f, r, c], lambda f, r, c: vec_all.at[1 - core, f, r, c])
    for first, second in (
        ((add_proj, 0), (add_proj, 1)), ((add_proj, 2), (add_map, 0)), ((add_proj, 4), (add_proj, 5)), ((add_proj, 3), (add_map, 1)),
        ((add_expand, 0), (add_expand, 1)), ((add_expand, 2), (add_expand, 3)), ((add_shrink, 0), (add_shrink, 1)), ((add_shrink, 2), (add_shrink, 3)),
    ):
        first[0]("column", first[1])
        second[0]("row", second[1])

    def cross(k, source, target):
        copy = pltpu.make_async_remote_copy(source, target, cross_send.at[k], cross_recv.at[k], device_id=to["core"], device_id_type=MESH)
        copy.start()
        return copy

    greet(to["far"] + [to["column"], to["row"], to["core"]])
    for n, own, other, target in raw:
        pltpu.make_async_remote_copy(other, target, raw_send.at[n], raw_recv.at[n], device_id=to["core"], device_id_type=MESH).start()
    crossed = [cross(0, tokens, inputs.at[own_t]), cross(1, rows_in, memory.at[own_m]), cross(4, memory_cot, cot.at[own_m])]
    keep(vec, vec_all.at[core, far, row, column])
    units[0].start()
    targets = (
        (proj_f, proj, proj_o.at[:, far, row, column]),
        (maps_f, maps, maps_o.at[:, far, row, column, :, span(core)]),
        (expand_f, expand, expand_o.at[far, row, column, :, pl.ds(pl.multiple_of(core * expand.shape[-1], 128), expand.shape[-1])]),
        (shrink_f, shrink, shrink_o.at[far, row, column, :, span(core)]),
    )
    groups = ((1, 2, 3), (4, 5, 6, 7, 8), (9, 10, 11, 12), (13, 14, 15, 16))
    for (n, own, other, target), (wide_block, block, place_of), group in zip(raw, targets, groups):
        pltpu.make_async_copy(own, target, raw_local.at[n]).wait()
        pltpu.make_async_remote_copy(other, target, raw_send.at[n], raw_recv.at[n], device_id=to["core"], device_id_type=MESH).wait()
        block[...] = wide_block[...].astype(LOW)
        keep(block, place_of)
        for index in group:
            units[index].start()
    for copy in copies:
        copy.wait()
    fetched = {}

    def fetch(key, source, target):
        copy = pltpu.make_async_copy(source, target, local.at[len(copies) + sum(len(v) for v in fetched.values())])
        copy.start()
        fetched.setdefault(key, []).append(copy)

    def need(*keys):
        for key in keys:
            for copy in fetched[key]:
                copy.wait()

    tall = width
    names = ("vec", "p0", "p1", "p2", "m0", "p4", "p5", "p3", "m1", "e0", "e1", "e2", "e3", "s0", "s1", "s2", "s3")

    def complete(name):
        k = int(name[1]) if name != "vec" else 0
        if name[0] == "p":
            fetch(name, proj_o.at[k], weights.at[k])
        elif name[0] == "m":
            fetch(name, maps_o.at[k], (map_p, map_u)[k])
        elif name[0] == "e":
            for side in range(2):
                columns = pl.ds(side * expand.shape[-1] + k * wide, wide)
                fetch(name, expand_o.at[:, :, :, :, columns], expand_w.at[:, :, :, :, columns])
        elif name[0] == "s":
            rows = shrink.shape[0] // 4
            part = pl.ds(k * rows, rows)
            fetch(name, shrink_o.at[:, :, :, part], shrink_w.at[:, :, :, part])

    def weight(p):
        return weights[p].reshape(-1, wide)

    def project(p, source, target, bias):
        need("p" + str(p))

        def one(piece):
            value = plain(source[piece], weight(p))
            if bias is not None:
                value = value + table[bias : bias + 1, span(core)]
            target[piece] = value.astype(LOW)

        one(slice(None))

    def gain(k):
        return table[6 + k : 7 + k]

    def shift(k):
        return table[9 + k : 10 + k]

    def from_other(k, ref):
        copy = pltpu.make_async_remote_copy(ref, ref, cross_send.at[k], cross_recv.at[k], device_id=to["core"], device_id_type=MESH)
        copy.wait_send()
        copy.wait_recv()

    def make_k():
        crossed[0].wait()
        project(1, inputs, kp, None)
        store(inputs, inputs_o)

    def make_q():
        table[...] = jnp.zeros_like(table)
        for k in range(8 * far_count):
            block = vec_all[k % 2, k // 8, (k // 4) % 2, (k // 2) % 2].astype(F32)
            for count, row, start in ((13, 0, small * k), (1, 13 + large * k // width, (large * k) % width)):
                first = 128 * min(start // 128, width // 128 - 2)
                from_row = 0 if count == 13 else 16
                table[row : row + count, first : first + 256] += block[from_row : from_row + count]
        store(table, table_o)
        crossed[1].wait()
        project(0, memory, qp, 0)
        store(memory, memory_o)

    def make_packed():
        from_other(2, mixed_p.at[:, span(core)])
        need("m0")
        for source, target in ((qp, qp_o), (kp, kp_o), (vp, vp_o), (probs_p, probs_p_o), (mixed_p, mixed_p_o)):
            store(source, target)
        value = plain(mixed_p[...], map_p[...].reshape(-1, width)) + table[2:3]
        packed[...] = value.astype(LOW)
        memory_sum[...] = memory[...].astype(F32) + value

    def make_memory():
        crossed[2].wait()
        unit, factor = norm_parts(memory_sum[...])
        memory_sum[...] = unit
        d_sum0[...] = norm_backward(unit, factor, gain(0), cot[...].astype(F32))
        unit, delta = memory_sum[own_m], cot[own_m].astype(F32)
        new_memory[...] = unit * gain(0) + shift(0)
        grad_table[...] = jnp.zeros_like(grad_table)
        grad_table[6:7] = total_rows(delta * unit)
        grad_table[9:10] = total_rows(delta)
        for source, target in ((packed, packed_o), (d_sum0, d_sum0_o), (new_memory, new_memory_o)):
            store(source, target)

    def make_unpack():
        project(4, packed, ku, None)
        project(5, packed, vu, 4)
        store(ku, ku_o)
        store(vu, vu_o)

    sent = []

    def make_middle():
        from_other(3, mixed_u.at[:, span(core)])
        need("m1")
        for source, target in ((qu, qu_o), (probs_u, probs_u_o), (mixed_u, mixed_u_o)):
            store(source, target)

        def attended(t, carry):
            here = pl.ds(pl.multiple_of(t * 256, 256), 256)
            there = pl.ds(pl.multiple_of(core * own_tokens + t * 256, 256), 256)
            value = plain(mixed_u[there], map_u[...].reshape(-1, width)) + table[5:6]
            value = inputs[there].astype(F32) + value
            middle_sum[here] = value
            value = norm_parts(value)[0] * gain(1) + shift(1)
            middle[here] = value
            middle_low[here] = value.astype(LOW)
            return carry

        lax.fori_loop(0, own_tokens // 256, attended, 0)
        store(middle_sum, middle_sum_o)
        store(middle_low, middle_full_o.at[own_t])
        sent.append(cross(5, middle_low, middle_full_o.at[own_t]))

    def widen(n):
        columns = pl.ds(n * tall, tall)
        if n < 2:
            need("e" + str(2 * n), "e" + str(2 * n + 1))
        value = plain(middle_low[...], expand_w[:, :, :, :, columns].reshape(-1, tall)) + table[13 + n : 14 + n]
        share = 0.5 + 0.5 * lax.erf(value * 0.5**0.5)
        hidden[:, columns] = (value * share).astype(LOW)
        slope[:, columns] = (share + value * (0.3989422804014327 * jnp.exp(-0.5 * value * value))).astype(LOW)
        store(hidden.at[:, columns], hidden_o.at[own_t, columns])
        store(slope.at[:, columns], slope_o.at[:, columns])
        sent.append(cross(6 + n, hidden.at[:, columns], hidden_o.at[own_t, columns]))

    def narrow(t, carry):
        here = pl.ds(pl.multiple_of(t * 256, 256), 256)
        value = middle[here] + (plain(hidden[here], shrink_w[...].reshape(-1, width)) + table[12:13])
        unit, factor = norm_parts(value)
        live = core * own_tokens + t * 256 + lax.broadcasted_iota(jnp.int32, (256, 1), 0) < length[0, 0]
        new_tokens[here] = jnp.where(live, unit * gain(2) + shift(2), 0.0)
        delta = jnp.where(live, token_cot[here].astype(F32), 0.0)
        grad_table[8:9] += total_rows(delta * unit)
        grad_table[11:12] += total_rows(delta)
        value = norm_backward(unit, factor, gain(2), delta)
        d_sum2[here] = value
        value = value.astype(LOW)
        d_branch[here] = value
        grad_table[12:13] += total_rows(value.astype(F32))
        return carry

    def make_tokens():
        need("s0", "s1", "s2", "s3")
        lax.fori_loop(0, own_tokens // 256, narrow, 0)
        sent.append(cross(10, d_branch.at[:, span(1 - core)], d_branch_x_o.at[own_t]))
        store(d_branch.at[:, span(core)], d_branch_x_o.at[own_t])
        for source, target in ((d_sum2, d_sum2_o), (d_branch, d_branch_o), (new_tokens, new_tokens_o), (grad_table, grad_table_o)):
            store(source, target)

    work = [
        make_k,
        make_q,
        lambda: project(2, inputs, vp, 1),
        lambda: cross(2, mixed_p.at[:, span(core)], mixed_p.at[:, span(core)]),
        make_packed,
        make_memory,
        make_unpack,
        lambda: project(3, inputs, qu, 3),
        lambda: cross(3, mixed_u.at[:, span(core)], mixed_u.at[:, span(core)]),
        make_middle,
        make_tokens,
    ]
    for n in range(3):
        work.append(functools.partial(attention_forward, (n, n + 1), qp, kp, vp, length, probs_p, mixed_p, core * wide, False))
        work.append(functools.partial(attention_forward, (n, n + 1), qu, ku, vu, None, probs_u, mixed_u, core * wide, True))
    for n in range(4):
        work.append(functools.partial(widen, n))
    for item in FORWARD:
        if isinstance(item, int):
            work[item]()
            continue
        index, stage = item
        units[index].step(stage)
        if stage == (3 if units[index].shared else 2):
            complete(names[index])
    for copy in sent:
        copy.wait()
    for copy in stores:
        copy.wait()
    for unit in units:
        unit.finish()


def gather_chips(far_count, weights, vectors, length, tokens, memory, token_cot, memory_cot):
    grid = (far_count, 2, 2)
    width, hidden = weights[0].shape[-1], weights[2].shape[-1]
    rows, wide = 2 * weights[0].shape[1], width // 2
    blocks = ((6, rows, wide), (2, rows, wide), (rows, hidden // 2), (2 * weights[3].shape[0], wide))
    table = (24, width)
    own_tokens, own_rows = tokens.shape[0], memory.shape[0]
    all_tokens, all_rows = 2 * own_tokens, 2 * own_rows
    count = wide // HEAD
    passed = (
        ((6,) + grid + (rows, wide), LOW),
        ((2,) + grid + (rows, width), LOW),
        (grid + (rows, hidden), LOW),
        (grid + (blocks[3][0], width), LOW),
        (table, F32),
        ((all_tokens, hidden), LOW),
        ((all_tokens, width), LOW),
        ((all_tokens, wide), LOW),
    )
    kept = (
        ((all_tokens, width), LOW),
        ((all_rows, width), LOW),
        ((all_rows, wide), LOW),
        ((all_tokens, wide), LOW),
        ((all_tokens, wide), LOW),
        ((all_tokens, wide), LOW),
        ((all_rows, wide), LOW),
        ((all_rows, wide), LOW),
        ((count, all_rows, all_tokens), LOW),
        ((count, all_rows, all_tokens), LOW),
        ((all_rows, width), LOW),
        ((all_tokens, width), LOW),
        ((all_rows, width), LOW),
        ((own_rows, width), F32),
        ((own_tokens, width), F32),
        ((own_tokens, hidden), LOW),
        ((own_tokens, width), F32),
        ((own_tokens, width), LOW),
        ((own_tokens, width), F32),
        ((all_rows, width), F32),
        (table, F32),
    )
    inner = (
        ((all_rows, width), F32),
        ((own_tokens, width), F32),
        ((own_tokens, width), LOW),
        ((own_tokens, hidden), LOW),
        ((all_rows, width), LOW),
        passed[2],
        passed[3],
        passed[0],
        (passed[1][0][1:], LOW),
        (passed[1][0][1:], LOW),
        ((own_tokens, width), LOW),
        (table, F32),
        ((24, 256), F32),
        ((32, 256), LOW),
        ((2,) + grid + (32, 256), LOW),
    ) + tuple((block, F32) for block in blocks) + tuple((block, LOW) for block in blocks)
    any_space = pl.BlockSpec(memory_space=pl.ANY)
    return pl.pallas_call(
        functools.partial(gather_kernel, far_count),
        out_shape=[jax.ShapeDtypeStruct(*entry) for entry in passed + kept],
        in_specs=[any_space] * 4
        + [pl.BlockSpec(memory_space=pltpu.VMEM)] * 5
        + [pl.BlockSpec(memory_space=pltpu.SMEM)]
        + [any_space] * 4,
        out_specs=[any_space] * (len(passed) + len(kept)),
        scratch_shapes=[pltpu.VMEM(*entry) for entry in kept + inner]
        + [
            pltpu.SemaphoreType.DMA((17, 10)),
            pltpu.SemaphoreType.DMA((17, 10)),
            pltpu.SemaphoreType.DMA((29,)),
            pltpu.SemaphoreType.DMA((36,)),
            pltpu.SemaphoreType.DMA((11,)),
            pltpu.SemaphoreType.DMA((11,)),
            pltpu.SemaphoreType.DMA((4,)),
            pltpu.SemaphoreType.DMA((4,)),
            pltpu.SemaphoreType.DMA((4,)),
        ],
        compiler_params=pltpu.CompilerParams(
            collective_id=0, has_side_effects=True, vmem_limit_bytes=62 << 20
        ),
        name="gather_and_forward",
    )(*weights, *vectors, length, tokens, memory, token_cot, memory_cot)


class Reduce:
    def __init__(self, where, to, first, at, half_in, quarter_in, far_in, sems):
        self.where, self.to, self.at = where, to, at
        self.half_in, self.quarter_in, self.far_in = half_in, quarter_in, far_in
        self.first, self.second = first, ("row" if first == "column" else "column")
        self.send, self.recv = sems

    def _copy(self, source, target, k, device):
        return pltpu.make_async_remote_copy(
            source, target, self.send.at[k], self.recv.at[k], device_id=device, device_id_type=MESH
        )

    def _go(self, *args):
        self._copy(*args).start()

    def _arrived(self, ref, k):
        self._copy(ref, ref, k, self.to["core"]).wait_recv()

    def _column(self, near):
        far, row, column = self.where
        row, column = (
            (1 - row if "row" in near else row),
            (1 - column if "column" in near else column),
        )
        return self.at(slice(None), row, column)

    def start(self):
        for k, names in ((1, (self.first, self.second)), (0, (self.second,))):
            self._go(self._column(names), self.half_in.at[k], k, self.to[self.second])

    def _add(self, target, other):
        for k in range(target.shape[0]):
            target[k] = (target[k].astype(F32) + other[k].astype(F32)).astype(LOW)

    def step(self, stage):
        count = len(self.to["far"])
        own, near = self._column(()), self._column((self.first,))
        if stage == 0:
            self.start()
        if stage == 1:
            self._arrived(self.half_in.at[1], 1)
            self._add(near, self.half_in.at[1])
            self._go(near, self.quarter_in, 2, self.to[self.first])
        if stage == 2:
            self._arrived(self.half_in.at[0], 0)
            self._add(own, self.half_in.at[0])
        if stage == 3:
            self._arrived(self.quarter_in, 2)
            self._add(own, self.quarter_in)
            for k, device in enumerate(self.to["far"]):
                self._go(own.at[self.to["far_index"][k]], self.far_in.at[k], 3 + k, device)
        if stage == 4:
            for k in range(count):
                self._arrived(self.far_in.at[k], 3 + k)

    def result(self):
        value = self._column(())[self.where[0]].astype(F32)
        for k in range(len(self.to["far"])):
            value = value + self.far_in[k].astype(F32)
        return value

    def finish(self):
        refs = [self.half_in.at[0], self.half_in.at[1], self.quarter_in]
        refs += [self.far_in.at[k] for k in range(len(self.to["far"]))]
        for k, ref in enumerate(refs):
            self._copy(ref, ref, k, self.to["core"]).wait_send()


class ReduceNear(Reduce):
    def __init__(self, where, to, first, at, far_in, half_in, last_in, sems):
        super().__init__(where, to, first, at, half_in, last_in, far_in, sems)

    def _line(self, other):
        far, row, column = self.where
        if self.second == "row":
            return self.at(far, 1 - row if other else row, slice(None))
        return self.at(far, slice(None), 1 - column if other else column)

    def _block(self, other):
        far, row, column = self.where
        if other:
            row, column = (1 - row, column) if self.first == "row" else (row, 1 - column)
        return self.at(far, row, column)

    def step(self, stage):
        far = self.where[0]
        count = len(self.to["far"])
        if stage == 0:
            for k, device in enumerate(self.to["far"]):
                self._go(self.at(self.to["far_index"][k], slice(None), slice(None)), self.far_in.at[k], k, device)
        if stage == 1:
            for k in range(count):
                self._arrived(self.far_in.at[k], k)
            plane = self.at(far, slice(None), slice(None))
            for r in range(2):
                for c in range(2):
                    value = plane[r, c].astype(F32)
                    for k in range(count):
                        value = value + self.far_in[k, r, c].astype(F32)
                    plane[r, c] = value.astype(LOW)
            self._go(self._line(True), self.half_in, count, self.to[self.second])
        if stage == 2:
            self._arrived(self.half_in, count)
            self._add(self._line(False), self.half_in)
            self._go(self._block(True), self.quarter_in, count + 1, self.to[self.first])
        if stage == 3:
            self._arrived(self.quarter_in, count + 1)

    def result(self):
        return self._block(False)[...].astype(F32) + self.quarter_in[...].astype(F32)

    def finish(self):
        refs = [self.far_in.at[k] for k in range(len(self.to["far"]))] + [self.half_in, self.quarter_in]
        for k, ref in enumerate(refs):
            self._copy(ref, ref, k, self.to["core"]).wait_send()


def window(start, width):
    return lax.min(lax.div(start, 128), width // 128 - 2)


def attention_backward(pairs, queries, keys, values, probs, mixed, d_query, d_key, d_value, turned):
    scale = HEAD ** (-0.5)
    for pair in range(*pairs):
        lanes = slice(pair * 128, pair * 128 + 128)
        query, delta = queries[:, lanes], mixed[:, lanes]
        key, value = keys[:, lanes], values[:, lanes]
        by_query, by_key = (transposed, plain) if turned else (plain, transposed)
        parts = ([], [], [])
        for j in range(2):
            part = slice(j * HEAD, (j + 1) * HEAD)
            prob_low = probs[pair * 2 + j]
            prob = prob_low.astype(F32)
            d_prob = against(value[:, part], delta[:, part]) if turned else against(delta[:, part], value[:, part])
            row_delta = jnp.sum(d_prob * prob, axis=0 if turned else 1, keepdims=True)
            d_score = (prob * (d_prob - row_delta)).astype(LOW)
            parts[0].append(by_query(d_score, key[:, part]))
            parts[1].append(by_key(d_score, query[:, part]))
            parts[2].append(by_key(prob_low, delta[:, part]))
        d_query[:, lanes] = (jnp.concatenate(parts[0], axis=1) * scale).astype(LOW)
        d_key[:, lanes] = (jnp.concatenate(parts[1], axis=1) * scale).astype(LOW)
        d_value[:, lanes] = jnp.concatenate(parts[2], axis=1).astype(LOW)


def reduce_kernel(far_count, table, vectors_in, hidden_h, d_branch_x_h, d_branch_h, slope_h, expand_h, shrink_h, middle_h, d_sum2_h, middle_sum_h,
                  mixed_u_h, mixed_p_h, inputs_h, memory_h, qu_h, ku_h, vu_h, qp_h, kp_h, vp_h, probs_u_h, probs_p_h, packed_h, d_sum0_h, proj_h, maps_h,
                  proj_o, maps_o, expand_o, shrink_o, vec_o, tokens_out, memory_out,
                  tokens_o, memory_o, near_in, near_half, near_last, vec_far, half_in, quarter_in, far_in, vec_sum, vec_in, sums,
                  grads, expand_grads, shrink_grads, d_hidden_x, d_unpacked, d_sum1, partial, partial_in, wide_out, wide_in, rows_out, rows_in,
                  send, recv, last_send, last_recv, last_local, in_sems, cross_send, cross_recv, vec_send, vec_recv):
    seq, core = lax.axis_index("seq"), lax.axis_index("mem")
    where = place(seq)
    to = peers(seq, core, far_count)
    wide = proj_h.shape[-1]
    width = 2 * wide
    rows = proj_o.shape[-2] * 2
    part = rows // 2
    own_rows = d_sum1.shape[0]
    mem_rows = packed_h.shape[0] // 2
    units, ends = [], []

    def span(which, start=0, whole=None):
        return pl.ds(pl.multiple_of(which * (whole or wide) + start, 128), wide)

    loads = {}

    def fetch(name, source, target):
        loads[name] = (source, target, len(loads))
        pltpu.make_async_copy(source, target, in_sems.at[len(loads) - 1]).start()

    def need(*names):
        for name in names:
            source, target, index = loads[name]
            pltpu.make_async_copy(source, target, in_sems.at[index]).wait()

    def below(refs):
        for name, source, target in refs:
            fetch(name, source, target)

    fetch("vectors", vectors_in, vec_sum.at[0])

    def add(at, end):
        k = len(units)
        first = "column" if k % 2 == 0 else "row"
        if k < 2:
            units.append(ReduceNear(where, to, first, at, near_in.at[k], near_half.at[k], near_last.at[k], (send.at[k], recv.at[k])))
        else:
            units.append(Reduce(where, to, first, at, half_in.at[k - 2], quarter_in.at[k - 2], far_in.at[k - 2], (send.at[k], recv.at[k])))
        ends.append(end)

    def add_expand(k):
        add(lambda f, r, c: expand_grads.at[k, f, r, c],
            lambda which: expand_o.at[:, span(which, k * wide, expand_o.shape[-1] // 2)])

    def add_shrink(k):
        add(lambda f, r, c: shrink_grads.at[f, r, c, pl.ds(k * rows, rows)], None)

    def add_map(p):
        add(lambda f, r, c: grads.at[6 + p, f, r, c], lambda which: maps_o.at[p, :, span(which)])

    def add_proj(p):
        add(lambda f, r, c: grads.at[p, f, r, c], lambda which: proj_o.at[p, :, span(which)])

    for k in range(4):
        add_shrink(k)
    for k in range(4):
        add_expand(k)
    for make, p in ((add_map, 1), (add_proj, 3), (add_proj, 4), (add_proj, 5), (add_map, 0), (add_proj, 0), (add_proj, 1), (add_proj, 2)):
        make(p)

    bias_sums = Vectors(to, vec_sum, vec_in, vec_send, vec_recv, ("core", "column", "row"))
    chips = 4 * far_count
    large = expand_o.shape[1] // (2 * chips)

    def cuts(far):
        device = 2 * (far * 4 + lax.rem(seq, 4)) + core
        return tuple(
            (rows_of, pl.ds(pl.multiple_of(128 * window(start, width), 128), 256))
            for rows_of, start in ((pl.ds(0, 16), part * device), (pl.ds(16, 8), lax.rem(large * device, width)))
        )


    def last(k, source, target):
        return pltpu.make_async_remote_copy(source, target, last_send.at[k], last_recv.at[k], device_id=to["core"], device_id_type=MESH)

    def close(k, start):
        if ends[k] is None:
            owner = k // 2
            row = pl.ds((k % 2) * rows, rows)

            @pl.when(core == owner)
            def _():
                local = pltpu.make_async_copy(sums.at[k], shrink_o.at[row, span(core)], last_local.at[k])
                if start:
                    local.start()
                else:
                    local.wait()
                    last(k, sums.at[k], shrink_o.at[row, span(1 - core)]).wait_recv()

            @pl.when(core != owner)
            def _():
                copy = last(k, sums.at[k], shrink_o.at[row, span(core)])
                if start:
                    copy.start()
                else:
                    copy.wait_send()

            return
        own = sums.at[k, pl.ds(pl.multiple_of(core * part, 8), part)]
        other = sums.at[k, pl.ds(pl.multiple_of((1 - core) * part, 8), part)]
        local = pltpu.make_async_copy(own, ends[k](core), last_local.at[k])
        copy = last(k, other, ends[k](core))
        if start:
            local.start()
            copy.start()
        else:
            local.wait()
            copy.wait_send()
            last(k, ends[k](1 - core), ends[k](1 - core)).wait_recv()

    place_in_plan = [0]

    def turn():
        while place_in_plan[0] < len(BACKWARD):
            item = BACKWARD[place_in_plan[0]]
            place_in_plan[0] += 1
            if isinstance(item, int):
                return
            index, stage = item
            if index == 16:
                if stage == 0:
                    bias_sums.start()
                elif stage < 3:
                    bias_sums.step(stage)
                elif stage == 3:
                    bias_sums.scatter(vec_far, cuts)
                else:
                    bias_sums.gathered(vec_far, cuts(where[0]), vec_o)
                continue
            units[index].step(stage)
            if stage == (3 if index < 2 else 4):
                sums[index] = units[index].result()
                close(index, True)

    def weight_grad(slots, left, *rights):
        right = rights[0] if len(rights) == 1 else jnp.concatenate(rights, axis=1)
        value = transposed(left[...], right).astype(LOW)
        for k, slot in enumerate(slots):
            grads[slot] = value[:, k * wide : (k + 1) * wide].reshape(grads.shape[1:])

    def put_bias(row, values):
        vec_sum[0, row : row + 1, span(core)] = jnp.sum(values.astype(F32), axis=0, keepdims=True)

    def cross(k, source, target):
        copy = pltpu.make_async_remote_copy(source, target, cross_send.at[k], cross_recv.at[k], device_id=to["core"], device_id_type=MESH)
        copy.start()
        return copy

    hidden = hidden_h.shape[1]
    quarter = hidden // 4
    own = pl.ds(pl.multiple_of(core * own_rows, 128), own_rows)
    other = pl.ds(pl.multiple_of((1 - core) * own_rows, 128), own_rows)

    def shrink_gradient(tiles, d_branch_x, d_branch, shrink_w, slope, middle):
        below((("d_branch_x", d_branch_x_h, d_branch_x),))
        ready = []
        for n in range(4):
            copy = pltpu.make_async_copy(hidden_h.at[:, pl.ds(n * quarter, quarter)], tiles.at[n % 2], in_sems.at[30 + n])
            ready.append(copy)
        ready[0].start()
        ready[1].start()
        below((("d_branch", d_branch_h, d_branch), ("shrink", shrink_h, shrink_w), ("slope", slope_h, slope), ("middle", middle_h, middle)))
        tall = shrink_grads.shape[3]
        greet(to["far"] + [to["column"], to["row"], to["core"]])
        need("d_branch_x")
        for n in range(4):
            ready[n].wait()
            value = transposed(tiles[n % 2], d_branch_x[...]).astype(LOW)
            for b in range(quarter // tall):
                block = n * (quarter // tall) + b
                shrink_grads[block // 4, (block // 2) % 2, block % 2] = value[b * tall : (b + 1) * tall]
            if n + 2 < 4:
                ready[n + 2].start()
        need("d_branch", "shrink", "slope", "vectors")
        sent = []
        for k in range(4):
            if k % 2 == 0:
                turn()
            which = 1 - core if k < 2 else core
            piece = which * 2 + k % 2
            columns = pl.ds(pl.multiple_of(piece * quarter, 128), quarter)
            here = pl.ds((k % 2) * quarter, quarter)
            value = against(d_branch[...], shrink_w[pl.ds(piece * (quarter // tall), quarter // tall)].reshape(quarter, width))
            value = (value * slope[:, columns].astype(F32)).astype(LOW)
            slope[:, columns] = value
            vec_sum[0, pl.ds(16 + piece, 1), :] = total_rows(value.astype(F32))
            if k < 2:
                sent.append(cross(3 + k, slope.at[:, columns], d_hidden_x.at[own, here]))
            else:
                d_hidden_x[own, here] = value
        for copy in sent:
            copy.wait()

    def expand_gradient(expand_w, d_sum2, middle_sum, d_hidden, middle):
        below((("expand", expand_h, expand_w), ("d_sum2", d_sum2_h, d_sum2), ("middle_sum", middle_sum_h, middle_sum)))
        need("middle")

        def one(k):
            value = transposed(middle[...], d_hidden_x[:, k * width : (k + 1) * width]).astype(LOW)
            for j in range(2):
                expand_grads[2 * k + j] = value[:, j * wide : (j + 1) * wide].reshape(expand_grads.shape[1:])

        turn()
        one(0)
        turn()
        one(1)
        need("expand", "d_sum2", "middle_sum")
        vec_sum[0, 5:6] = jnp.zeros((1, width), F32)
        vec_sum[0, 7:8] = jnp.zeros((1, width), F32)
        vec_sum[0, 10:11] = jnp.zeros((1, width), F32)

        def two(t, carry):
            here = pl.ds(pl.multiple_of(t * 256, 256), 256)
            delta = d_sum2[here] + against(d_hidden[here], expand_w[...].reshape(width, hidden))
            unit, factor = norm_parts(middle_sum[here])
            vec_sum[0, 7:8] += total_rows(delta * unit)
            vec_sum[0, 10:11] += total_rows(delta)
            delta = norm_backward(unit, factor, table[7:8], delta)
            d_sum1[here] = delta
            low = delta.astype(LOW)
            d_unpacked[pl.ds(pl.multiple_of(core * own_rows + t * 256, 256), 256)] = low
            vec_sum[0, 5:6] += total_rows(low.astype(F32))
            return carry

        turn()
        lax.fori_loop(0, own_rows // 512, two, 0)
        turn()
        lax.fori_loop(own_rows // 512, own_rows // 256, two, 0)
        return cross(5, d_unpacked.at[own], d_unpacked.at[own])

    def feed_forward(slope, middle):
        like = lambda ref: pltpu.VMEM(ref.shape, ref.dtype)
        pl.run_scoped(
            lambda *refs: shrink_gradient(*refs, slope, middle),
            pltpu.VMEM((2, hidden_h.shape[0], quarter), LOW), like(d_branch_x_h), like(d_branch_h), like(shrink_h),
        )
        pl.run_scoped(
            lambda *refs: expand_gradient(*refs, slope, middle).wait(),
            like(expand_h), like(d_sum2_h), like(middle_sum_h),
        )

    pl.run_scoped(feed_forward, pltpu.VMEM(slope_h.shape, LOW), pltpu.VMEM(middle_h.shape, LOW))

    def attention(map_u, map_p, mixed_u, mixed_p, inputs, memory, qu, ku, vu, qp, kp, vp, probs, packed, d_sum0, weights,
                  d_mixed, d_query, d_key, d_value, d_token_key, d_token_value, d_packed):
        mine = pl.ds(pl.multiple_of(core * wide, 128), wide)
        below((
            ("map_u", maps_h.at[1, mine], map_u), ("mixed_u", mixed_u_h, mixed_u), ("qu", qu_h, qu), ("ku", ku_h, ku), ("vu", vu_h, vu), ("probs_u", probs_u_h, probs),
            ("inputs", inputs_h, inputs), ("packed", packed_h, packed), ("weights", proj_h, weights), ("d_sum0", d_sum0_h, d_sum0),
            ("map_p", maps_h.at[0, mine], map_p), ("mixed_p", mixed_p_h, mixed_p), ("qp", qp_h, qp), ("kp", kp_h, kp), ("vp", vp_h, vp), ("memory", memory_h, memory),
        ))
        need("map_u")

        def from_map_u(piece):
            d_mixed[piece] = against(d_unpacked[piece], map_u[...]).astype(LOW)

        turn()
        from_map_u(slice(None))
        need("mixed_u")
        turn()
        weight_grad((7,), mixed_u, d_unpacked[:, span(core)])
        need("qu", "ku", "vu", "probs_u")
        for n in range(3):
            turn()
            attention_backward((n, n + 1), qu, ku, vu, probs, d_mixed, d_query, d_key, d_value, True)
        below((("probs_p", probs_p_h, probs),))
        need("inputs", "packed", "weights", "d_sum0")
        turn()
        partial[...] = against(d_key[...], weights[4]) + against(d_value[...], weights[5])
        packing = cross(0, partial, partial_in)
        turn()
        weight_grad((3,), inputs, d_query[...])
        turn()
        weight_grad((4, 5), packed, d_key[...], d_value[...])
        put_bias(3, d_query[...])
        put_bias(4, d_value[...])

        turn()
        packing.wait()
        d_packed[...] = (d_sum0[...] + (partial[...] + partial_in[...])).astype(LOW)
        need("map_p", "mixed_p")
        d_mixed_p = d_mixed.at[pl.ds(0, 2 * mem_rows)]
        d_mixed_p[...] = against(d_packed[...], map_p[...]).astype(LOW)
        weight_grad((6,), mixed_p, d_packed[:, span(core)])
        vec_sum[0, 2:3, :] = total_rows(d_packed[pl.ds(pl.multiple_of(core * mem_rows, 128), mem_rows)].astype(F32))
        need("qp", "kp", "vp", "probs_p")
        for n in range(3):
            turn()
            attention_backward((n, n + 1), qp, kp, vp, probs, d_mixed_p, d_key, d_token_key, d_token_value, False)
        need("memory")
        turn()
        weight_grad((0,), memory, d_key[...])
        turn()
        weight_grad((1, 2), inputs, d_token_key[...], d_token_value[...])
        put_bias(0, d_key[...])
        put_bias(1, d_token_value[...])
        turn()
        own_mem = pl.ds(pl.multiple_of(core * mem_rows, 128), mem_rows)
        other_mem = pl.ds(pl.multiple_of((1 - core) * mem_rows, 128), mem_rows)
        rows_out[...] = against(d_key[...], weights[0])
        memory_terms = cross(2, rows_out.at[other_mem], rows_in)
        wide_out[...] = against(d_query[other], weights[3]) + against(d_token_key[other], weights[1]) + against(d_token_value[other], weights[2])
        token_terms = cross(1, wide_out, wide_in)
        turn()
        tokens_o[...] = d_sum1[...] + against(d_query[own], weights[3])
        turn()
        tokens_o[...] = tokens_o[...] + against(d_token_key[own], weights[1]) + against(d_token_value[own], weights[2])
        turn()
        memory_terms.wait()
        memory_o[...] = d_sum0[own_mem] + rows_out[own_mem] + rows_in[...]
        token_terms.wait()
        tokens_o[...] = tokens_o[...] + wide_in[...]
        copies = [
            pltpu.make_async_copy(source, target, in_sems.at[28 + k])
            for k, (source, target) in enumerate(((tokens_o, tokens_out), (memory_o, memory_out)))
        ]
        for copy in copies:
            copy.start()
        turn()
        for copy in copies:
            copy.wait()
        for k in range(len(units)):
            close(k, False)
        for unit in units:
            unit.finish()

    like = lambda ref: pltpu.VMEM(ref.shape, ref.dtype)
    tokens, memories = like(qu_h), like(ku_h)
    pl.run_scoped(
        attention,
        pltpu.VMEM((wide, width), LOW), pltpu.VMEM((wide, width), LOW), like(mixed_u_h), like(mixed_p_h), like(inputs_h), like(memory_h),
        tokens, memories, memories, memories, tokens, tokens, like(probs_u_h), like(packed_h), like(d_sum0_h), like(proj_h),
        tokens, tokens, memories, memories, tokens, tokens, like(packed_h),
    )


def reduce_chips(far_count, table, vectors, arrays):
    hidden_full, slope, d_sum2, inputs, memory = arrays[0], arrays[3], arrays[7], arrays[11], arrays[12]
    proj = arrays[-2]
    rows, wide = proj.shape[1] // (4 * far_count), proj.shape[2]
    part, width, hidden = rows // 2, 2 * wide, hidden_full.shape[1]
    all_tokens, own_tokens, all_rows = inputs.shape[0], slope.shape[0], memory.shape[0]
    grid = (far_count, 2, 2)
    any_space = pl.BlockSpec(memory_space=pl.ANY)
    vmem = pl.BlockSpec(memory_space=pltpu.VMEM)
    shapes = ((6, part, width), (2, part, width), (part, hidden), (hidden // (8 * far_count), width), (24, 256), d_sum2.shape, (all_rows // 2, width))
    return pl.pallas_call(
        functools.partial(reduce_kernel, far_count),
        out_shape=[jax.ShapeDtypeStruct(shape, F32) for shape in shapes],
        in_specs=[vmem] + [any_space] * (1 + len(arrays)),
        out_specs=[any_space] * 4 + [vmem] + [any_space] * 2,
        scratch_shapes=[
            pltpu.VMEM(shapes[5], F32),
            pltpu.VMEM(shapes[6], F32),
            pltpu.VMEM((2, far_count - 1, 2, 2, rows, wide), LOW),
            pltpu.VMEM((2, 2, rows, wide), LOW),
            pltpu.VMEM((2, rows, wide), LOW),
            pltpu.VMEM((far_count - 1, 24, 256), F32),
            pltpu.VMEM((14, 2, far_count, rows, wide), LOW),
            pltpu.VMEM((14, far_count, rows, wide), LOW),
            pltpu.VMEM((14, far_count - 1, rows, wide), LOW),
            pltpu.VMEM((4,) + vectors.shape, F32),
            pltpu.VMEM((3,) + vectors.shape, F32),
            pltpu.VMEM((16, rows, wide), F32),
            pltpu.VMEM((8,) + grid + (rows, wide), LOW),
            pltpu.VMEM((4,) + grid + (rows, wide), LOW),
            pltpu.VMEM(grid + (hidden // (4 * far_count), wide), LOW),
            pltpu.VMEM((all_tokens, hidden // 2), LOW),
            pltpu.VMEM((all_tokens, width), LOW),
            pltpu.VMEM((own_tokens, width), F32),
            pltpu.VMEM((all_rows, width), F32),
            pltpu.VMEM((all_rows, width), F32),
            pltpu.VMEM((own_tokens, width), F32),
            pltpu.VMEM((own_tokens, width), F32),
            pltpu.VMEM((all_rows, width), F32),
            pltpu.VMEM((all_rows // 2, width), F32),
            pltpu.SemaphoreType.DMA((16, 6)),
            pltpu.SemaphoreType.DMA((16, 6)),
            pltpu.SemaphoreType.DMA((16,)),
            pltpu.SemaphoreType.DMA((16,)),
            pltpu.SemaphoreType.DMA((16,)),
            pltpu.SemaphoreType.DMA((34,)),
            pltpu.SemaphoreType.DMA((6,)),
            pltpu.SemaphoreType.DMA((6,)),
            pltpu.SemaphoreType.DMA((2 * far_count + 1,)),
            pltpu.SemaphoreType.DMA((2 * far_count + 1,)),
        ],
        compiler_params=pltpu.CompilerParams(
            collective_id=1, has_side_effects=True, vmem_limit_bytes=62 << 20
        ),
        name="backward_and_sums",
    )(table, vectors, *arrays)


def deliver_kernel(count, *refs):
    sources, table, targets, vectors = refs[:count], refs[count], refs[count + 1 : 2 * count + 1], refs[2 * count + 1 : 2 * count + 6]
    held, sems = refs[2 * count + 6 : 3 * count + 6], refs[3 * count + 6]
    loads = [pltpu.make_async_copy(source, hold, sems.at[0, k]) for k, (source, hold) in enumerate(zip(sources, held))]
    stores = [pltpu.make_async_copy(hold, target, sems.at[1, k]) for k, (hold, target) in enumerate(zip(held, targets))]
    for copy in loads:
        copy.start()
    device = 2 * lax.axis_index("seq") + lax.axis_index("mem")
    small, large = vectors[0].shape[1], vectors[3].shape[1]
    width = targets[0].shape[1]

    def turn(values, start):
        return pltpu.roll(values, lax.rem(256 - (start - 128 * window(start, width)), 256), 1)

    turned = turn(table[0:16], small * device)[:, 0:small]
    vectors[0][...] = turned[0:6]
    vectors[1][...] = turned[6:9]
    vectors[2][...] = turned[9:12]
    vectors[4][...] = turned[12:13]
    row, column = lax.div(large * device, width), lax.rem(large * device, width)
    vectors[3][...] = turn(table[pl.ds(16 + row, 1)], column)[:, 0:large]
    for load, copy in zip(loads, stores):
        load.wait()
        copy.start()
    for copy in stores:
        copy.wait()


def deliver(arrays, table, part, count):
    any_space, vmem = pl.BlockSpec(memory_space=pl.ANY), pl.BlockSpec(memory_space=pltpu.VMEM)
    shapes = [array.shape for array in arrays] + [(6, part), (3, part), (3, part), (1, count), (1, part)]
    return pl.pallas_call(
        functools.partial(deliver_kernel, len(arrays)),
        out_shape=[jax.ShapeDtypeStruct(shape, F32) for shape in shapes],
        in_specs=[any_space] * len(arrays) + [vmem],
        out_specs=[any_space] * len(arrays) + [vmem] * 5,
        scratch_shapes=[pltpu.VMEM(array.shape, F32) for array in arrays] + [pltpu.SemaphoreType.DMA((2, len(arrays)))],
        compiler_params=pltpu.CompilerParams(vmem_limit_bytes=62 << 20),
        name="deliver",
    )(*arrays, table)


def norm_apply(values, gain, shift):
    centre = values - jnp.mean(values, axis=-1, keepdims=True)
    spread = jnp.mean(centre * centre, axis=-1, keepdims=True)
    return centre * lax.rsqrt(spread + epsilon) * gain + shift


def gelu_exact(values):
    return jax.nn.gelu(values, approximate=False)


def heads_of(values):
    return values.reshape(values.shape[0], values.shape[1] // HEAD, HEAD)


def scores_of(queries, keys, valid):
    scores = jnp.einsum(
        "rhd,chd->hrc", heads_of(queries), heads_of(keys), preferred_element_type=F32
    ) * HEAD ** (-0.5)
    if valid is not None:
        scores = jnp.where(valid[None, None, :], scores, -1e30)
    return scores


def attend_forward(queries, keys, values, valid):
    scores = scores_of(queries, keys, valid)
    top = jnp.max(scores, axis=-1, keepdims=True)
    expon = jnp.exp(scores - top)
    total = jnp.sum(expon, axis=-1, keepdims=True)
    probs = to_low(expon / total)
    mixed = jnp.einsum("hrc,chd->rhd", probs, heads_of(values), preferred_element_type=F32)
    return to_low(mixed.reshape(queries.shape)), top + jnp.log(total), probs


def attend_backward(queries, keys, values, valid, log_total, delta_mixed):
    probs = jnp.exp(scores_of(queries, keys, valid) - log_total)
    delta_heads = heads_of(delta_mixed)
    delta_values = jnp.einsum("hrc,rhd->chd", to_low(probs), delta_heads, preferred_element_type=F32)
    delta_probs = jnp.einsum("rhd,chd->hrc", delta_heads, heads_of(values), preferred_element_type=F32)
    row_delta = jnp.sum(delta_probs * probs, axis=-1, keepdims=True)
    score_low = to_low(probs * (delta_probs - row_delta))
    scale = HEAD ** (-0.5)
    delta_query = jnp.einsum("hrc,chd->rhd", score_low, heads_of(keys), preferred_element_type=F32) * scale
    delta_keys = jnp.einsum("hrc,rhd->chd", score_low, heads_of(queries), preferred_element_type=F32) * scale
    return (
        to_low(delta_query.reshape(queries.shape)),
        to_low(delta_keys.reshape(keys.shape)),
        to_low(delta_values.reshape(keys.shape)),
    )


def body(
    custom,
    tokens,
    memory,
    lengths,
    tokens_cotangent,
    memory_cotangent,
    projections,
    output_maps,
    expand_weight,
    shrink_weight,
    projection_bias,
    norm_gain,
    norm_bias,
    expand_bias,
    shrink_bias,
):
    share = lax.axis_index("mem")
    chips = lax.axis_size("seq")
    width = tokens.shape[1]
    hidden = expand_weight.shape[1]
    part = projections.shape[1]
    rows = 2 * part

    def block(values, axis):
        low = to_low(values)
        wide = axis + 1
        return join(half(low, share, wide), swap(half(low, 1 - share, wide)), axis)

    own_count = tokens.shape[0]
    device = 2 * lax.axis_index("seq") + share
    if custom:
        (
            proj_all, maps_all, expand_mat, shrink_mat, table, hidden_full, middle_full, d_branch_x, inputs, rows_all, pack_query, pack_keys,
            pack_values, unpack_query, unpack_keys, unpack_values, pack_probs, unpack_probs, pack_mixed, unpack_mixed, packed_low, new_memory,
            middle_sum, slope, delta_sum2, delta_branch, new_tokens, delta_sum0, vectors,
        ) = gather_chips(
            chips // 4,
            (projections, output_maps, expand_weight, shrink_weight),
            (projection_bias, norm_gain, norm_bias, shrink_bias[None], expand_bias[None]),
            lengths[None], tokens, memory, tokens_cotangent, memory_cotangent,
        )
        proj_all = proj_all.reshape(6, width, width // 2)
        maps_all = maps_all.reshape(2, width, width)
        shrink_mat = shrink_mat.reshape(chips, hidden // chips, width)
        proj_o, maps_o, expand_o, shrink_o, vec_o, tokens_grad, memory_grad = reduce_chips(
            chips // 4,
            table,
            vectors,
            (
                hidden_full, d_branch_x, delta_branch, slope, expand_mat, shrink_mat, middle_full, delta_sum2, middle_sum,
                unpack_mixed, pack_mixed, inputs, rows_all, unpack_query, unpack_keys, unpack_values,
                pack_query, pack_keys, pack_values, unpack_probs, pack_probs, packed_low, delta_sum0, proj_all, maps_all,
            ),
        )
        results = deliver(
            (new_tokens, new_memory, tokens_grad, memory_grad, proj_o, maps_o, expand_o, shrink_o), vec_o, part, hidden // (2 * chips)
        )
        return tuple(results[:11]) + (results[11][0], results[12][0])
    else:
        vectors = [to_low(v).astype(F32) for v in (projection_bias, norm_gain, norm_bias, shrink_bias[None], expand_bias)]
        blocks = (block(projections, 1), block(output_maps, 1), block(expand_weight, 0), block(shrink_weight, 0))
        length = lengths[0]
        own_valid = share * own_count + jnp.arange(own_count) < length
        all_valid = jnp.arange(2 * own_count) < length
        gather = lambda values, axis: lax.all_gather(values, "seq", axis=axis, tiled=True)
        proj_all = gather(blocks[0], 1)
        maps_all = both(gather(blocks[1], 1), 2)
        expand_mat = both(gather(blocks[2], 0), 1)
        shrink_mat = both(gather(blocks[3], 0), 1)
        table = lax.all_gather(jnp.concatenate(vectors[:4]), AXES, axis=1, tiled=True)
        line = lax.all_gather(vectors[4], AXES, axis=0, tiled=True)
        table = jnp.concatenate([table, line.reshape(-1, width)])
        biases, gains, shifts, shrink_shift = table[0:6], table[6:9], table[9:12], table[12]
        expand_shift = table[13 : 13 + hidden // width].reshape(hidden)
        bias_half = half(biases, share, 1)
        inputs, rows_all, memory_cot = both(tokens), both(memory), both(memory_cotangent)
        pack_query = to_low(matmul(rows_all, proj_all[0]) + bias_half[0])
        pack_keys = to_low(matmul(inputs, proj_all[1]))
        pack_values = to_low(matmul(inputs, proj_all[2]) + bias_half[1])
        pack_own, pack_total, pack_probs = attend_forward(pack_query, pack_keys, pack_values, all_valid)
        pack_mixed = both(pack_own, 1)
        packed = matmul(pack_mixed, maps_all[0]) + biases[2]
        packed_low = to_low(packed)
        memory_sum = rows_all.astype(F32) + packed
        new_memory = norm_apply(half(memory_sum, share, 0), gains[0], shifts[0])
        unpack_keys = to_low(matmul(packed_low, proj_all[4]))
        unpack_values = to_low(matmul(packed_low, proj_all[5]) + bias_half[4])
        unpack_query = to_low(matmul(inputs, proj_all[3]) + bias_half[3])
        unpack_own, unpack_total, unpack_probs = attend_forward(unpack_query, unpack_keys, unpack_values, None)
        unpack_mixed = both(unpack_own, 1)
        middle_sum = tokens.astype(F32) + matmul(half(unpack_mixed, share, 0), maps_all[1]) + biases[5]
        middle = norm_apply(middle_sum, gains[1], shifts[1])
        middle_low = to_low(middle)
        hidden_in = matmul(middle_low, expand_mat) + expand_shift
        hidden_low = to_low(gelu_exact(hidden_in))
        output_sum = middle + matmul(hidden_low, shrink_mat) + shrink_shift
        layer_out = norm_apply(output_sum, gains[2], shifts[2])
        new_tokens = jnp.where(own_valid[:, None], layer_out, 0.0)

        delta_out = jnp.where(own_valid[:, None], tokens_cotangent.astype(F32), 0.0)
        dropped, norm_back = jax.vjp(norm_apply, output_sum, gains[2], shifts[2])
        delta_sum2, delta_gain2, delta_shift2 = norm_back(delta_out)
        delta_branch = to_low(delta_sum2)
        delta_hidden = matmul_right(delta_branch, shrink_mat)
        dropped, gelu_back = jax.vjp(gelu_exact, hidden_in)
        delta_hidden_in = to_low(gelu_back(delta_hidden)[0])
        delta_shrink = matmul_left(
            both(hidden_low), join(half(delta_branch, share, 1), swap(half(delta_branch, 1 - share, 1)))
        )
        delta_expand = matmul_left(
            both(middle_low), join(half(delta_hidden_in, share, 1), swap(half(delta_hidden_in, 1 - share, 1)))
        )
        delta_middle = delta_sum2 + matmul_right(delta_hidden_in, expand_mat)
        dropped, norm_back = jax.vjp(norm_apply, middle_sum, gains[1], shifts[1])
        delta_sum1, delta_gain1, delta_shift1 = norm_back(delta_middle)
        delta_own = to_low(delta_sum1)
        delta_unpacked = both(delta_own)
        dropped, norm_back = jax.vjp(norm_apply, memory_sum, gains[0], shifts[0])
        delta_sum0 = norm_back(memory_cot.astype(F32))[0]
        dropped, norm_back = jax.vjp(norm_apply, half(memory_sum, share, 0), gains[0], shifts[0])
        dropped, delta_gain0, delta_shift0 = norm_back(memory_cotangent.astype(F32))
        known = [delta_gain0, delta_gain1, delta_gain2, delta_shift0, delta_shift1, delta_shift2, column_sum(delta_branch)]
        delta_map1 = matmul_left(unpack_mixed, half(delta_unpacked, share, 1))
        delta_mixed = to_low(matmul_right(delta_unpacked, half(maps_all[1], share, 0)))
        delta_uquery, delta_ukeys, delta_uvalues = attend_backward(
            unpack_query, unpack_keys, unpack_values, None, unpack_total, delta_mixed
        )
        delta_proj3 = matmul_left(inputs, delta_uquery)
        delta_proj4 = matmul_left(packed_low, delta_ukeys)
        delta_proj5 = matmul_left(packed_low, delta_uvalues)
        partial = matmul_right(delta_ukeys, proj_all[4]) + matmul_right(delta_uvalues, proj_all[5])
        delta_packed = to_low(delta_sum0 + (partial + swap(partial)))
        delta_map0 = matmul_left(pack_mixed, half(delta_packed, share, 1))
        delta_mixed = to_low(matmul_right(delta_packed, half(maps_all[0], share, 0)))
        delta_pquery, delta_pkeys, delta_pvalues = attend_backward(
            pack_query, pack_keys, pack_values, all_valid, pack_total, delta_mixed
        )
        delta_proj0 = matmul_left(rows_all, delta_pquery)
        delta_proj1 = matmul_left(inputs, delta_pkeys)
        delta_proj2 = matmul_left(inputs, delta_pvalues)
        partial = matmul_right(delta_pquery, proj_all[0])
        memory_grad = half(delta_sum0, share, 0) + half(partial, share, 0) + swap(half(partial, 1 - share, 0))
        partial = (
            matmul_right(delta_uquery, proj_all[3])
            + matmul_right(delta_pkeys, proj_all[1])
            + matmul_right(delta_pvalues, proj_all[2])
        )
        tokens_grad = delta_sum1 + half(partial, share, 0) + swap(half(partial, 1 - share, 0))

        zero = jnp.zeros((1, width // 2), F32)

        def spread(values):
            return join(values, zero[0])

        bias_grads = [
            spread(column_sum(delta_pquery)),
            spread(column_sum(delta_pvalues)),
            column_sum(half(delta_packed, share, 0)),
            spread(column_sum(delta_uquery)),
            spread(column_sum(delta_uvalues)),
            column_sum(delta_own),
        ]
        vec_grads = jnp.stack(
            bias_grads + known
        )
        vec_grads = vec_grads.reshape(13, 2 * chips, part).transpose(1, 0, 2).reshape(2 * chips, 13 * part)
        vec_grads = jnp.concatenate([vec_grads, column_sum(delta_hidden_in).reshape(2 * chips, -1)], axis=1)
        vec_grads = jnp.pad(vec_grads, ((0, 0), (0, 1024 - vec_grads.shape[1])))
        reduce = lambda values, axis: lax.psum_scatter(values, "seq", scatter_dimension=axis, tiled=True)

        def finish(values, axis):
            return join(half(values, share, axis), swap(half(values, 1 - share, axis)), axis + 1)

        proj_o = finish(reduce(jnp.stack([delta_proj0, delta_proj1, delta_proj2, delta_proj3, delta_proj4, delta_proj5]), 1), 1)
        maps_o = finish(reduce(jnp.stack([delta_map0, delta_map1]), 1), 1)
        expand_o = finish(reduce(delta_expand, 0), 0)
        shrink_o = finish(reduce(delta_shrink, 0), 0)
        vec_o = lax.psum_scatter(vec_grads, AXES, scatter_dimension=0, tiled=True).reshape(-1)
        small = vec_o[: 13 * part].reshape(13, part)
        expand_small = vec_o[13 * part : 13 * part + hidden // (2 * chips)]
    return (
        new_tokens,
        new_memory,
        tokens_grad,
        memory_grad,
        proj_o,
        maps_o,
        expand_o,
        shrink_o,
        small[0:6],
        small[6:9],
        small[9:12],
        expand_small,
        small[12],
    )


def solution(mesh):
    rows, stacked = P(AXES, None), P(None, AXES, None)
    table, line = P(None, AXES), P(AXES)
    custom = mesh.shape["seq"] == 16 and mesh.shape["mem"] == 2
    return jax.shard_map(
        functools.partial(body, custom),
        mesh=mesh,
        in_specs=(rows, rows, P("seq"), rows, rows, stacked, stacked, rows, rows, table, table, table, line, line),
        out_specs=(rows, rows, rows, rows, stacked, stacked, rows, rows, table, table, table, line, line),
        check_vma=False,
    )
```
